32 devices in a mesh: wide: 8 (over z, x), narrow: 4 (over y, core).
Axes of the slice: x: 2, y: 2, z: 4, core: 2. Of those that a mesh axis runs over, the one named last changes fastest.
Arguments:
- patches: bfloat16 [4096, 256], P(('wide', 'narrow')), may hold values from -6 to 6
- token_kind: int32 [4096], P(('wide', 'narrow')), may hold values 0 or 1
- mask_slots: int32 [16, 64], P('wide'), may hold values from 0 to 255
- projector: bfloat16 [2, 256, 768], replicated, may hold values from -0.375 to 0.375
- offsets: bfloat16 [2, 768], replicated, may hold values from -3 to 3
- placeholder: bfloat16 [768], replicated, may hold values from -4 to 4
- positions: bfloat16 [256, 768], replicated, may hold values from -3 to 3
- scales: bfloat16 [2, 2, 768], replicated, may hold values from 0.5 to 1.5
- shifts: bfloat16 [2, 2, 768], replicated, may hold values from -3 to 3
- attention: bfloat16 [2, 3, 768, 768], P(None, None, None, 'narrow'), may hold values from -0.21875 to 0.21875
- attn_bias: bfloat16 [2, 2, 768], P(None, None, 'narrow'), may hold values from -3 to 3
- combiner: bfloat16 [2, 768, 768], P(None, 'narrow'), may hold values from -1.75 to 1.75
- comb_bias: bfloat16 [2, 768], replicated, may hold values from -3 to 3
- expander: bfloat16 [2, 768, 3072], P(None, None, 'narrow'), may hold values from -0.21875 to 0.21875
- expand_bias: bfloat16 [2, 3072], P(None, 'narrow'), may hold values from -3 to 3
- reducer: bfloat16 [2, 3072, 768], P(None, 'narrow'), may hold values from -0.15625 to 0.15625
- reduce_bias: bfloat16 [2, 768], replicated, may hold values from -3 to 3
- cotangent: bfloat16 [4096, 768], P(('wide', 'narrow')), may hold values from -6 to 6
Outputs:
- encoded: float32 [4096, 768], P(('wide', 'narrow'))
- grad_patches: float32 [4096, 256], P(('wide', 'narrow'))
- grad_projector: float32 [2, 256, 768], replicated
- grad_offsets: float32 [2, 768], replicated
- grad_placeholder: float32 [768], replicated
- grad_positions: float32 [256, 768], replicated
- grad_scales: float32 [2, 2, 768], replicated
- grad_shifts: float32 [2, 2, 768], replicated
- grad_attention: float32 [2, 3, 768, 768], P(None, None, None, 'narrow')
- grad_attnbias: float32 [2, 2, 768], P(None, None, 'narrow')
- grad_combiner: float32 [2, 768, 768], P(None, 'narrow')
- grad_combbias: float32 [2, 768], replicated
- grad_expander: float32 [2, 768, 3072], P(None, None, 'narrow')
- grad_expbias: float32 [2, 3072], P(None, 'narrow')
- grad_reducer: float32 [2, 3072, 768], P(None, 'narrow')
- grad_redbias: float32 [2, 768], replicated
The draws below stay inside these ranges and needn't reach their ends.
Inputs may be any that keep to these rules, and one draw needn't show every extreme that they name: `mask_slots`: positions within the clip; a position may appear more than once.
All inputs are finite; a program needn't handle non-finite values. No bound on the sum of `token_kind` on one device may be relied on, other than what follows from the above.
Results may differ from the reference program's by a relative error of at most 0.025.
Values may be sent and summed in bfloat16 or wider, within the bound.
A program may use at most 128 MiB of HBM per device.

```python
from functools import partial
import jax
import jax.numpy as jnp
from jax import lax

D = 768
HEADS = 12
HD = 64
FF = 3072
PATCH = 256
SEQ = 256
LAYERS = 2
MASKED = 64
CLIPS_DEV = 2
CLIPS = 16
TOKENS = 4096


def touch_ends(array, key, low, largest):
    extent = array.shape
    spot = [jax.random.randint(jax.random.fold_in(key, axis), (), 0, extent[axis]) for axis in range(len(extent))]
    array = array.at[tuple(spot)].set(low)
    longest = extent.index(max(extent))
    spot[longest] = (spot[longest] + 1) % extent[longest]
    return array.at[tuple(spot)].set(largest)


def shard_levels(own_key, shape, split, low, top_value):
    def one(dim, blocks):
        steps = jax.random.uniform(jax.random.fold_in(jax.random.fold_in(own_key, 6), dim), (blocks,), jnp.float32, low / len(split), top_value / len(split))
        return jnp.repeat(jnp.exp(steps), shape[dim] // blocks).reshape((-1,) + (1,) * (len(shape) - dim - 1))

    level = one(*split[0])
    for cut in split[1:]:
        level = level * one(*cut)
    return level


def gaussian(stream_key, dims, spread, limit, cuts=(), kind=jnp.bfloat16):
    entries = jax.random.normal(stream_key, dims, jnp.float32) * spread
    if len(cuts) > 0:
        entries = shard_levels(stream_key, dims, cuts, -0.22, 0.18) * entries
    return jnp.clip(entries, min=-limit, max=limit).astype(kind)


def setup_inputs(seed: int = 0) -> dict:
    key_of = jax.random.split(jax.random.key(seed), 19)
    patches = gaussian(key_of[0], (TOKENS, PATCH), 1.0, 6.0, ((0, 32),))
    token_kind = touch_ends((jax.random.randint(key_of[1], (TOKENS,), 0, 2) < 1).astype(jnp.int32), jax.random.fold_in(key_of[1], 1), 0, 1)
    mask_slots = touch_ends(jax.random.randint(key_of[2], (CLIPS, MASKED), 0, SEQ), jax.random.fold_in(key_of[2], 1), 0, SEQ - 1).astype(jnp.int32)
    projector = gaussian(key_of[3], (2, PATCH, D), PATCH ** -0.5, 0.375)
    offsets = gaussian(key_of[4], (2, D), 0.5, 3.0)
    placeholder = gaussian(key_of[5], (D,), 1.0, 4.0)
    positions = gaussian(key_of[6], (SEQ, D), 0.5, 3.0)
    scales = jnp.clip(1.0 + 0.1 * jax.random.normal(key_of[7], (LAYERS, 2, D), jnp.float32), 0.5, 1.5).astype(jnp.bfloat16)
    shifts = gaussian(key_of[8], (LAYERS, 2, D), 0.5, 3.0)
    attention = gaussian(key_of[9], (LAYERS, 3, D, D), D ** -0.5, 0.21875, ((3, 4),))
    attn_bias = gaussian(key_of[10], (LAYERS, 2, D), 0.5, 3.0, ((2, 4),))
    combiner = gaussian(key_of[11], (LAYERS, D, D), (D // 64) ** -0.5, 1.75, ((1, 4),))
    comb_bias = gaussian(key_of[12], (LAYERS, D), 0.5, 3.0)
    expander = gaussian(key_of[13], (LAYERS, D, FF), D ** -0.5, 0.21875, ((2, 4),))
    expand_bias = gaussian(key_of[14], (LAYERS, FF), 0.5, 3.0, ((1, 4),))
    reducer = gaussian(key_of[15], (LAYERS, FF, D), (FF // 2) ** -0.5, 0.15625, ((1, 4),))
    reduce_bias = gaussian(key_of[16], (LAYERS, D), 0.5, 3.0)
    cotangent = gaussian(key_of[17], (TOKENS, D), 1.0, 6.0, ((0, 32),))
    return {"patches": patches, "token_kind": token_kind, "mask_slots": mask_slots, "projector": projector, "offsets": offsets, "placeholder": placeholder, "positions": positions, "scales": scales, "shifts": shifts, "attention": attention, "attn_bias": attn_bias, "combiner": combiner, "comb_bias": comb_bias, "expander": expander, "expand_bias": expand_bias, "reducer": reducer, "reduce_bias": reduce_bias, "cotangent": cotangent}


@jax.custom_vjp
def low(v):
    return lax.optimization_barrier(v.astype(jnp.bfloat16)).astype(jnp.float32)

@jax.custom_vjp
def low_back(v):
    return v

def low_keep(v):
    return (low(v), None)

def low_pass(kept, grad):
    return (grad,)

def back_keep(v):
    return (v, None)

def back_low(kept, grad):
    return (low(grad),)
low.defvjp(low_keep, low_pass)
low_back.defvjp(back_keep, back_low)
norm_eps = 1e-06

def matmul(left, right):
    return jnp.matmul(left, right, precision=lax.Precision.HIGHEST)

def normalize(values, gain, shift):
    center = values - lax.optimization_barrier(jnp.mean(values, axis=-1, keepdims=True))
    variance = lax.optimization_barrier(jnp.mean(center * center, axis=-1, keepdims=True))
    return center * lax.rsqrt(variance + norm_eps) * gain + shift

def attend(inputs):
    query, key, value = inputs
    scores = low_back(jnp.einsum('bqhd,bkhd->bhqk', query, key, precision=lax.Precision.HIGHEST))
    top = lax.optimization_barrier(jnp.max(scores, axis=-1, keepdims=True))
    raised = jnp.exp(scores - top)
    weights = raised / lax.optimization_barrier(jnp.sum(raised, axis=-1, keepdims=True))
    return jnp.einsum('bhqk,bkhd->bqhd', low(weights), value, precision=lax.Precision.HIGHEST)

def forward(is_patch, masked, patches, projector, offsets, placeholder, positions, scales, shifts, attention, attn_bias, combiner, comb_bias, expander, expand_bias, reducer, reduce_bias):
    rows = patches.shape[0]
    clips = rows // SEQ
    groups = clips // CLIPS_DEV
    scale = HD ** (-0.5)
    lifted = low_back(jnp.where(is_patch, matmul(patches, projector[1]), matmul(patches, projector[0])))
    shifted = lifted + jnp.where(is_patch, offsets[1], offsets[0])
    embedded = jnp.where(masked, placeholder, shifted)
    stream = (embedded.reshape(clips, SEQ, D) + positions).reshape(rows, D)
    head_shape = (groups, CLIPS_DEV, SEQ, HEADS, HD)
    for layer in range(LAYERS):
        first = low(normalize(stream, scales[layer, 0], shifts[layer, 0]))
        query = low_back(low((matmul(first, attention[layer, 0]) + attn_bias[layer, 0]) * scale))
        key = low_back(low(matmul(first, attention[layer, 1])))
        value = low_back(low(matmul(first, attention[layer, 2]) + attn_bias[layer, 1]))
        mixed = lax.map(jax.checkpoint(attend), (query.reshape(head_shape), key.reshape(head_shape), value.reshape(head_shape)))
        mixed = low_back(low(mixed.reshape(rows, D)))
        middle = stream + low_back(matmul(mixed, combiner[layer])) + comb_bias[layer]
        second = low(normalize(middle, scales[layer, 1], shifts[layer, 1]))
        pre_act = low_back(matmul(second, expander[layer])) + expand_bias[layer]
        hidden = low(jax.nn.gelu(pre_act, approximate=False))
        stream = middle + low_back(matmul(hidden, reducer[layer])) + reduce_bias[layer]
    return stream

def reference(patches, token_kind, mask_slots, projector, offsets, placeholder, positions, scales, shifts, attention, attn_bias, combiner, comb_bias, expander, expand_bias, reducer, reduce_bias, cotangent):
    rows = patches.shape[0]
    place = jnp.arange(SEQ, dtype=jnp.int32)
    masked = jnp.any(mask_slots[:, :, None] == place[None, None, :], axis=1).reshape(rows, 1)
    is_patch = (token_kind == 1).reshape(rows, 1)
    floats = tuple((item.astype(jnp.float32) for item in (patches, projector, offsets, placeholder, positions, scales, shifts, attention, attn_bias, combiner, comb_bias, expander, expand_bias, reducer, reduce_bias)))
    encoded, pullback = jax.vjp(partial(forward, is_patch, masked), *floats)
    grads = pullback(cotangent.astype(jnp.float32))
    return (encoded, grads[0], grads[1], grads[2], grads[3], grads[4], grads[5], grads[6], grads[7], grads[8], grads[9], grads[10], grads[11], grads[12], grads[13], grads[14])
```

```python
import functools

import jax
import jax.numpy as jnp
from jax import lax
from jax.experimental import pallas as pl
from jax.experimental.pallas import tpu as pltpu
from jax.sharding import PartitionSpec as P

HD = 64
EPS = 1e-06
BF = jnp.bfloat16
F32 = jnp.float32
MESH = pl.DeviceIdType.MESH


def nn(left, right):
    return jnp.dot(left, right, preferred_element_type=F32)


def nt(left, right):
    return lax.dot_general(left, right, (((1,), (1,)), ((), ())), preferred_element_type=F32)


def tn(left, right):
    return lax.dot_general(left, right, (((0,), (0,)), ((), ())), preferred_element_type=F32)


def loop(count, body):
    def step(index, carry):
        body(index)
        return carry

    lax.fori_loop(0, count, step, 0)


def hat_of(values):
    center = values - jnp.mean(values, axis=-1, keepdims=True)
    variance = jnp.mean(center * center, axis=-1, keepdims=True)
    scale = lax.rsqrt(variance + EPS)
    return center * scale, scale


def column_sums(values):
    return jnp.sum(values, axis=0, keepdims=True)


class Copy:
    def __init__(self, src, dst, send, recv, target):
        self.args = dict(src_ref=src, dst_ref=dst, send_sem=send, recv_sem=recv, device_id=target, device_id_type=MESH)

    def start(self):
        pltpu.make_async_remote_copy(**self.args).start()

    def wait(self):
        pltpu.make_async_remote_copy(**self.args).wait()

    def wait_send(self):
        pltpu.make_async_remote_copy(**self.args).wait_send()

    def wait_recv(self):
        pltpu.make_async_remote_copy(**self.args).wait_recv()


def add_into(dst, dst_row, src, src_row, rows):
    block = next(b for b in (96, 64, 112, 48, 32, 16) if rows % b == 0)

    def step(index):
        into = pl.ds(pl.multiple_of(dst_row + index * block, 16), block)
        give = pl.ds(pl.multiple_of(src_row + index * block, 16), block)
        dst[into, :] = (dst[into, :].astype(F32) + src[give, :].astype(F32)).astype(BF)

    loop(rows // block, step)


class Place:
    def __init__(self, wide_count):
        self.w = lax.axis_index("wide")
        self.n = lax.axis_index("narrow")
        self.y = self.n // 2
        self.c = self.n % 2
        self.x = self.w % 2
        self.z = self.w // 2
        line = wide_count // 2
        self.half = line // 2
        self.low = self.z < self.half
        self.side = jnp.where(self.low, 0, 1)
        self.depth = jnp.where(self.low, self.z, line - 1 - self.z)
        step = jnp.where(self.low, 2, -2)
        self.sibling = (self.w, self.n + 1 - 2 * self.c)
        self.partner = (self.w, self.n + 2 - 4 * self.y)
        self.pair = (self.w + 1 - 2 * self.x, self.n)
        self.inward = (self.w + step, self.n)
        self.outward = (self.w - jnp.where(self.depth > 0, step, -step), self.n)
        self.has_out = self.depth > 0
        self.inner = self.depth == self.half - 1


def hops(count, hop):
    if count == 1:
        hop(0)
    elif count > 1:
        loop(count, hop)


class PairFirst:
    def __init__(self, place, total, row, rows, buf, at, out, send, recv, store):
        self.place, self.total, self.buf = place, total, buf
        half = rows // 2
        self.half, self.at = half, at
        mine = pl.multiple_of(row + place.x * half, 16)
        other = pl.multiple_of(row + (1 - place.x) * half, 16)
        self.mine = mine
        keep, give = total.at[pl.ds(mine, half)], total.at[pl.ds(other, half)]
        out_keep, out_give = out.at[pl.ds(mine, half)], out.at[pl.ds(other, half)]
        slots = [buf.at[pl.ds(at + k * half, half)] for k in range(3)]
        self.pair_in = Copy(give, slots[0], send.at[0], recv.at[0], place.pair)
        self.line_in = Copy(keep, slots[1], send.at[1], recv.at[1], place.inward)
        self.middle = Copy(keep, slots[2], send.at[2], recv.at[2], place.inward)
        self.line_out = Copy(keep, out_keep, send.at[3], recv.at[3], place.outward)
        self.line_on = Copy(out_keep, out_keep, send.at[3], recv.at[3], place.outward)
        self.pair_out = Copy(keep, out_keep, send.at[4], recv.at[4], place.pair)
        self.pair_on = Copy(out_keep, out_keep, send.at[4], recv.at[4], place.pair)
        self.other = Copy(out_give, out_give, send.at[4], recv.at[4], place.pair)
        self.store = pltpu.make_async_copy(keep, out_keep, store)
        self.stages = [self.s0, self.s1, self.s2, self.s3, self.s4, self.s5]

    def s0(self):
        self.pair_in.start()

    def s1(self):
        place = self.place
        self.pair_in.wait()
        add_into(self.total, self.mine, self.buf, self.at, self.half)
        if place.half == 1:
            self.middle.start()
            return

        @pl.when(place.depth == 0)
        def _():
            self.line_in.start()

    def s2(self):
        place = self.place

        def hop(k):
            @pl.when(place.depth == k + 1)
            def _():
                self.line_in.wait_recv()
                add_into(self.total, self.mine, self.buf, self.at + self.half, self.half)

            @pl.when((place.depth == k + 1) & jnp.logical_not(place.inner))
            def _():
                self.line_in.start()

        hops(place.half - 1, hop)
        if place.half > 1:

            @pl.when(place.inner)
            def _():
                self.middle.start()

    def s3(self):
        place = self.place

        @pl.when(place.inner)
        def _():
            self.middle.wait()
            add_into(self.total, self.mine, self.buf, self.at + 2 * self.half, self.half)
            if place.half > 1:
                self.line_out.start()
            self.pair_out.start()
            self.store.start()

    def s4(self):
        place = self.place

        def hop(k):
            @pl.when(place.depth == place.half - 2 - k)
            def _():
                self.line_on.wait_recv()
                self.pair_on.start()

            @pl.when((place.depth == place.half - 2 - k) & place.has_out)
            def _():
                self.line_on.start()

        hops(place.half - 1, hop)

    def s5(self):
        place = self.place

        @pl.when(place.inner)
        def _():
            self.store.wait()

        if place.half > 1:

            @pl.when(jnp.logical_not(place.inner))
            def _():
                self.line_in.wait_send()

            @pl.when(place.has_out)
            def _():
                self.line_out.wait_send()

        self.pair_out.wait_send()
        self.other.wait_recv()


class LineFirst:
    def __init__(self, place, total, row, rows, buf, at, out, send, recv, store):
        self.place, self.total, self.buf = place, total, buf
        half = rows // 2
        self.row, self.rows, self.half, self.at = row, rows, half, at
        mine = pl.multiple_of(row + place.side * half, 16)
        other = pl.multiple_of(row + (1 - place.side) * half, 16)
        self.mine = mine
        whole = total.at[pl.ds(row, rows)]
        keep, give = total.at[pl.ds(mine, half)], total.at[pl.ds(other, half)]
        out_keep, out_give = out.at[pl.ds(mine, half)], out.at[pl.ds(other, half)]
        self.line_in = Copy(whole, buf.at[pl.ds(at, rows)], send.at[0], recv.at[0], place.inward)
        self.middle = Copy(give, buf.at[pl.ds(at + rows, half)], send.at[1], recv.at[1], place.inward)
        self.across = Copy(keep, buf.at[pl.ds(at + rows + half, half)], send.at[2], recv.at[2], place.pair)
        self.middle_out = Copy(keep, out_keep, send.at[3], recv.at[3], place.inward)
        self.middle_back = Copy(out_give, out_give, send.at[3], recv.at[3], place.inward)
        self.keep_out = Copy(keep, out_keep, send.at[4], recv.at[4], place.outward)
        self.keep_on = Copy(out_keep, out_keep, send.at[4], recv.at[4], place.outward)
        self.give_on = Copy(out_give, out_give, send.at[5], recv.at[5], place.outward)
        self.store = pltpu.make_async_copy(keep, out_keep, store)
        self.stages = [self.s0, self.s1, self.s2, self.s3, self.s4, self.s5]

    def s0(self):
        place = self.place
        if place.half == 1:
            self.middle.start()
            return

        @pl.when(place.depth == 0)
        def _():
            self.line_in.start()

    def s1(self):
        place = self.place

        def hop(k):
            @pl.when(place.depth == k + 1)
            def _():
                self.line_in.wait_recv()
                add_into(self.total, self.row, self.buf, self.at, self.rows)

            @pl.when((place.depth == k + 1) & jnp.logical_not(place.inner))
            def _():
                self.line_in.start()

        hops(place.half - 1, hop)
        if place.half > 1:

            @pl.when(place.inner)
            def _():
                self.middle.start()

    def s2(self):
        @pl.when(self.place.inner)
        def _():
            self.middle.wait()
            add_into(self.total, self.mine, self.buf, self.at + self.rows, self.half)
            self.across.start()

    def s3(self):
        place = self.place

        @pl.when(place.inner)
        def _():
            self.across.wait()
            add_into(self.total, self.mine, self.buf, self.at + self.rows + self.half, self.half)
            self.middle_out.start()
            if place.half > 1:
                self.keep_out.start()
            self.store.start()

    def s4(self):
        place = self.place

        @pl.when(place.inner)
        def _():
            self.middle_back.wait_recv()
            if place.half > 1:
                self.give_on.start()

    def s5(self):
        place = self.place

        def hop(k):
            @pl.when(place.depth == place.half - 2 - k)
            def _():
                self.keep_on.wait_recv()
                self.give_on.wait_recv()

            @pl.when((place.depth == place.half - 2 - k) & place.has_out)
            def _():
                self.keep_on.start()
                self.give_on.start()

        hops(place.half - 1, hop)

        @pl.when(place.inner)
        def _():
            self.middle_out.wait_send()
            self.store.wait()

        if place.half > 1:

            @pl.when(jnp.logical_not(place.inner))
            def _():
                self.line_in.wait_send()

            @pl.when(place.has_out)
            def _():
                self.keep_out.wait_send()
                self.give_on.wait_send()


def encoder(
    wide_count,
    rows_in,
    cot_in,
    slots_in,
    proj_in,
    offs_in,
    plc_in,
    pos_in,
    scales,
    shifts,
    att_in,
    abias_in,
    comb_in,
    cbias,
    exp_in,
    ebias_in,
    red_in,
    rbias,
    sums_out,
    shared_out,
    encoded_out,
    patches_out,
    wa,
    wc,
    we,
    wr,
    abias,
    ebias,
    proj,
    pos,
    rows_all,
    grad,
    stream,
    middle,
    first,
    second,
    qkv,
    probs,
    mixed,
    slope,
    hidden,
    out_round,
    pre,
    mid_round,
    grad_mixed,
    grad_qkv,
    key_acc,
    acc,
    give,
    take,
    take_top,
    cot,
    send_part,
    recv_part,
    total,
    ring,
    shared,
    shared_buf,
    top_own,
    top_other,
    patch_own,
    patch_other,
    small,
    bias_rows,
    load_sem,
    weight_send,
    weight_recv,
    rows_send,
    rows_recv,
    y_send,
    y_recv,
    part_send,
    part_recv,
    ring_send,
    ring_recv,
    shared_send,
    shared_recv,
    last_send,
    last_recv,
    store_sem,
    credit,
):
    place = Place(wide_count)
    y, c, w, n = place.y, place.c, place.w, place.n
    sibling, partner = place.sibling, place.partner
    local, width = cot_in.shape
    patch = proj_in.shape[0] // 2
    seq = pos_in.shape[0]
    layers = scales.shape[0]
    cols = att_in.shape[3]
    heads = cols // HD
    hid = exp_in.shape[2]
    scale = HD ** (-0.5)
    diagonal = y == c
    chunks = seq // local

    barrier = pltpu.get_barrier_semaphore()
    for step in (1, 2, 3):
        pl.semaphore_signal(barrier, 1, device_id=(w, (n + step) % 4), device_id_type=MESH)
    pl.semaphore_signal(barrier, 1, device_id=place.pair, device_id_type=MESH)
    pl.semaphore_signal(barrier, 1, device_id=place.inward, device_id_type=MESH)

    @pl.when(place.has_out)
    def _():
        pl.semaphore_signal(barrier, 1, device_id=place.outward, device_id_type=MESH)
        pl.semaphore_wait(barrier, 6)

    @pl.when(jnp.logical_not(place.has_out))
    def _():
        pl.semaphore_wait(barrier, 5)

    def span(index, size):
        return pl.ds(pl.multiple_of(index * size, size), size)

    far = (w, 2 - y)
    near = (w, 3 * y)
    here = span(c, local)
    row_copies = []
    for k, (src, dst) in enumerate(((rows_in, rows_all), (cot_in, cot))):
        row_copies.append(
            (
                Copy(src, dst.at[here], rows_send.at[k, 0], rows_recv.at[k, c], far),
                Copy(src, dst.at[here], rows_send.at[k, 1], rows_recv.at[k, c], near),
                pltpu.make_async_copy(src, dst.at[here], rows_recv.at[k, c]),
            )
        )

    def send_rows(k):
        to_far, to_near, to_self = row_copies[k]
        to_far.start()

        @pl.when(diagonal)
        def _():
            to_self.start()

        @pl.when(jnp.logical_not(diagonal))
        def _():
            to_near.start()

    def wait_rows(k, dst):
        for h in range(2):
            spot = dst.at[pl.ds(h * local, local)]
            pltpu.make_async_copy(spot, spot, rows_recv.at[k, h]).wait()

    send_rows(0)
    weights = []
    for layer in range(layers):
        for src, dst in ((att_in, wa), (comb_in, wc), (exp_in, we), (red_in, wr)):
            weights.append((src.at[layer], dst.at[layer]))
    own_loads = [pltpu.make_async_copy(src, dst.at[0], load_sem.at[k]) for k, (src, dst) in enumerate(weights)]
    sib_loads = [
        Copy(src, dst.at[1], weight_send.at[k], weight_recv.at[k], sibling) for k, (src, dst) in enumerate(weights)
    ]
    proj_load = pltpu.make_async_copy(proj_in, proj, load_sem.at[8])
    pos_load = pltpu.make_async_copy(pos_in, pos, load_sem.at[9])
    abias_copy = Copy(abias_in, abias.at[1], weight_send.at[8], weight_recv.at[8], sibling)
    ebias_copy = Copy(ebias_in, ebias.at[1], weight_send.at[9], weight_recv.at[9], sibling)
    abias_copy.start()
    ebias_copy.start()
    proj_load.start()
    pos_load.start()
    for k in range(8):
        own_loads[k].start()
        sib_loads[k].start()
        if k == 3:
            send_rows(1)
    abias[0] = abias_in[...]
    ebias[0] = ebias_in[...]
    small[...] = jnp.zeros_like(small)
    bias_rows[...] = jnp.zeros_like(bias_rows)

    def need(k):
        own_loads[k].wait()
        sib_loads[k].wait_recv()

    def note(row, values):
        small[row : row + 1, :] += column_sums(values)

    def param(ref, layer, row):
        return ref[layer, row : row + 1, :].astype(F32)

    def y_copy(index, slot, rows):
        return Copy(
            give.at[slot, rows], take.at[slot, rows], y_send.at[index[0], index[1]], y_recv.at[index[0], index[1]], partner
        )

    def offer(exchange, slot, ch, values):
        rows = span(ch, local)
        give[slot, rows, :] = values.astype(BF)
        y_copy((exchange, ch), slot, rows).start()

    def collect(exchange, slot, ch):
        rows = span(ch, local)
        y_copy((exchange, ch), slot, rows).wait()
        return give[slot, rows, :].astype(F32) + take[slot, rows, :].astype(F32)

    def head_mask(rows, h):
        lane = lax.broadcasted_iota(jnp.int32, (rows, cols), 1)
        return (lane >= h * HD) & (lane < (h + 1) * HD)

    place_col = lax.broadcasted_iota(jnp.int32, (seq, slots_in.shape[1]), 0)
    slot_row = slots_in[pl.ds(c, 1), :]
    masked = jnp.max(jnp.where(place_col == slot_row, 1.0, 0.0).astype(F32), axis=1, keepdims=True)
    wait_rows(0, rows_all)
    proj_load.wait()
    pos_load.wait()
    flags = rows_all[:, patch : patch + 128]
    wide_flags = jnp.concatenate([flags] * (patch // 128), axis=1)
    patches = rows_all[:, :patch]
    kind_one = patches * wide_flags
    kind_zero = patches - kind_one
    is_one = flags[:, 0:1].astype(F32)
    lifted = nn(kind_zero, proj[0:patch, :]) + nn(kind_one, proj[patch : 2 * patch, :])
    offset = jnp.where(is_one > 0.5, offs_in[1:2, :].astype(F32), offs_in[0:1, :].astype(F32))
    stream[0] = jnp.where(masked > 0.5, plc_in[...].astype(F32), lifted + offset) + pos[...].astype(F32)

    def before_attention(layer):
        def norm(ch):
            rows = span(ch, local)
            hat, _ = hat_of(stream[layer, rows, :])
            first[layer, rows, :] = (hat * param(scales, layer, 0) + param(shifts, layer, 0)).astype(BF)

        loop(chunks, norm)

    def project(layer):
        need(4 * layer)
        if layer == 0:
            abias_copy.wait_recv()
            ebias_copy.wait_recv()

        def group(g):
            rows = first[layer]
            query = (nn(rows, wa[layer, g, 0]) + abias[g, layer, 0:1, :].astype(F32)) * scale
            qkv[layer, g, 0] = query.astype(BF)
            qkv[layer, g, 1] = nn(rows, wa[layer, g, 1]).astype(BF)
            qkv[layer, g, 2] = (nn(rows, wa[layer, g, 2]) + abias[g, layer, 1:2, :].astype(F32)).astype(BF)

        loop(2, group)

    def attend(layer, exchange, slot):
        need(4 * layer + 1)

        def chunk(ch):
            rows = span(ch, local)

            def group(g):
                total_mixed = jnp.zeros((local, cols), F32)
                query, key, value = qkv[layer, g, 0, rows, :], qkv[layer, g, 1], qkv[layer, g, 2]
                for h in range(heads):
                    scores = nt(jnp.where(head_mask(local, h), query, 0), key)
                    raised = jnp.exp(scores - jnp.max(scores, axis=-1, keepdims=True))
                    prob = (raised / jnp.sum(raised, axis=-1, keepdims=True)).astype(BF)
                    probs[layer, g * heads + h, rows, :] = prob
                    total_mixed += nn(prob, jnp.where(head_mask(seq, h), value, 0))
                mixed[layer, g, rows, :] = total_mixed.astype(BF)

            loop(2, group)
            offer(exchange, slot, ch, nn(mixed[layer, 0, rows, :], wc[layer, 0]) + nn(mixed[layer, 1, rows, :], wc[layer, 1]))

        loop(chunks, chunk)

    def to_middle(layer, exchange, slot, ch):
        rows = span(ch, local)
        values = stream[layer, rows, :] + collect(exchange, slot, ch) + cbias[layer : layer + 1, :].astype(F32)
        middle[layer, rows, :] = values
        hat, _ = hat_of(values)
        second[layer, rows, :] = (hat * param(scales, layer, 1) + param(shifts, layer, 1)).astype(BF)

    def activate(layer, g, rows):
        value = nn(second[layer, rows, :], we[layer, g]) + ebias[g, layer : layer + 1, :].astype(F32)
        cdf = 0.5 * (1.0 + lax.erf(value * (0.5**0.5)))
        hidden[layer, g, rows, :] = (value * cdf).astype(BF)
        density = jnp.exp(-0.5 * value * value) * 0.3989422804014327
        slope[layer, g, rows, :] = (cdf + value * density).astype(BF)

    def feed_back(layer, g, rows):
        grad_hidden = nt(out_round[rows, :], wr[layer, g])
        grad_pre = grad_hidden * slope[layer, g, rows, :].astype(F32)
        bias_rows[layer, g, 0:1, :] += column_sums(grad_pre)
        pre[g, rows, :] = grad_pre.astype(BF)

    def settle(row, layer, part, base, values, gain_row):
        hat, inverse = hat_of(base)
        note(2 * layer + part, values * hat)
        note(4 + 2 * layer + part, values)
        scaled = values * param(scales, layer, part)
        inner = scaled - jnp.mean(scaled, axis=-1, keepdims=True)
        return inverse * (inner - hat * jnp.mean(scaled * hat, axis=-1, keepdims=True))

    for layer in range(layers):
        before_attention(layer)
        project(layer)
        attend(layer, 2 * layer, 0)
        need(4 * layer + 2)
        need(4 * layer + 3)
        if layer + 1 < layers:

            def chunk(ch):
                rows = span(ch, local)
                to_middle(layer, 2 * layer, 0, ch)

                def group(g):
                    activate(layer, g, rows)
                    part = nn(hidden[layer, g, rows, :], wr[layer, g])

                    @pl.when(g == 0)
                    def _():
                        acc[...] = part

                    @pl.when(g == 1)
                    def _():
                        acc[...] += part

                loop(2, group)
                offer(2 * layer + 1, 1, ch, acc[...])

            loop(chunks, chunk)

            def after(ch):
                rows = span(ch, local)
                stream[layer + 1, rows, :] = (
                    middle[layer, rows, :] + collect(2 * layer + 1, 1, ch) + rbias[layer : layer + 1, :].astype(F32)
                )

            loop(chunks, after)

    pieces = []
    base = 0
    at = 0
    plan = (
        (PairFirst, 0, hid // 2),
        (PairFirst, hid // 2, hid // 2),
        (LineFirst, hid, hid // 2),
        (LineFirst, hid + hid // 2, hid // 2),
        (PairFirst, 2 * hid, 2 * cols),
        (PairFirst, 2 * hid + 2 * cols, cols),
        (LineFirst, 2 * hid + 3 * cols, cols + 32),
    )
    per_layer = len(plan)
    for layer in reversed(range(layers)):
        for kind, row, count in plan:
            k = len(pieces)
            pieces.append((kind(place, total.at[layer], row, count, ring, at, sums_out.at[layer], ring_send.at[k], ring_recv.at[k], store_sem.at[k]), layer, row, count))
            at += count // 2 * 3 if kind is PairFirst else count * 2

    def parts(k, own, other):
        piece, layer, row, count = pieces[k]
        slot = k % 2
        copy = Copy(
            send_part.at[slot, pl.ds(0, count)], recv_part.at[pl.ds(row, count)], part_send.at[k], part_recv.at[k], sibling
        )
        if k >= 2:
            old = pieces[k - 2]
            Copy(
                send_part.at[slot, pl.ds(0, old[3])],
                recv_part.at[pl.ds(old[2], old[3])],
                part_send.at[k - 2],
                part_recv.at[k - 2],
                sibling,
            ).wait_send()
        if k == per_layer:
            pl.semaphore_wait(credit, 1)
        other(send_part.at[slot])
        copy.start()
        own(total.at[layer, pl.ds(row, count)])
        copy.wait_recv()
        add_into(total.at[layer], row, recv_part, row, count)
        if k == per_layer - 1:
            pl.semaphore_signal(credit, 1, device_id=sibling, device_id_type=MESH)
        piece.stages[0]()

    done = {}

    def advance(k):
        stage = done.get(k, 1)
        if stage < 6:
            pieces[k][0].stages[stage]()
        done[k] = stage + 1

    def weight_grad(left, right, g):
        count = left.shape[1] // 128

        def into(ref):
            def step(t):
                ref[span(t, 128), :] = tn(left[:, span(t, 128)], right).astype(BF)

            loop(count, step)

        return into

    def feed_grads(layer, base):
        for t in range(2):
            cut = pl.ds(t * (hid // 2), hid // 2)
            parts(
                base + t,
                weight_grad(second.at[layer, :, cut], pre[0], 0),
                weight_grad(second.at[layer, :, cut], pre[1], 1),
            )
        for t in range(2):
            cut = pl.ds(t * (hid // 2), hid // 2)
            parts(
                base + 2 + t,
                weight_grad(hidden.at[layer, 0, :, cut], out_round[...], 0),
                weight_grad(hidden.at[layer, 1, :, cut], out_round[...], 1),
            )

    def attention_grads(layer, base):
        def stack(g, which):
            def into(ref):
                for j, index in enumerate(which):
                    ref[pl.ds(j * cols, cols), :] = tn(grad_qkv[g, index], first[layer]).astype(BF)

            return into

        def comb(g):
            def into(ref):
                ref[pl.ds(0, cols), :] = tn(mixed[layer, g], mid_round[...]).astype(BF)
                ref[pl.ds(cols, 32), :] = bias_rows[layer, g].astype(BF)

            return into

        parts(base + 4, stack(0, (0, 1)), stack(1, (0, 1)))
        parts(base + 5, stack(0, (2,)), stack(1, (2,)))
        parts(base + 6, comb(0), comb(1))

    wait_rows(1, cot)
    last = layers - 1

    def start_back(ch):
        rows = span(ch, local)
        grad[rows, :] = cot[rows, :].astype(F32)

    loop(chunks, start_back)

    def top_send():
        return Copy(top_other, top_own, last_send.at[0], last_recv.at[0], sibling)

    top_copy = Copy(give.at[2], take_top, last_send.at[1], last_recv.at[1], partner)

    for layer in reversed(range(layers)):
        base = (last - layer) * per_layer
        exchange = 4 + 2 * (last - layer)

        def chunk(ch):
            rows = span(ch, local)
            note(10 + layer, grad[rows, :])
            out_round[rows, :] = grad[rows, :].astype(BF)
            if layer == last:
                to_middle(layer, 2 * layer, 0, ch)

            def group(g):
                if layer == last:
                    activate(layer, g, rows)
                feed_back(layer, g, rows)
                part = nt(pre[g, rows, :], we[layer, g])

                @pl.when(g == 0)
                def _():
                    acc[...] = part

                @pl.when(g == 1)
                def _():
                    acc[...] += part

            loop(2, group)
            offer(exchange, 1, ch, acc[...])

        loop(chunks, chunk)

        if layer == last:

            def top(ch):
                rows = span(ch, local)
                give[2, rows, :] = (
                    nn(hidden[layer, 0, rows, :], wr[layer, 0]) + nn(hidden[layer, 1, rows, :], wr[layer, 1])
                ).astype(BF)

            loop(chunks, top)

            @pl.when(jnp.logical_not(diagonal))
            def _():
                top_copy.start()

        feed_grads(layer, base)

        def chunk(ch):
            rows = span(ch, local)
            grad_second = collect(exchange, 1, ch)
            grad_middle = grad[rows, :] + settle(rows, layer, 1, middle[layer, rows, :], grad_second, None)
            note(8 + layer, grad_middle)
            grad[rows, :] = grad_middle
            mid_round[rows, :] = grad_middle.astype(BF)

            def group(g):
                mixed_back = nt(mid_round[rows, :], wc[layer, g]).astype(BF)
                query, key, value = qkv[layer, g, 0, rows, :], qkv[layer, g, 1], qkv[layer, g, 2]
                query_acc = jnp.zeros((local, cols), F32)
                key_sum = jnp.zeros((seq, cols), F32)
                value_sum = jnp.zeros((seq, cols), F32)
                for h in range(heads):
                    prob = probs[layer, g * heads + h, rows, :]
                    back = jnp.where(head_mask(local, h), mixed_back, 0)
                    grad_probs = nt(back, value)
                    value_sum += tn(prob, back)
                    weight = prob.astype(F32)
                    center = jnp.sum(weight * grad_probs, axis=-1, keepdims=True)
                    grad_scores = (weight * (grad_probs - center)).astype(BF)
                    query_acc += nn(grad_scores, jnp.where(head_mask(seq, h), key, 0))
                    key_sum += tn(grad_scores, jnp.where(head_mask(local, h), query, 0))
                grad_query = (query_acc.astype(BF).astype(F32) * scale).astype(BF)
                grad_qkv[g, 0, rows, :] = grad_query
                bias_rows[layer, g, 1:2, 0:cols] += column_sums(grad_query.astype(F32))

                @pl.when(ch == 0)
                def _():
                    key_acc[g, 0] = key_sum
                    key_acc[g, 1] = value_sum

                @pl.when(ch > 0)
                def _():
                    key_acc[g, 0] += key_sum
                    key_acc[g, 1] += value_sum

            loop(2, group)

        loop(chunks, chunk)

        def close(g):
            grad_qkv[g, 1] = key_acc[g, 0].astype(BF)
            grad_value = key_acc[g, 1].astype(BF)
            grad_qkv[g, 2] = grad_value
            bias_rows[layer, g, 2:3, 0:cols] += column_sums(grad_value.astype(F32))

        loop(2, close)

        def chunk(ch):
            rows = span(ch, local)

            def group(g):
                part = (
                    nt(grad_qkv[g, 0, rows, :], wa[layer, g, 0])
                    + nt(grad_qkv[g, 1, rows, :], wa[layer, g, 1])
                    + nt(grad_qkv[g, 2, rows, :], wa[layer, g, 2])
                )

                @pl.when(g == 0)
                def _():
                    acc[...] = part

                @pl.when(g == 1)
                def _():
                    acc[...] += part

            loop(2, group)
            offer(exchange + 1, 0, ch, acc[...])

        loop(chunks, chunk)
        attention_grads(layer, base)

        if layer == last:

            @pl.when(jnp.logical_not(diagonal))
            def _():
                top_copy.wait_send()

            @pl.when(diagonal)
            def _():
                top_copy.wait_recv()

                def finish_top(dst, half):
                    rows = span(half, local)
                    dst[...] = (
                        middle[layer, rows, :]
                        + (give[2, rows, :].astype(F32) + take_top[rows, :].astype(F32))
                        + rbias[layer : layer + 1, :].astype(F32)
                    )

                finish_top(top_other, 1 - c)
                top_send().start()
                finish_top(top_own, c)

        def chunk(ch):
            rows = span(ch, local)
            grad_first = collect(exchange + 1, 0, ch)
            grad[rows, :] += settle(rows, layer, 0, stream[layer, rows, :], grad_first, None)

        loop(chunks, chunk)

    lifted_grad = jnp.where(masked > 0.5, 0.0, grad[...])
    note(14, grad[...] - lifted_grad)
    one_grad = jnp.where(is_one > 0.5, lifted_grad, 0.0)
    note(12, lifted_grad - one_grad)
    note(13, one_grad)
    lifted_round = lifted_grad.astype(BF)
    shared_rows = shared.shape[0]
    half_rows = shared_rows // 2
    flag_side = jnp.where(y == 1, wide_flags.astype(F32), 1.0 - wide_flags.astype(F32)).astype(BF)
    shared[0:patch, :] = tn(rows_all[:, :patch] * flag_side, lifted_round).astype(BF)
    shared[patch : patch + local, :] = grad[span(y, local), :].astype(BF)
    shared[patch + local : shared_rows, :] = small[...].astype(BF)
    keep_row, give_row = span(c, half_rows), span(1 - c, half_rows)
    shared_part = Copy(
        shared.at[give_row], shared_buf.at[pl.ds(0, half_rows)], last_send.at[2], last_recv.at[2], sibling
    )
    shared_part.start()

    patch_copy = Copy(patch_other, patch_own, last_send.at[3], last_recv.at[3], sibling)

    @pl.when(diagonal)
    def _():
        def half_back(dst, half):
            rows = span(half, local)
            flag = rows_all[rows, patch : patch + 128].astype(F32)[:, 0:1]
            masks = jnp.max(
                jnp.where(
                    lax.broadcasted_iota(jnp.int32, (local, slots_in.shape[1]), 0) + half * local == slot_row, 1.0, 0.0
                ).astype(F32),
                axis=1,
                keepdims=True,
            )
            values = jnp.where(masks > 0.5, 0.0, grad[rows, :]).astype(BF)
            dst[...] = jnp.where(flag > 0.5, nt(values, proj[patch : 2 * patch, :]), nt(values, proj[0:patch, :]))

        half_back(patch_other, 1 - c)
        patch_copy.start()
        half_back(patch_own, c)

    shared_part.wait()
    add_into(shared, pl.multiple_of(c * half_rows, 16), shared_buf, 0, half_rows)
    shared_piece = PairFirst(
        place,
        shared,
        pl.multiple_of(c * half_rows, 16),
        half_rows,
        shared_buf,
        half_rows,
        shared_out.at[y],
        shared_send,
        shared_recv,
        store_sem.at[len(pieces)],
    )
    shared_piece.stages[0]()

    count = len(pieces)
    for stage in range(1, 5):
        shared_piece.stages[stage]()
        for k in range(count):
            advance(k)
    shared_piece.stages[5]()
    across = Copy(shared_out.at[y, keep_row], shared_out.at[y, keep_row], last_send.at[4], last_recv.at[4], partner)
    across_back = Copy(
        shared_out.at[1 - y, keep_row], shared_out.at[1 - y, keep_row], last_send.at[4], last_recv.at[4], partner
    )
    across.start()
    for k in range(count):
        advance(k)
    across.wait_send()
    across_back.wait_recv()
    ends = []
    for k in range(2):
        ends.append(
            (
                Copy(
                    shared_out.at[k, keep_row], shared_out.at[k, keep_row], last_send.at[5 + k], last_recv.at[5 + k], sibling
                ),
                Copy(
                    shared_out.at[k, give_row], shared_out.at[k, give_row], last_send.at[5 + k], last_recv.at[5 + k], sibling
                ),
            )
        )
    for out, _ in ends:
        out.start()
    for out, back in ends:
        out.wait_send()
        back.wait_recv()

    @pl.when(diagonal)
    def _():
        top_send().wait_send()
        patch_copy.wait_send()

    @pl.when(jnp.logical_not(diagonal))
    def _():
        top_send().wait_recv()
        patch_copy.wait_recv()

    finals = (
        pltpu.make_async_copy(top_own, encoded_out, store_sem.at[count + 1]),
        pltpu.make_async_copy(patch_own, patches_out, store_sem.at[count + 2]),
    )
    for copy in finals:
        copy.start()
    for copy in finals:
        copy.wait()

    for to_far, to_near, _ in row_copies:
        to_far.wait_send()

        @pl.when(jnp.logical_not(diagonal))
        def _():
            to_near.wait_send()

    for copy in sib_loads + [abias_copy, ebias_copy]:
        copy.wait_send()
    for k in (count - 2, count - 1):
        piece, layer, row, size = pieces[k]
        Copy(
            send_part.at[k % 2, pl.ds(0, size)],
            recv_part.at[pl.ds(row, size)],
            part_send.at[k],
            part_recv.at[k],
            sibling,
        ).wait_send()


def per_device(
    wide_count,
    patches,
    token_kind,
    mask_slots,
    projector,
    offsets,
    placeholder,
    positions,
    scales,
    shifts,
    attention,
    attn_bias,
    combiner,
    comb_bias,
    expander,
    expand_bias,
    reducer,
    reduce_bias,
    cotangent,
):
    local, patch = patches.shape
    seq, width = positions.shape
    layers = scales.shape[0]
    cols = attention.shape[3]
    heads = cols // HD
    hid = expander.shape[2]
    flags = jnp.broadcast_to((token_kind == 1)[:, None], (local, 128)).astype(BF)
    rows_in = jnp.concatenate([patches, flags], axis=1)
    per_layer = 2 * hid + 4 * cols + 32
    shared_rows = patch + local + 64
    pieces = 7 * layers
    ring_rows = layers * (
        3 * (hid // 2) + 3 * cols + 3 * (cols // 2) + 2 * hid + 2 * (cols + 32)
    )
    vmem = pl.BlockSpec(memory_space=pltpu.VMEM)
    anyw = pl.BlockSpec(memory_space=pl.ANY)
    dma = pltpu.SemaphoreType.DMA
    scratch = [
        pltpu.VMEM((layers, 2, 3, width, cols), BF),
        pltpu.VMEM((layers, 2, cols, width), BF),
        pltpu.VMEM((layers, 2, width, hid), BF),
        pltpu.VMEM((layers, 2, hid, width), BF),
        pltpu.VMEM((2, layers, 2, cols), BF),
        pltpu.VMEM((2, layers, hid), BF),
        pltpu.VMEM((2 * patch, width), BF),
        pltpu.VMEM((seq, width), BF),
        pltpu.VMEM((seq, patch + 128), BF),
        pltpu.VMEM((seq, width), F32),
        pltpu.VMEM((layers, seq, width), F32),
        pltpu.VMEM((layers, seq, width), F32),
        pltpu.VMEM((layers, seq, width), BF),
        pltpu.VMEM((layers, seq, width), BF),
        pltpu.VMEM((layers, 2, 3, seq, cols), BF),
        pltpu.VMEM((layers, 2 * heads, seq, seq), BF),
        pltpu.VMEM((layers, 2, seq, cols), BF),
        pltpu.VMEM((layers, 2, seq, hid), BF),
        pltpu.VMEM((layers, 2, seq, hid), BF),
        pltpu.VMEM((seq, width), BF),
        pltpu.VMEM((2, seq, hid), BF),
        pltpu.VMEM((seq, width), BF),
        pltpu.VMEM((8, 128), BF),
        pltpu.VMEM((2, 3, seq, cols), BF),
        pltpu.VMEM((2, 2, seq, cols), F32),
        pltpu.VMEM((local, width), F32),
        pltpu.VMEM((3, seq, width), BF),
        pltpu.VMEM((2, seq, width), BF),
        pltpu.VMEM((seq, width), BF),
        pltpu.VMEM((seq, width), BF),
        pltpu.VMEM((2, 2 * cols, width), BF),
        pltpu.VMEM((per_layer, width), BF),
        pltpu.VMEM((layers, per_layer, width), BF),
        pltpu.VMEM((ring_rows, width), BF),
        pltpu.VMEM((shared_rows, width), BF),
        pltpu.VMEM((shared_rows // 2 + 3 * (shared_rows // 4), width), BF),
        pltpu.VMEM((local, width), F32),
        pltpu.VMEM((local, width), F32),
        pltpu.VMEM((local, patch), F32),
        pltpu.VMEM((local, patch), F32),
        pltpu.VMEM((64, width), F32),
        pltpu.VMEM((layers, 2, 32, width), F32),
        dma((10,)),
        dma((10,)),
        dma((10,)),
        dma((2, 2)),
        dma((2, 2)),
        dma((8, 2)),
        dma((8, 2)),
        dma((pieces,)),
        dma((pieces,)),
        dma((pieces, 6)),
        dma((pieces, 6)),
        dma((5,)),
        dma((5,)),
        dma((7,)),
        dma((7,)),
        dma((pieces + 3,)),
        pltpu.SemaphoreType.REGULAR,
    ]
    sums, shared, encoded, grad_patches = pl.pallas_call(
        functools.partial(encoder, wide_count),
        out_shape=(
            jax.ShapeDtypeStruct((layers, per_layer, width), BF),
            jax.ShapeDtypeStruct((2, shared_rows, width), BF),
            jax.ShapeDtypeStruct((local, width), F32),
            jax.ShapeDtypeStruct((local, patch), F32),
        ),
        in_specs=[anyw, anyw, vmem, anyw, vmem, vmem, anyw, vmem, vmem, anyw, vmem, anyw, vmem, anyw, vmem, anyw, vmem],
        out_specs=(anyw, anyw, anyw, anyw),
        scratch_shapes=scratch,
        compiler_params=pltpu.CompilerParams(
            collective_id=0, has_side_effects=True, vmem_limit_bytes=63 * 1024 * 1024 + 512 * 1024
        ),
        name="encoder",
    )(
        rows_in,
        cotangent,
        mask_slots,
        projector.reshape(2 * patch, width),
        offsets,
        placeholder.reshape(1, width),
        positions,
        scales,
        shifts,
        attention,
        attn_bias,
        combiner,
        comb_bias,
        expander,
        expand_bias,
        reducer,
        reduce_bias,
    )
    total = sums.astype(F32)
    both = shared.astype(F32)
    grad_expander = total[:, 0:hid]
    grad_reducer = total[:, hid : 2 * hid]
    grad_attention = total[:, 2 * hid : 2 * hid + 3 * cols].reshape(layers, 3, cols, width).transpose(0, 1, 3, 2)
    grad_combiner = total[:, 2 * hid + 3 * cols : 2 * hid + 4 * cols]
    bias = total[:, 2 * hid + 4 * cols :]
    grad_expbias = bias[:, 0, :]
    grad_attnbias = bias[:, 1:3, :cols]
    grad_projector = both[:, 0:patch]
    grad_positions = both[:, patch : patch + local].reshape(seq, width)
    small = both[0, patch + local :]
    return (
        encoded,
        grad_patches,
        grad_projector,
        small[12:14],
        small[14],
        grad_positions,
        small[0:4].reshape(layers, 2, width),
        small[4:8].reshape(layers, 2, width),
        grad_attention,
        grad_attnbias,
        grad_combiner,
        small[8:10],
        grad_expander,
        grad_expbias,
        grad_reducer,
        small[10:12],
    )


def solution(mesh):
    rows = ("wide", "narrow")
    return jax.shard_map(
        functools.partial(per_device, mesh.shape["wide"]),
        mesh=mesh,
        in_specs=(
            P(rows, None),
            P(rows),
            P("wide", None),
            P(),
            P(),
            P(),
            P(),
            P(),
            P(),
            P(None, None, None, "narrow"),
            P(None, None, "narrow"),
            P(None, "narrow", None),
            P(),
            P(None, None, "narrow"),
            P(None, "narrow"),
            P(None, "narrow", None),
            P(),
            P(rows, None),
        ),
        out_specs=(
            P(rows, None),
            P(rows, None),
            P(),
            P(),
            P(),
            P(),
            P(),
            P(),
            P(None, None, None, "narrow"),
            P(None, None, "narrow"),
            P(None, "narrow", None),
            P(),
            P(None, None, "narrow"),
            P(None, "narrow"),
            P(None, "narrow", None),
            P(),
        ),
        check_vma=False,
    )
```

```python
import functools

import jax
import jax.numpy as jnp
from jax import lax
from jax.experimental import pallas as pl
from jax.experimental.pallas import tpu as pltpu
from jax.sharding import PartitionSpec as P

HD = 64
EPS = 1e-06
BF = jnp.bfloat16
F32 = jnp.float32
MESH = pl.DeviceIdType.MESH


def nn(left, right):
    return jnp.dot(left, right, preferred_element_type=F32)


def nt(left, right):
    return lax.dot_general(left, right, (((1,), (1,)), ((), ())), preferred_element_type=F32)


def tn(left, right):
    return lax.dot_general(left, right, (((0,), (0,)), ((), ())), preferred_element_type=F32)


def loop(count, body):
    def step(index, carry):
        body(index)
        return carry

    lax.fori_loop(0, count, step, 0)


def hat_of(values):
    center = values - jnp.mean(values, axis=-1, keepdims=True)
    variance = jnp.mean(center * center, axis=-1, keepdims=True)
    scale = lax.rsqrt(variance + EPS)
    return center * scale, scale


def column_sums(values):
    return jnp.sum(values, axis=0, keepdims=True)


class Copy:
    def __init__(self, src, dst, send, recv, target):
        self.args = dict(src_ref=src, dst_ref=dst, send_sem=send, recv_sem=recv, device_id=target, device_id_type=MESH)

    def start(self):
        pltpu.make_async_remote_copy(**self.args).start()

    def wait(self):
        pltpu.make_async_remote_copy(**self.args).wait()

    def wait_send(self):
        pltpu.make_async_remote_copy(**self.args).wait_send()

    def wait_recv(self):
        pltpu.make_async_remote_copy(**self.args).wait_recv()


def add_into(dst, dst_row, src, src_row, rows):
    block = next(b for b in (96, 64, 112, 48, 32, 16) if rows % b == 0)

    def step(index):
        into = pl.ds(pl.multiple_of(dst_row + index * block, 16), block)
        give = pl.ds(pl.multiple_of(src_row + index * block, 16), block)
        dst[into, :] = (dst[into, :].astype(F32) + src[give, :].astype(F32)).astype(BF)

    loop(rows // block, step)


class Place:
    def __init__(self, wide_count):
        self.w = lax.axis_index("wide")
        self.n = lax.axis_index("narrow")
        self.y = self.n // 2
        self.c = self.n % 2
        self.x = self.w % 2
        self.z = self.w // 2
        line = wide_count // 2
        self.half = line // 2
        self.low = self.z < self.half
        self.side = jnp.where(self.low, 0, 1)
        self.depth = jnp.where(self.low, self.z, line - 1 - self.z)
        step = jnp.where(self.low, 2, -2)
        self.sibling = (self.w, self.n + 1 - 2 * self.c)
        self.partner = (self.w, self.n + 2 - 4 * self.y)
        self.pair = (self.w + 1 - 2 * self.x, self.n)
        self.inward = (self.w + step, self.n)
        self.outward = (self.w - jnp.where(self.depth > 0, step, -step), self.n)
        self.has_out = self.depth > 0
        self.inner = self.depth == self.half - 1


def hops(count, hop):
    if count == 1:
        hop(0)
    elif count > 1:
        loop(count, hop)


class PairFirst:
    @staticmethod
    def space(rows):
        return rows // 2 * 3

    def __init__(self, place, total, row, rows, buf, at, out, send, recv, store):
        self.place, self.total, self.buf = place, total, buf
        half = rows // 2
        self.half, self.at = half, at
        mine = pl.multiple_of(row + place.x * half, 16)
        other = pl.multiple_of(row + (1 - place.x) * half, 16)
        self.mine = mine
        keep, give = total.at[pl.ds(mine, half)], total.at[pl.ds(other, half)]
        out_keep, out_give = out.at[pl.ds(mine, half)], out.at[pl.ds(other, half)]
        slots = [buf.at[pl.ds(at + k * half, half)] for k in range(3)]
        self.pair_in = Copy(give, slots[0], send.at[0], recv.at[0], place.pair)
        self.line_in = Copy(keep, slots[1], send.at[1], recv.at[1], place.inward)
        self.middle = Copy(keep, slots[2], send.at[2], recv.at[2], place.inward)
        self.line_out = Copy(keep, out_keep, send.at[3], recv.at[3], place.outward)
        self.line_on = Copy(out_keep, out_keep, send.at[3], recv.at[3], place.outward)
        self.pair_out = Copy(keep, out_keep, send.at[4], recv.at[4], place.pair)
        self.pair_on = Copy(out_keep, out_keep, send.at[4], recv.at[4], place.pair)
        self.other = Copy(out_give, out_give, send.at[4], recv.at[4], place.pair)
        self.store = pltpu.make_async_copy(keep, out_keep, store)
        self.stages = [self.s0, self.s1, self.s2, self.s3, self.s4, self.s5]

    def s0(self):
        self.pair_in.start()

    def s1(self):
        place = self.place
        self.pair_in.wait()
        add_into(self.total, self.mine, self.buf, self.at, self.half)
        if place.half == 1:
            self.middle.start()
            return

        @pl.when(place.depth == 0)
        def _():
            self.line_in.start()

    def s2(self):
        place = self.place

        def hop(k):
            @pl.when(place.depth == k + 1)
            def _():
                self.line_in.wait_recv()
                add_into(self.total, self.mine, self.buf, self.at + self.half, self.half)

            @pl.when((place.depth == k + 1) & jnp.logical_not(place.inner))
            def _():
                self.line_in.start()

        hops(place.half - 1, hop)
        if place.half > 1:

            @pl.when(place.inner)
            def _():
                self.middle.start()

    def s3(self):
        place = self.place

        @pl.when(place.inner)
        def _():
            self.middle.wait()
            add_into(self.total, self.mine, self.buf, self.at + 2 * self.half, self.half)
            if place.half > 1:
                self.line_out.start()
            self.pair_out.start()
            self.store.start()

    def s4(self):
        place = self.place

        def hop(k):
            @pl.when(place.depth == place.half - 2 - k)
            def _():
                self.line_on.wait_recv()
                self.pair_on.start()

            @pl.when((place.depth == place.half - 2 - k) & place.has_out)
            def _():
                self.line_on.start()

        hops(place.half - 1, hop)

    def s5(self):
        place = self.place

        @pl.when(place.inner)
        def _():
            self.store.wait()

        if place.half > 1:

            @pl.when(jnp.logical_not(place.inner))
            def _():
                self.line_in.wait_send()

            @pl.when(place.has_out)
            def _():
                self.line_out.wait_send()

        self.pair_out.wait_send()
        self.other.wait_recv()


class LineFirst:
    @staticmethod
    def space(rows):
        return rows * 2

    def __init__(self, place, total, row, rows, buf, at, out, send, recv, store):
        self.place, self.total, self.buf = place, total, buf
        half = rows // 2
        self.row, self.rows, self.half, self.at = row, rows, half, at
        mine = pl.multiple_of(row + place.side * half, 16)
        other = pl.multiple_of(row + (1 - place.side) * half, 16)
        self.mine = mine
        whole = total.at[pl.ds(row, rows)]
        keep, give = total.at[pl.ds(mine, half)], total.at[pl.ds(other, half)]
        out_keep, out_give = out.at[pl.ds(mine, half)], out.at[pl.ds(other, half)]
        self.line_in = Copy(whole, buf.at[pl.ds(at, rows)], send.at[0], recv.at[0], place.inward)
        self.middle = Copy(give, buf.at[pl.ds(at + rows, half)], send.at[1], recv.at[1], place.inward)
        self.across = Copy(keep, buf.at[pl.ds(at + rows + half, half)], send.at[2], recv.at[2], place.pair)
        self.middle_out = Copy(keep, out_keep, send.at[3], recv.at[3], place.inward)
        self.middle_back = Copy(out_give, out_give, send.at[3], recv.at[3], place.inward)
        self.keep_out = Copy(keep, out_keep, send.at[4], recv.at[4], place.outward)
        self.keep_on = Copy(out_keep, out_keep, send.at[4], recv.at[4], place.outward)
        self.give_on = Copy(out_give, out_give, send.at[5], recv.at[5], place.outward)
        self.store = pltpu.make_async_copy(keep, out_keep, store)
        self.stages = [self.s0, self.s1, self.s2, self.s3, self.s4, self.s5]

    def s0(self):
        place = self.place
        if place.half == 1:
            self.middle.start()
            return

        @pl.when(place.depth == 0)
        def _():
            self.line_in.start()

    def s1(self):
        place = self.place

        def hop(k):
            @pl.when(place.depth == k + 1)
            def _():
                self.line_in.wait_recv()
                add_into(self.total, self.row, self.buf, self.at, self.rows)

            @pl.when((place.depth == k + 1) & jnp.logical_not(place.inner))
            def _():
                self.line_in.start()

        hops(place.half - 1, hop)
        if place.half > 1:

            @pl.when(place.inner)
            def _():
                self.middle.start()

    def s2(self):
        @pl.when(self.place.inner)
        def _():
            self.middle.wait()
            add_into(self.total, self.mine, self.buf, self.at + self.rows, self.half)
            self.across.start()

    def s3(self):
        place = self.place

        @pl.when(place.inner)
        def _():
            self.across.wait()
            add_into(self.total, self.mine, self.buf, self.at + self.rows + self.half, self.half)
            self.middle_out.start()
            if place.half > 1:
                self.keep_out.start()
            self.store.start()

    def s4(self):
        place = self.place

        @pl.when(place.inner)
        def _():
            self.middle_back.wait_recv()
            if place.half > 1:
                self.give_on.start()

    def s5(self):
        place = self.place

        def hop(k):
            @pl.when(place.depth == place.half - 2 - k)
            def _():
                self.keep_on.wait_recv()
                self.give_on.wait_recv()

            @pl.when((place.depth == place.half - 2 - k) & place.has_out)
            def _():
                self.keep_on.start()
                self.give_on.start()

        hops(place.half - 1, hop)

        @pl.when(place.inner)
        def _():
            self.middle_out.wait_send()
            self.store.wait()

        if place.half > 1:

            @pl.when(jnp.logical_not(place.inner))
            def _():
                self.line_in.wait_send()

            @pl.when(place.has_out)
            def _():
                self.keep_out.wait_send()
                self.give_on.wait_send()


KINDS = (PairFirst, LineFirst,)
PLAN = (1, 0, 0, 0, 0, 0, 1, 1, 0, 1, 0, 0, 0, 0, 0, 1, 0, 0, 0, 0, 1, 1, 0, 1)
TICKS = (
    (),
    (),
    (),
    (),
    (),
    (),
    (),
    (),
    (),
    ((1, 1), (0, 1), (2, 1), (3, 1)),
    ((6, 1),),
    ((4, 1),),
    (),
    (),
    ((5, 1), (0, 2)),
    ((7, 1), (6, 2), (8, 1), (1, 2)),
    ((10, 1), (2, 2), (11, 1), (3, 2)),
    ((7, 2),),
    ((0, 3),),
    ((4, 2),),
    ((1, 3),),
    ((6, 3),),
    (),
    (),
    ((2, 3), (12, 1)),
    ((9, 1), (3, 3), (7, 3), (1, 4), (5, 2), (0, 4), (13, 1)),
    ((8, 2), (4, 3)),
    ((14, 1),),
    ((2, 4), (10, 2)),
    ((6, 4),),
    (),
    ((3, 4), (11, 2), (9, 2), (16, 1), (7, 4), (17, 1)),
    ((0, 5), (15, 1)),
    ((5, 3), (1, 5), (18, 1), (4, 4), (12, 2), (8, 3), (19, 1), (6, 5), (13, 2), (10, 3), (2, 5), (7, 5), (11, 3), (3, 5), (5, 4), (20, 1), (15, 2), (8, 4), (14, 2), (12, 3), (4, 5), (22, 1), (10, 4), (13, 3), (9, 3), (11, 4), (21, 1), (20, 2), (24, 1), (12, 4), (14, 3), (5, 5), (13, 4), (23, 1), (9, 4), (8, 5), (16, 2), (21, 2), (10, 5), (14, 4), (17, 2), (23, 2), (11, 5), (9, 5), (18, 2), (16, 3), (15, 3), (19, 2), (17, 3), (12, 5), (22, 2), (16, 4), (18, 3), (13, 5), (24, 2), (15, 4), (20, 3), (17, 4), (19, 3), (14, 5), (18, 4), (22, 3), (21, 3), (15, 5), (24, 3), (23, 3), (20, 4), (16, 5), (19, 4), (21, 4), (17, 5), (22, 4), (23, 4), (18, 5), (19, 5), (24, 4), (22, 5), (24, 5), (20, 5), (21, 5), (23, 5), (24, 6), (24, 7)),
)


def encoder(
    wide_count,
    patches_in,
    kinds_in,
    cot_in,
    slots_in,
    proj_in,
    offs_in,
    plc_in,
    pos_in,
    scales,
    shifts,
    att_in,
    abias_in,
    comb_in,
    cbias,
    exp_in,
    ebias_in,
    red_in,
    rbias,
    sums_out,
    shared_out,
    encoded_out,
    patches_out,
    wa,
    wc,
    we,
    wr,
    abias,
    ebias,
    proj,
    pos,
    rows_all,
    kinds_all,
    flags,
    grad,
    stream,
    middle,
    first,
    second,
    qkv,
    probs,
    mixed,
    slope,
    hidden,
    out_round,
    pre,
    mid_round,
    grad_mixed,
    grad_qkv,
    key_acc,
    acc,
    give,
    take,
    take_top,
    cot,
    send_part,
    recv_part,
    total,
    ring,
    shared,
    shared_buf,
    top_own,
    top_other,
    patch_own,
    patch_other,
    small,
    bias_rows,
    load_sem,
    weight_send,
    weight_recv,
    rows_send,
    rows_recv,
    y_send,
    y_recv,
    part_send,
    part_recv,
    ring_send,
    ring_recv,
    shared_send,
    shared_recv,
    last_send,
    last_recv,
    store_sem,
    credit,
):
    place = Place(wide_count)
    y, c, w, n = place.y, place.c, place.w, place.n
    sibling, partner = place.sibling, place.partner
    local, width = cot_in.shape
    patch = proj_in.shape[0] // 2
    seq = pos_in.shape[0]
    layers = scales.shape[0]
    cols = att_in.shape[2]
    heads = cols // HD
    hid = exp_in.shape[2]
    scale = HD ** (-0.5)
    diagonal = y == c
    chunks = seq // local

    barrier = pltpu.get_barrier_semaphore()
    for step in (1, 2, 3):
        pl.semaphore_signal(barrier, 1, device_id=(w, (n + step) % 4), device_id_type=MESH)
    pl.semaphore_signal(barrier, 1, device_id=place.pair, device_id_type=MESH)
    pl.semaphore_signal(barrier, 1, device_id=place.inward, device_id_type=MESH)

    @pl.when(place.has_out)
    def _():
        pl.semaphore_signal(barrier, 1, device_id=place.outward, device_id_type=MESH)
        pl.semaphore_wait(barrier, 6)

    @pl.when(jnp.logical_not(place.has_out))
    def _():
        pl.semaphore_wait(barrier, 5)

    def span(index, size):
        return pl.ds(pl.multiple_of(index * size, size), size)

    far = (w, 2 - y)
    near = (w, 3 * y)
    here = span(c, local)
    row_copies = []
    for k, (src, dst, here) in enumerate(
        ((patches_in, rows_all, here), (cot_in, cot, here), (kinds_in, kinds_all, pl.ds(c, 1)))
    ):
        row_copies.append(
            (
                Copy(src, dst.at[here], rows_send.at[k, 0], rows_recv.at[k, c], far),
                Copy(src, dst.at[here], rows_send.at[k, 1], rows_recv.at[k, c], near),
                pltpu.make_async_copy(src, dst.at[here], rows_recv.at[k, c]),
            )
        )

    def send_rows(k):
        to_far, to_near, to_self = row_copies[k]
        to_far.start()

        @pl.when(diagonal)
        def _():
            to_self.start()

        @pl.when(jnp.logical_not(diagonal))
        def _():
            to_near.start()

    def wait_rows(k, dst, size):
        for h in range(2):
            spot = dst.at[pl.ds(h * size, size)]
            pltpu.make_async_copy(spot, spot, rows_recv.at[k, h]).wait()

    send_rows(0)
    send_rows(2)
    weights = []
    for layer in range(layers):
        for src, dst in ((att_in, wa), (comb_in, wc), (exp_in, we), (red_in, wr)):
            weights.append((src.at[layer], dst.at[layer]))
    own_loads = [pltpu.make_async_copy(src, dst.at[0], load_sem.at[k]) for k, (src, dst) in enumerate(weights)]
    sib_loads = [
        Copy(src, dst.at[1], weight_send.at[k], weight_recv.at[k], sibling) for k, (src, dst) in enumerate(weights)
    ]
    proj_load = pltpu.make_async_copy(proj_in, proj, load_sem.at[8])
    pos_load = pltpu.make_async_copy(pos_in, pos, load_sem.at[9])
    abias_copy = Copy(abias_in, abias.at[1], weight_send.at[8], weight_recv.at[8], sibling)
    ebias_copy = Copy(ebias_in, ebias.at[1], weight_send.at[9], weight_recv.at[9], sibling)
    abias_copy.start()
    ebias_copy.start()
    proj_load.start()
    pos_load.start()
    for k in range(8):
        own_loads[k].start()
        sib_loads[k].start()
        if k == 3:
            send_rows(1)
    abias[0] = abias_in[...]
    ebias[0] = ebias_in[...]
    small[...] = jnp.zeros_like(small)
    bias_rows[...] = jnp.zeros_like(bias_rows)

    def need(k):
        own_loads[k].wait()
        sib_loads[k].wait_recv()

    def note(row, values):
        small[row : row + 1, :] += column_sums(values)

    def param(ref, layer, row):
        return ref[layer, row : row + 1, :].astype(F32)

    def y_copy(index, slot, rows):
        return Copy(
            give.at[slot, rows], take.at[slot, rows], y_send.at[index[0], index[1]], y_recv.at[index[0], index[1]], partner
        )

    def offer(exchange, slot, ch, values):
        rows = span(ch, local)
        give[slot, rows, :] = values.astype(BF)
        y_copy((exchange, ch), slot, rows).start()

    def collect(exchange, slot, ch):
        rows = span(ch, local)
        y_copy((exchange, ch), slot, rows).wait()
        return give[slot, rows, :].astype(F32) + take[slot, rows, :].astype(F32)

    def head_mask(rows, h):
        lane = lax.broadcasted_iota(jnp.int32, (rows, cols), 1)
        return (lane >= h * HD) & (lane < (h + 1) * HD)

    place_col = lax.broadcasted_iota(jnp.int32, (seq, slots_in.shape[1]), 0)
    slot_row = slots_in[pl.ds(c, 1), :]
    masked = jnp.max(jnp.where(place_col == slot_row, 1.0, 0.0).astype(F32), axis=1, keepdims=True)
    wait_rows(0, rows_all, local)
    wait_rows(2, kinds_all, 1)
    for h in range(2):
        kinds = jnp.broadcast_to(jnp.where(kinds_all[h : h + 1, :] == 1, 1.0, 0.0), (128, 128)).astype(F32)
        flags[pl.ds(h * local, local), :] = kinds.T.astype(BF)
    proj_load.wait()
    pos_load.wait()
    wide_flags = jnp.concatenate([flags[...]] * (patch // 128), axis=1)
    patches = rows_all[...]
    kind_one = patches * wide_flags
    kind_zero = patches - kind_one
    is_one = flags[:, 0:1].astype(F32)
    lifted = nn(kind_zero, proj[0:patch, :]) + nn(kind_one, proj[patch : 2 * patch, :])
    offset = jnp.where(is_one > 0.5, offs_in[1:2, :].astype(F32), offs_in[0:1, :].astype(F32))
    stream[0] = jnp.where(masked > 0.5, plc_in[...].reshape(1, width).astype(F32), lifted + offset) + pos[...].astype(F32)

    def before_attention(layer):
        def norm(ch):
            rows = span(ch, local)
            hat, _ = hat_of(stream[layer, rows, :])
            first[layer, rows, :] = (hat * param(scales, layer, 0) + param(shifts, layer, 0)).astype(BF)

        loop(chunks, norm)

    def project(layer):
        need(4 * layer)
        if layer == 0:
            abias_copy.wait_recv()
            ebias_copy.wait_recv()

        def group(g):
            rows = first[layer]
            query = (nt(rows, wa[layer, g, 0]) + abias[g, layer, 0:1, :].astype(F32)) * scale
            qkv[layer, g, 0] = query.astype(BF)
            qkv[layer, g, 1] = nt(rows, wa[layer, g, 1]).astype(BF)
            qkv[layer, g, 2] = (nt(rows, wa[layer, g, 2]) + abias[g, layer, 1:2, :].astype(F32)).astype(BF)

        loop(2, group)

    def attend(layer, exchange, slot):
        need(4 * layer + 1)

        def chunk(ch):
            rows = span(ch, local)

            def group(g):
                total_mixed = jnp.zeros((local, cols), F32)
                query, key, value = qkv[layer, g, 0, rows, :], qkv[layer, g, 1], qkv[layer, g, 2]
                for h in range(heads):
                    scores = nt(jnp.where(head_mask(local, h), query, 0), key)
                    raised = jnp.exp(scores - jnp.max(scores, axis=-1, keepdims=True))
                    prob = (raised / jnp.sum(raised, axis=-1, keepdims=True)).astype(BF)
                    probs[layer, g * heads + h, rows, :] = prob
                    total_mixed += nn(prob, jnp.where(head_mask(seq, h), value, 0))
                mixed[layer, g, rows, :] = total_mixed.astype(BF)

            loop(2, group)
            offer(exchange, slot, ch, nn(mixed[layer, 0, rows, :], wc[layer, 0]) + nn(mixed[layer, 1, rows, :], wc[layer, 1]))

        loop(chunks, chunk)

    def to_middle(layer, exchange, slot, ch):
        rows = span(ch, local)
        values = stream[layer, rows, :] + collect(exchange, slot, ch) + cbias[layer : layer + 1, :].astype(F32)
        middle[layer, rows, :] = values
        hat, _ = hat_of(values)
        second[layer, rows, :] = (hat * param(scales, layer, 1) + param(shifts, layer, 1)).astype(BF)

    def activate(layer, g, rows):
        value = nn(second[layer, rows, :], we[layer, g]) + ebias[g, layer : layer + 1, :].astype(F32)
        cdf = 0.5 * (1.0 + lax.erf(value * (0.5**0.5)))
        hidden[layer, g, rows, :] = (value * cdf).astype(BF)
        density = jnp.exp(-0.5 * value * value) * 0.3989422804014327
        slope[layer, g, rows, :] = (cdf + value * density).astype(BF)

    def feed_back(layer, g, rows):
        grad_hidden = nt(out_round[rows, :], wr[layer, g])
        grad_pre = grad_hidden * slope[layer, g, rows, :].astype(F32)
        bias_rows[layer, g, 0:1, :] += column_sums(grad_pre)
        pre[g, rows, :] = grad_pre.astype(BF)

    def settle(row, layer, part, base, values, gain_row):
        hat, inverse = hat_of(base)
        note(2 * layer + part, values * hat)
        note(4 + 2 * layer + part, values)
        scaled = values * param(scales, layer, part)
        inner = scaled - jnp.mean(scaled, axis=-1, keepdims=True)
        return inverse * (inner - hat * jnp.mean(scaled * hat, axis=-1, keepdims=True))

    for layer in range(layers):
        before_attention(layer)
        project(layer)
        attend(layer, 2 * layer, 0)
        need(4 * layer + 2)
        need(4 * layer + 3)
        if layer + 1 < layers:

            def chunk(ch):
                rows = span(ch, local)
                to_middle(layer, 2 * layer, 0, ch)

                def group(g):
                    activate(layer, g, rows)
                    part = nn(hidden[layer, g, rows, :], wr[layer, g])

                    @pl.when(g == 0)
                    def _():
                        acc[...] = part

                    @pl.when(g == 1)
                    def _():
                        acc[...] += part

                loop(2, group)
                offer(2 * layer + 1, 1, ch, acc[...])

            loop(chunks, chunk)

            def after(ch):
                rows = span(ch, local)
                stream[layer + 1, rows, :] = (
                    middle[layer, rows, :] + collect(2 * layer + 1, 1, ch) + rbias[layer : layer + 1, :].astype(F32)
                )

            loop(chunks, after)

    pieces = []
    at = 0
    cut = hid // 4
    spots = [(hid + (k // 2) * cut if k % 2 == 0 else (k // 2) * cut, cut) for k in range(8)]
    spots += [(2 * hid + j * cols, cols) for j in range(3)] + [(2 * hid + 3 * cols, cols + 32)]
    per_layer = len(spots)
    for layer in reversed(range(layers)):
        for row, count in spots:
            k = len(pieces)
            kind = KINDS[PLAN[k]]
            piece = kind(
                place,
                total.at[layer],
                row,
                count,
                ring,
                at,
                sums_out.at[layer],
                ring_send.at[k],
                ring_recv.at[k],
                store_sem.at[k],
            )
            pieces.append((piece, layer, row, count))
            at += kind.space(count)

    def part_copy(k):
        _, _, row, count = pieces[k]
        return Copy(
            send_part.at[k % 4, pl.ds(0, count)],
            recv_part.at[pl.ds(row, count)],
            part_send.at[k],
            part_recv.at[k],
            sibling,
        )

    def begin(k, own, other):
        _, layer, row, count = pieces[k]
        if k >= 4:
            part_copy(k - 4).wait_send()
        if k == per_layer:
            pl.semaphore_wait(credit, 1)
        other(send_part.at[k % 4])
        part_copy(k).start()
        own(total.at[layer, pl.ds(row, count)])

    def join(k):
        piece, layer, row, count = pieces[k]
        part_copy(k).wait_recv()
        add_into(total.at[layer], row, recv_part, row, count)
        if k == per_layer - 1:
            pl.semaphore_signal(credit, 1, device_id=sibling, device_id_type=MESH)
        piece.stages[0]()

    ticks = iter(TICKS)

    def tick():
        for k, stage in next(ticks):
            (pieces[k][0] if k < len(pieces) else shared_piece[0]).stages[stage]()

    shared_piece = []

    def weight_grad(left, right):
        def into(ref):
            ref[pl.ds(0, left.shape[1]), :] = tn(left[...], right[...]).astype(BF)

        return into

    def run_pieces(base, works):
        for i, (own, other) in enumerate(works):
            begin(base + i, own, other)
            if i > 0:
                join(base + i - 1)
                tick()
        join(base + len(works) - 1)
        tick()

    def feed_grads(layer, base):
        works = []
        for k in range(8):
            lanes = pl.ds((k // 2) * cut, cut)
            if k % 2 == 0:
                works.append([weight_grad(hidden.at[layer, g, :, lanes], out_round) for g in range(2)])
            else:
                works.append([weight_grad(second.at[layer, :, lanes], pre.at[g]) for g in range(2)])
        run_pieces(base, works)

    def attention_grads(layer, base):
        def comb(g):
            grad_comb = weight_grad(mixed.at[layer, g], mid_round)

            def into(ref):
                grad_comb(ref)
                ref[pl.ds(cols, 32), :] = bias_rows[layer, g].astype(BF)

            return into

        works = [[weight_grad(grad_qkv.at[g, j], first.at[layer]) for g in range(2)] for j in range(3)]
        works.append([comb(g) for g in range(2)])
        run_pieces(base + 8, works)

    wait_rows(1, cot, local)
    last = layers - 1

    def start_back(ch):
        rows = span(ch, local)
        grad[rows, :] = cot[rows, :].astype(F32)

    loop(chunks, start_back)

    def top_send():
        return Copy(top_other, top_own, last_send.at[0], last_recv.at[0], sibling)

    top_copy = Copy(give.at[2], take_top, last_send.at[1], last_recv.at[1], partner)

    for layer in reversed(range(layers)):
        base = (last - layer) * per_layer
        exchange = 4 + 2 * (last - layer)

        def chunk(ch):
            rows = span(ch, local)
            note(10 + layer, grad[rows, :])
            out_round[rows, :] = grad[rows, :].astype(BF)
            if layer == last:
                to_middle(layer, 2 * layer, 0, ch)

            def group(g):
                if layer == last:
                    activate(layer, g, rows)
                feed_back(layer, g, rows)
                part = nt(pre[g, rows, :], we[layer, g])

                @pl.when(g == 0)
                def _():
                    acc[...] = part

                @pl.when(g == 1)
                def _():
                    acc[...] += part

            loop(2, group)
            offer(exchange, 1, ch, acc[...])

        loop(chunks, chunk)
        tick()

        if layer == last:

            def top(ch):
                rows = span(ch, local)
                give[2, rows, :] = (
                    nn(hidden[layer, 0, rows, :], wr[layer, 0]) + nn(hidden[layer, 1, rows, :], wr[layer, 1])
                ).astype(BF)

            loop(chunks, top)

            @pl.when(jnp.logical_not(diagonal))
            def _():
                top_copy.start()

        feed_grads(layer, base)

        def chunk(ch):
            rows = span(ch, local)
            grad_second = collect(exchange, 1, ch)
            grad_middle = grad[rows, :] + settle(rows, layer, 1, middle[layer, rows, :], grad_second, None)
            note(8 + layer, grad_middle)
            grad[rows, :] = grad_middle
            mid_round[rows, :] = grad_middle.astype(BF)

            def group(g):
                mixed_back = nt(mid_round[rows, :], wc[layer, g]).astype(BF)
                query, key, value = qkv[layer, g, 0, rows, :], qkv[layer, g, 1], qkv[layer, g, 2]
                query_acc = jnp.zeros((local, cols), F32)
                key_sum = jnp.zeros((seq, cols), F32)
                value_sum = jnp.zeros((seq, cols), F32)
                for h in range(heads):
                    prob = probs[layer, g * heads + h, rows, :]
                    back = jnp.where(head_mask(local, h), mixed_back, 0)
                    grad_probs = nt(back, value)
                    value_sum += tn(prob, back)
                    weight = prob.astype(F32)
                    center = jnp.sum(weight * grad_probs, axis=-1, keepdims=True)
                    grad_scores = (weight * (grad_probs - center)).astype(BF)
                    query_acc += nn(grad_scores, jnp.where(head_mask(seq, h), key, 0))
                    key_sum += tn(grad_scores, jnp.where(head_mask(local, h), query, 0))
                grad_query = (query_acc.astype(BF).astype(F32) * scale).astype(BF)
                grad_qkv[g, 0, rows, :] = grad_query
                bias_rows[layer, g, 1:2, 0:cols] += column_sums(grad_query.astype(F32))

                @pl.when(ch == 0)
                def _():
                    key_acc[g, 0] = key_sum
                    key_acc[g, 1] = value_sum

                @pl.when(ch > 0)
                def _():
                    key_acc[g, 0] += key_sum
                    key_acc[g, 1] += value_sum

            loop(2, group)

        loop(chunks, chunk)
        tick()

        def close(g):
            grad_qkv[g, 1] = key_acc[g, 0].astype(BF)
            grad_value = key_acc[g, 1].astype(BF)
            grad_qkv[g, 2] = grad_value
            bias_rows[layer, g, 2:3, 0:cols] += column_sums(grad_value.astype(F32))

        loop(2, close)

        def chunk(ch):
            rows = span(ch, local)

            def group(g):
                part = (
                    nn(grad_qkv[g, 0, rows, :], wa[layer, g, 0])
                    + nn(grad_qkv[g, 1, rows, :], wa[layer, g, 1])
                    + nn(grad_qkv[g, 2, rows, :], wa[layer, g, 2])
                )

                @pl.when(g == 0)
                def _():
                    acc[...] = part

                @pl.when(g == 1)
                def _():
                    acc[...] += part

            loop(2, group)
            offer(exchange + 1, 0, ch, acc[...])

        loop(chunks, chunk)
        tick()
        attention_grads(layer, base)

        if layer == last:

            @pl.when(jnp.logical_not(diagonal))
            def _():
                top_copy.wait_send()

            @pl.when(diagonal)
            def _():
                top_copy.wait_recv()

                def finish_top(dst, half):
                    rows = span(half, local)
                    dst[...] = (
                        middle[layer, rows, :]
                        + (give[2, rows, :].astype(F32) + take_top[rows, :].astype(F32))
                        + rbias[layer : layer + 1, :].astype(F32)
                    )

                finish_top(top_other, 1 - c)
                top_send().start()
                finish_top(top_own, c)

        def chunk(ch):
            rows = span(ch, local)
            grad_first = collect(exchange + 1, 0, ch)
            grad[rows, :] += settle(rows, layer, 0, stream[layer, rows, :], grad_first, None)

        loop(chunks, chunk)
        tick()

    lifted_grad = jnp.where(masked > 0.5, 0.0, grad[...])
    note(14, grad[...] - lifted_grad)
    one_grad = jnp.where(is_one > 0.5, lifted_grad, 0.0)
    note(12, lifted_grad - one_grad)
    note(13, one_grad)
    lifted_round = lifted_grad.astype(BF)
    shared_rows = shared.shape[0]
    half_rows = shared_rows // 2
    flag_side = jnp.where(y == 1, wide_flags.astype(F32), 1.0 - wide_flags.astype(F32)).astype(BF)
    shared[0:patch, :] = tn(rows_all[...] * flag_side, lifted_round).astype(BF)
    shared[patch : patch + local, :] = grad[span(y, local), :].astype(BF)
    shared[patch + local : shared_rows, :] = small[...].astype(BF)
    keep_row, give_row = span(c, half_rows), span(1 - c, half_rows)
    shared_part = Copy(
        shared.at[give_row], shared_buf.at[pl.ds(0, half_rows)], last_send.at[2], last_recv.at[2], sibling
    )
    shared_part.start()

    patch_copy = Copy(patch_other, patch_own, last_send.at[3], last_recv.at[3], sibling)

    @pl.when(diagonal)
    def _():
        def half_back(dst, half):
            rows = span(half, local)
            flag = flags[rows, :].astype(F32)[:, 0:1]
            masks = jnp.max(
                jnp.where(
                    lax.broadcasted_iota(jnp.int32, (local, slots_in.shape[1]), 0) + half * local == slot_row, 1.0, 0.0
                ).astype(F32),
                axis=1,
                keepdims=True,
            )
            values = jnp.where(masks > 0.5, 0.0, grad[rows, :]).astype(BF)
            dst[...] = jnp.where(flag > 0.5, nt(values, proj[patch : 2 * patch, :]), nt(values, proj[0:patch, :]))

        half_back(patch_other, 1 - c)
        patch_copy.start()
        half_back(patch_own, c)

    shared_part.wait()
    add_into(shared, pl.multiple_of(c * half_rows, 16), shared_buf, 0, half_rows)
    sum_shared = PairFirst(
        place,
        shared,
        pl.multiple_of(c * half_rows, 16),
        half_rows,
        shared_buf,
        half_rows,
        shared_out.at[y],
        shared_send,
        shared_recv,
        store_sem.at[len(pieces)],
    )
    across = Copy(shared_out.at[y, keep_row], shared_out.at[y, keep_row], last_send.at[4], last_recv.at[4], partner)
    across_back = Copy(
        shared_out.at[1 - y, keep_row], shared_out.at[1 - y, keep_row], last_send.at[4], last_recv.at[4], partner
    )
    ends = []
    for k in range(2):
        ends.append(
            (
                Copy(
                    shared_out.at[k, keep_row], shared_out.at[k, keep_row], last_send.at[5 + k], last_recv.at[5 + k], sibling
                ),
                Copy(
                    shared_out.at[k, give_row], shared_out.at[k, give_row], last_send.at[5 + k], last_recv.at[5 + k], sibling
                ),
            )
        )

    def to_partner():
        sum_shared.s5()
        across.start()

    def to_sibling():
        across.wait_send()
        across_back.wait_recv()
        for out, _ in ends:
            out.start()

    def close_shared():
        for out, back in ends:
            out.wait_send()
            back.wait_recv()

    sum_shared.stages = sum_shared.stages[:5] + [to_partner, to_sibling, close_shared]
    shared_piece.append(sum_shared)
    sum_shared.s0()
    tick()
    tick()
    count = len(pieces)

    @pl.when(diagonal)
    def _():
        top_send().wait_send()
        patch_copy.wait_send()

    @pl.when(jnp.logical_not(diagonal))
    def _():
        top_send().wait_recv()
        patch_copy.wait_recv()

    finals = (
        pltpu.make_async_copy(top_own, encoded_out, store_sem.at[count + 1]),
        pltpu.make_async_copy(patch_own, patches_out, store_sem.at[count + 2]),
    )
    for copy in finals:
        copy.start()
    for copy in finals:
        copy.wait()

    for to_far, to_near, _ in row_copies:
        to_far.wait_send()

        @pl.when(jnp.logical_not(diagonal))
        def _():
            to_near.wait_send()

    for copy in sib_loads + [abias_copy, ebias_copy]:
        copy.wait_send()
    for k in range(count - 4, count):
        part_copy(k).wait_send()


def per_device(
    wide_count,
    patches,
    token_kind,
    mask_slots,
    projector,
    offsets,
    placeholder,
    positions,
    scales,
    shifts,
    attention,
    attn_bias,
    combiner,
    comb_bias,
    expander,
    expand_bias,
    reducer,
    reduce_bias,
    cotangent,
):
    local, patch = patches.shape
    seq, width = positions.shape
    layers = scales.shape[0]
    cols = attention.shape[3]
    heads = cols // HD
    hid = expander.shape[2]
    per_layer = 2 * hid + 4 * cols + 32
    shared_rows = patch + local + 64
    pieces = 12 * layers
    counts = ([hid // 4] * 8 + [cols] * 3 + [cols + 32]) * layers
    ring_rows = sum(KINDS[kind].space(count) for kind, count in zip(PLAN, counts))
    vmem = pl.BlockSpec(memory_space=pltpu.VMEM)
    anyw = pl.BlockSpec(memory_space=pl.ANY)
    dma = pltpu.SemaphoreType.DMA
    scratch = [
        pltpu.VMEM((layers, 2, 3, cols, width), BF),
        pltpu.VMEM((layers, 2, cols, width), BF),
        pltpu.VMEM((layers, 2, width, hid), BF),
        pltpu.VMEM((layers, 2, hid, width), BF),
        pltpu.VMEM((2, layers, 2, cols), BF),
        pltpu.VMEM((2, layers, hid), BF),
        pltpu.VMEM((2 * patch, width), BF),
        pltpu.VMEM((seq, width), BF),
        pltpu.VMEM((seq, patch), BF),
        pltpu.VMEM((2, local), jnp.int32),
        pltpu.VMEM((seq, 128), BF),
        pltpu.VMEM((seq, width), F32),
        pltpu.VMEM((layers, seq, width), F32),
        pltpu.VMEM((layers, seq, width), F32),
        pltpu.VMEM((layers, seq, width), BF),
        pltpu.VMEM((layers, seq, width), BF),
        pltpu.VMEM((layers, 2, 3, seq, cols), BF),
        pltpu.VMEM((layers, 2 * heads, seq, seq), BF),
        pltpu.VMEM((layers, 2, seq, cols), BF),
        pltpu.VMEM((layers, 2, seq, hid), BF),
        pltpu.VMEM((layers, 2, seq, hid), BF),
        pltpu.VMEM((seq, width), BF),
        pltpu.VMEM((2, seq, hid), BF),
        pltpu.VMEM((seq, width), BF),
        pltpu.VMEM((8, 128), BF),
        pltpu.VMEM((2, 3, seq, cols), BF),
        pltpu.VMEM((2, 2, seq, cols), F32),
        pltpu.VMEM((local, width), F32),
        pltpu.VMEM((3, seq, width), BF),
        pltpu.VMEM((2, seq, width), BF),
        pltpu.VMEM((seq, width), BF),
        pltpu.VMEM((seq, width), BF),
        pltpu.VMEM((4, cols + 32, width), BF),
        pltpu.VMEM((per_layer, width), BF),
        pltpu.VMEM((layers, per_layer, width), BF),
        pltpu.VMEM((ring_rows, width), BF),
        pltpu.VMEM((shared_rows, width), BF),
        pltpu.VMEM((shared_rows // 2 + 3 * (shared_rows // 4), width), BF),
        pltpu.VMEM((local, width), F32),
        pltpu.VMEM((local, width), F32),
        pltpu.VMEM((local, patch), F32),
        pltpu.VMEM((local, patch), F32),
        pltpu.VMEM((64, width), F32),
        pltpu.VMEM((layers, 2, 32, width), F32),
        dma((10,)),
        dma((10,)),
        dma((10,)),
        dma((3, 2)),
        dma((3, 2)),
        dma((8, 2)),
        dma((8, 2)),
        dma((pieces,)),
        dma((pieces,)),
        dma((pieces, 6)),
        dma((pieces, 6)),
        dma((5,)),
        dma((5,)),
        dma((7,)),
        dma((7,)),
        dma((pieces + 3,)),
        pltpu.SemaphoreType.REGULAR,
    ]
    sums, shared, encoded, grad_patches = pl.pallas_call(
        functools.partial(encoder, wide_count),
        out_shape=(
            jax.ShapeDtypeStruct((layers, per_layer, width), BF),
            jax.ShapeDtypeStruct((2, shared_rows, width), BF),
            jax.ShapeDtypeStruct((local, width), F32),
            jax.ShapeDtypeStruct((local, patch), F32),
        ),
        in_specs=[anyw, vmem, anyw, vmem, anyw, vmem, vmem, anyw, vmem, vmem, anyw, vmem, anyw, vmem, anyw, vmem, anyw, vmem],
        out_specs=(anyw, anyw, anyw, anyw),
        scratch_shapes=scratch,
        compiler_params=pltpu.CompilerParams(
            collective_id=0, has_side_effects=True, vmem_limit_bytes=63 * 1024 * 1024 + 512 * 1024
        ),
        name="encoder",
    )(
        patches,
        token_kind.reshape(1, local),
        cotangent,
        mask_slots,
        projector.reshape(2 * patch, width),
        offsets,
        placeholder,
        positions,
        scales,
        shifts,
        attention.transpose(0, 1, 3, 2),
        attn_bias,
        combiner,
        comb_bias,
        expander,
        expand_bias,
        reducer,
        reduce_bias,
    )
    f32 = functools.partial(jax.ShapeDtypeStruct, dtype=F32)
    finished = pl.pallas_call(
        widen,
        out_shape=(
            f32((local, width)),
            f32((local, patch)),
            f32((2, patch, width)),
            f32((2, width)),
            f32((width,)),
            f32((seq, width)),
            f32((layers, 2, width)),
            f32((layers, 2, width)),
            f32((layers, 3, cols, width)),
            f32((layers, 2, cols)),
            f32((layers, cols, width)),
            f32((layers, width)),
            f32((layers, width, hid)),
            f32((layers, hid)),
            f32((layers, hid, width)),
            f32((layers, width)),
        ),
        in_specs=[anyw] * 4,
        out_specs=[anyw, anyw, anyw, vmem, vmem, anyw, vmem, vmem, anyw, vmem, anyw, vmem, anyw, vmem, anyw, vmem],
        scratch_shapes=[
            pltpu.VMEM((layers, per_layer, width), BF),
            pltpu.VMEM((layers, per_layer - 32, width), F32),
            pltpu.VMEM((2, shared_rows, width), BF),
            pltpu.VMEM((2, patch + local, width), F32),
            pltpu.VMEM((local, width), F32),
            pltpu.VMEM((local, patch), F32),
            dma((layers, 4)),
            dma((layers, 6)),
            dma((2,)),
            dma((2, 2)),
            dma((2, 2)),
        ],
        compiler_params=pltpu.CompilerParams(vmem_limit_bytes=62 * 1024 * 1024),
        name="widen",
    )(sums, shared, encoded, grad_patches)
    return tuple(item.transpose(0, 1, 3, 2) if k == 8 else item for k, item in enumerate(finished))


def widen(
    sums,
    shared,
    encoded,
    grad_patches,
    encoded_out,
    patches_out,
    projector,
    offsets,
    placeholder,
    positions,
    scales,
    shifts,
    attention,
    attn_bias,
    combiner,
    comb_bias,
    expander,
    expand_bias,
    reducer,
    reduce_bias,
    sums_in,
    sums_wide,
    shared_in,
    shared_wide,
    encoded_held,
    patches_held,
    load_sem,
    store_sem,
    shared_sem,
    shared_store,
    through_sem,
):
    layers, width, hid = expander.shape
    cols = combiner.shape[1]
    patch = projector.shape[1]
    local = encoded.shape[0]
    through = [
        (pltpu.make_async_copy(src, held, through_sem.at[k, 0]), pltpu.make_async_copy(held, dst, through_sem.at[k, 1]))
        for k, (src, held, dst) in enumerate(
            ((encoded, encoded_held, encoded_out), (grad_patches, patches_held, patches_out))
        )
    ]
    tail = sums.shape[1] - 3 * cols - 2 * hid
    cuts = ((0, hid), (hid, hid), (2 * hid, 3 * cols), (2 * hid + 3 * cols, tail))
    loads = []
    for layer in range(layers):
        for k, (row, count) in enumerate(cuts):
            spot = (layer, pl.ds(row, count))
            loads.append(pltpu.make_async_copy(sums.at[spot], sums_in.at[spot], load_sem.at[layer, k]))
    shared_loads = [pltpu.make_async_copy(shared.at[k], shared_in.at[k], shared_sem.at[k]) for k in range(2)]
    for copy in loads + shared_loads + [load for load, _ in through]:
        copy.start()
    stores = []

    def convert(src, dst, row, count):
        def step(t):
            rows = pl.ds(pl.multiple_of(row + t * 64, 64), 64)
            dst[rows, :] = src[rows, :].astype(F32)

        loop(count // 64, step)

    for layer in range(layers):
        for k, (row, count) in enumerate(cuts):
            loads[layer * len(cuts) + k].wait()
            wide = min(count, sums_wide.shape[1] - row)
            convert(sums_in.at[layer], sums_wide.at[layer], row, wide)
            if k == 2:
                targets = [(attention.at[layer, j], row + j * cols, cols, 2 + j) for j in range(3)]
            else:
                targets = [((expander, reducer, None, combiner)[k].at[layer], row, wide, (0, 1, None, 5)[k])]
            for target, start, size, sem in targets:
                copy = pltpu.make_async_copy(sums_wide.at[layer, pl.ds(start, size)], target, store_sem.at[layer, sem])
                copy.start()
                stores.append(copy)
        bias = sums_in[layer, pl.ds(2 * hid + 4 * cols, 16), :].astype(F32)
        expand_bias[layer : layer + 1, :] = bias[0:1, :]
        attn_bias[layer, 0:1, :] = bias[1:2, :cols]
        attn_bias[layer, 1:2, :] = bias[2:3, :cols]
    for k in range(2):
        shared_loads[k].wait()
        convert(shared_in.at[k], shared_wide.at[k], 0, patch + local)
        for target, start, size, sem in (
            (projector.at[k], 0, patch, 0),
            (positions.at[pl.ds(k * local, local)], patch, local, 1),
        ):
            copy = pltpu.make_async_copy(shared_wide.at[k, pl.ds(start, size)], target, shared_store.at[k, sem])
            copy.start()
            stores.append(copy)
    for load, store in through:
        load.wait()
        store.start()
    small = shared_in[0, pl.ds(patch + local, 16), :].astype(F32)
    for layer in range(layers):
        scales[layer] = small[2 * layer : 2 * layer + 2, :]
        shifts[layer] = small[4 + 2 * layer : 6 + 2 * layer, :]
    comb_bias[...] = small[8:10, :]
    reduce_bias[...] = small[10:12, :]
    offsets[...] = small[12:14, :]
    placeholder[...] = small[14:15, :].reshape(width)
    for copy in stores + [store for _, store in through]:
        copy.wait()


def solution(mesh):
    rows = ("wide", "narrow")
    return jax.shard_map(
        functools.partial(per_device, mesh.shape["wide"]),
        mesh=mesh,
        in_specs=(
            P(rows, None),
            P(rows),
            P("wide", None),
            P(),
            P(),
            P(),
            P(),
            P(),
            P(),
            P(None, None, None, "narrow"),
            P(None, None, "narrow"),
            P(None, "narrow", None),
            P(),
            P(None, None, "narrow"),
            P(None, "narrow"),
            P(None, "narrow", None),
            P(),
            P(rows, None),
        ),
        out_specs=(
            P(rows, None),
            P(rows, None),
            P(),
            P(),
            P(),
            P(),
            P(),
            P(),
            P(None, None, None, "narrow"),
            P(None, None, "narrow"),
            P(None, "narrow", None),
            P(),
            P(None, None, "narrow"),
            P(None, "narrow"),
            P(None, "narrow", None),
            P(),
        ),
        check_vma=False,
    )
```

```python
import functools

import jax
import jax.numpy as jnp
from jax import lax
from jax.experimental import pallas as pl
from jax.experimental.pallas import tpu as pltpu
from jax.sharding import PartitionSpec as P

HD = 64
EPS = 1e-06
BF = jnp.bfloat16
F32 = jnp.float32
MESH = pl.DeviceIdType.MESH


def nn(left, right):
    return jnp.dot(left, right, preferred_element_type=F32)


def nt(left, right):
    return lax.dot_general(left, right, (((1,), (1,)), ((), ())), preferred_element_type=F32)


def tn(left, right):
    return lax.dot_general(left, right, (((0,), (0,)), ((), ())), preferred_element_type=F32)


def loop(count, body):
    def step(index, carry):
        body(index)
        return carry

    lax.fori_loop(0, count, step, 0)


def hat_of(values):
    center = values - jnp.mean(values, axis=-1, keepdims=True)
    variance = jnp.mean(center * center, axis=-1, keepdims=True)
    scale = lax.rsqrt(variance + EPS)
    return center * scale, scale


def column_sums(values):
    return jnp.sum(values, axis=0, keepdims=True)


class Copy:
    def __init__(self, src, dst, send, recv, target):
        self.args = dict(src_ref=src, dst_ref=dst, send_sem=send, recv_sem=recv, device_id=target, device_id_type=MESH)

    def start(self):
        pltpu.make_async_remote_copy(**self.args).start()

    def wait(self):
        pltpu.make_async_remote_copy(**self.args).wait()

    def wait_send(self):
        pltpu.make_async_remote_copy(**self.args).wait_send()

    def wait_recv(self):
        pltpu.make_async_remote_copy(**self.args).wait_recv()


def add_into(dst, dst_row, src, src_row, rows):
    block = next(b for b in (96, 64, 112, 48, 32, 16) if rows % b == 0)

    def step(index):
        into = pl.ds(pl.multiple_of(dst_row + index * block, 16), block)
        give = pl.ds(pl.multiple_of(src_row + index * block, 16), block)
        dst[into, :] = (dst[into, :].astype(F32) + src[give, :].astype(F32)).astype(BF)

    loop(rows // block, step)


class Place:
    def __init__(self, wide_count):
        self.w = lax.axis_index("wide")
        self.n = lax.axis_index("narrow")
        self.y = self.n // 2
        self.c = self.n % 2
        self.x = self.w % 2
        self.z = self.w // 2
        line = wide_count // 2
        self.half = line // 2
        self.low = self.z < self.half
        self.side = jnp.where(self.low, 0, 1)
        self.depth = jnp.where(self.low, self.z, line - 1 - self.z)
        step = jnp.where(self.low, 2, -2)
        self.sibling = (self.w, self.n + 1 - 2 * self.c)
        self.partner = (self.w, self.n + 2 - 4 * self.y)
        self.pair = (self.w + 1 - 2 * self.x, self.n)
        self.inward = (self.w + step, self.n)
        self.outward = (self.w - jnp.where(self.depth > 0, step, -step), self.n)
        self.has_out = self.depth > 0
        self.inner = self.depth == self.half - 1


def hops(count, hop):
    if count == 1:
        hop(0)
    elif count > 1:
        loop(count, hop)


class PairFirst:
    @staticmethod
    def space(rows):
        return rows // 2 * 3

    def __init__(self, place, total, row, rows, buf, at, out, send, recv, store):
        self.place, self.total, self.buf = place, total, buf
        half = rows // 2
        self.half, self.at = half, at
        mine = pl.multiple_of(row + place.x * half, 16)
        other = pl.multiple_of(row + (1 - place.x) * half, 16)
        self.mine = mine
        keep, give = total.at[pl.ds(mine, half)], total.at[pl.ds(other, half)]
        out_keep, out_give = out.at[pl.ds(mine, half)], out.at[pl.ds(other, half)]
        slots = [buf.at[pl.ds(at + k * half, half)] for k in range(3)]
        self.pair_in = Copy(give, slots[0], send.at[0], recv.at[0], place.pair)
        self.line_in = Copy(keep, slots[1], send.at[1], recv.at[1], place.inward)
        self.middle = Copy(keep, slots[2], send.at[2], recv.at[2], place.inward)
        self.line_out = Copy(keep, out_keep, send.at[3], recv.at[3], place.outward)
        self.line_on = Copy(out_keep, out_keep, send.at[3], recv.at[3], place.outward)
        self.pair_out = Copy(keep, out_keep, send.at[4], recv.at[4], place.pair)
        self.pair_on = Copy(out_keep, out_keep, send.at[4], recv.at[4], place.pair)
        self.other = Copy(out_give, out_give, send.at[4], recv.at[4], place.pair)
        self.store = pltpu.make_async_copy(keep, out_keep, store)
        self.stages = [self.s0, self.s1, self.s2, self.s3, self.s4, self.s5]

    def s0(self):
        self.pair_in.start()

    def s1(self):
        place = self.place
        self.pair_in.wait()
        add_into(self.total, self.mine, self.buf, self.at, self.half)
        if place.half == 1:
            self.middle.start()
            return

        @pl.when(place.depth == 0)
        def _():
            self.line_in.start()

    def s2(self):
        place = self.place

        def hop(k):
            @pl.when(place.depth == k + 1)
            def _():
                self.line_in.wait_recv()
                add_into(self.total, self.mine, self.buf, self.at + self.half, self.half)

            @pl.when((place.depth == k + 1) & jnp.logical_not(place.inner))
            def _():
                self.line_in.start()

        hops(place.half - 1, hop)
        if place.half > 1:

            @pl.when(place.inner)
            def _():
                self.middle.start()

    def s3(self):
        place = self.place

        @pl.when(place.inner)
        def _():
            self.middle.wait()
            add_into(self.total, self.mine, self.buf, self.at + 2 * self.half, self.half)
            if place.half > 1:
                self.line_out.start()
            self.pair_out.start()
            self.store.start()

    def s4(self):
        place = self.place

        def hop(k):
            @pl.when(place.depth == place.half - 2 - k)
            def _():
                self.line_on.wait_recv()
                self.pair_on.start()

            @pl.when((place.depth == place.half - 2 - k) & place.has_out)
            def _():
                self.line_on.start()

        hops(place.half - 1, hop)

    def s5(self):
        place = self.place

        @pl.when(place.inner)
        def _():
            self.store.wait()

        if place.half > 1:

            @pl.when(jnp.logical_not(place.inner))
            def _():
                self.line_in.wait_send()

            @pl.when(place.has_out)
            def _():
                self.line_out.wait_send()

        self.pair_out.wait_send()
        self.other.wait_recv()


class LineScatter:
    @staticmethod
    def space(rows):
        return rows // 4 * 7

    def __init__(self, place, total, row, rows, buf, at, out, send, recv, store):
        quarter = rows // 4
        self.place, self.total, self.row, self.quarter = place, total, row, quarter
        self.buf, self.at = buf, at
        mine = pl.multiple_of(row + place.z * quarter, 16)
        self.mine = mine
        low, high = (place.w - 2, place.n), (place.w + 2, place.n)

        def own(start, stop):
            return total.at[pl.ds(row + start * quarter, (stop - start) * quarter)]

        def slot(start, count):
            return buf.at[pl.ds(at + start * quarter, count * quarter)]

        self.up = [Copy(own(z + 1, 4), slot(z, 3 - z), send.at[0], recv.at[0], high) for z in range(3)]
        self.down = [Copy(own(0, z), slot(3, z), send.at[1], recv.at[1], low) for z in range(4)]
        keep, land = total.at[pl.ds(mine, quarter)], out.at[pl.ds(mine, quarter)]
        self.across = Copy(keep, slot(6, 1), send.at[2], recv.at[2], place.pair)
        self.store = pltpu.make_async_copy(keep, land, store)

        def spread(src, dst, k, target, way):
            return Copy(src, dst, send.at[3 + 4 * way + k], recv.at[3 + k], target)

        spots = [out.at[pl.ds(row + k * quarter, quarter)] for k in range(4)]
        self.first_up = [spread(own(k, k + 1), spots[k], k, high, 0) for k in range(4)]
        self.first_down = [spread(own(k, k + 1), spots[k], k, low, 1) for k in range(4)]
        self.on_up = [spread(spots[k], spots[k], k, high, 0) for k in range(4)]
        self.on_down = [spread(spots[k], spots[k], k, low, 1) for k in range(4)]
        self.stages = [self.s0, self.s1, self.s2, self.s3, self.s4, self.s5, self.s6, self.s7]

    def at_z(self, *works):
        for z, work in works:
            pl.when(self.place.z == z)(work)

    def take(self, copy, first, slot, count):
        copy.wait_recv()
        add_into(self.total, self.row + first * self.quarter, self.buf, self.at + slot * self.quarter, count * self.quarter)

    def s0(self):
        self.at_z((0, self.up[0].start), (3, self.down[3].start))

    def s1(self):
        def one():
            self.take(self.up[0], 1, 0, 3)
            self.up[1].start()

        def two():
            self.take(self.down[3], 0, 3, 3)
            self.down[2].start()

        self.at_z((1, one), (2, two))

    def s2(self):
        def one():
            self.take(self.down[2], 0, 3, 2)
            self.down[1].start()

        def two():
            self.take(self.up[1], 2, 1, 2)
            self.up[2].start()

        self.at_z((1, one), (2, two))

    def s3(self):
        self.at_z((0, lambda: self.take(self.down[1], 0, 3, 1)), (3, lambda: self.take(self.up[2], 3, 2, 1)))
        self.across.start()

    def s4(self):
        self.across.wait()
        add_into(self.total, self.mine, self.buf, self.at + 6 * self.quarter, self.quarter)
        self.store.start()

        def both(z):
            def work():
                self.first_up[z].start()
                self.first_down[z].start()

            return work

        self.at_z((0, self.first_up[0].start), (1, both(1)), (2, both(2)), (3, self.first_down[3].start))

    def s5(self):
        def one():
            self.on_up[0].wait_recv()
            self.on_up[0].start()
            self.on_down[2].wait_recv()
            self.on_down[2].start()

        def two():
            self.on_down[3].wait_recv()
            self.on_down[3].start()
            self.on_up[1].wait_recv()
            self.on_up[1].start()

        self.at_z((1, one), (2, two))

    def s6(self):
        def one():
            self.on_down[3].wait_recv()
            self.on_down[3].start()

        def two():
            self.on_up[0].wait_recv()
            self.on_up[0].start()

        self.at_z((1, one), (2, two))

    def s7(self):
        self.store.wait()

        def zero():
            for k in (1, 2, 3):
                self.on_down[k].wait_recv()
            for copy in (self.up[0], self.first_up[0]):
                copy.wait_send()

        def one():
            for copy in (self.up[1], self.down[1], self.first_up[1], self.on_up[0]):
                copy.wait_send()
            for copy in (self.first_down[1], self.on_down[2], self.on_down[3]):
                copy.wait_send()

        def two():
            for copy in (self.up[2], self.down[2], self.first_up[2], self.on_up[1], self.on_up[0]):
                copy.wait_send()
            for copy in (self.first_down[2], self.on_down[3]):
                copy.wait_send()

        def three():
            for k in (0, 1, 2):
                self.on_up[k].wait_recv()
            for copy in (self.down[3], self.first_down[3]):
                copy.wait_send()

        self.at_z((0, zero), (1, one), (2, two), (3, three))


KINDS = (PairFirst, LineScatter,)
PLAN = (1, 0, 0, 1, 0, 0, 1, 0, 0, 0, 0, 0, 1, 0, 0, 0, 0, 0, 1, 1, 0, 1, 1, 0)
TICKS = (
    (),
    (),
    (),
    (),
    (),
    (),
    (),
    (),
    (),
    ((1, 1), (0, 1), (2, 1), (3, 1), (4, 1)),
    (),
    ((5, 1), (6, 1)),
    (),
    (),
    ((7, 1), (0, 2), (1, 2)),
    ((3, 2), (2, 2), (8, 1), (0, 3), (6, 2), (4, 2), (9, 1)),
    ((1, 3), (5, 2), (10, 1), (3, 3)),
    ((6, 3), (2, 3), (7, 2)),
    ((11, 1),),
    (),
    ((0, 4), (4, 3), (8, 2)),
    (),
    ((1, 4),),
    (),
    ((5, 3), (9, 2), (3, 4)),
    ((2, 4), (6, 4), (7, 3), (10, 2), (4, 4)),
    ((8, 3), (12, 1), (13, 1), (5, 4)),
    (),
    ((9, 3), (11, 2), (14, 1)),
    (),
    ((0, 5),),
    ((15, 1), (7, 4), (10, 3), (18, 1), (1, 5), (8, 4)),
    ((12, 2), (2, 5), (16, 1)),
    ((9, 4), (19, 1), (11, 3), (3, 5), (4, 5), (17, 1), (0, 6), (6, 5), (10, 4), (5, 5), (12, 3), (18, 2), (13, 2), (19, 2), (11, 4), (3, 6), (21, 1), (6, 6), (0, 7), (14, 2), (20, 1), (7, 5), (13, 3), (18, 3), (19, 3), (8, 5), (21, 2), (22, 1), (3, 7), (6, 7), (23, 1), (14, 3), (15, 2), (13, 4), (9, 5), (22, 2), (16, 2), (21, 3), (24, 1), (10, 5), (15, 3), (17, 2), (14, 4), (22, 3), (16, 3), (20, 2), (11, 5), (12, 4), (15, 4), (17, 3), (23, 2), (16, 4), (20, 3), (18, 4), (24, 2), (13, 5), (19, 4), (12, 5), (17, 4), (23, 3), (14, 5), (21, 4), (18, 5), (20, 4), (24, 3), (15, 5), (22, 4), (19, 5), (12, 6), (16, 5), (21, 5), (23, 4), (18, 6), (17, 5), (22, 5), (19, 6), (20, 5), (21, 6), (24, 4), (22, 6), (23, 5), (12, 7), (24, 5), (18, 7), (19, 7), (21, 7), (22, 7), (24, 6), (24, 7)),
)


def kind_of(k, wide_count):
    return KINDS[PLAN[k]] if wide_count == 8 else PairFirst


def encoder(
    wide_count,
    patches_in,
    kinds_in,
    cot_in,
    slots_in,
    proj_in,
    offs_in,
    plc_in,
    pos_in,
    scales,
    shifts,
    att_in,
    abias_in,
    comb_in,
    cbias,
    exp_in,
    ebias_in,
    red_in,
    rbias,
    sums_out,
    shared_out,
    encoded_out,
    patches_out,
    wa,
    wc,
    we,
    wr,
    abias,
    ebias,
    proj,
    pos,
    rows_all,
    kinds_all,
    flags,
    grad,
    stream,
    middle,
    first,
    second,
    qkv,
    probs,
    mixed,
    slope,
    hidden,
    out_round,
    pre,
    mid_round,
    grad_mixed,
    grad_qkv,
    key_acc,
    acc,
    give,
    take,
    take_top,
    cot,
    send_part,
    recv_part,
    total,
    ring,
    shared,
    shared_buf,
    top_own,
    top_other,
    patch_own,
    patch_other,
    small,
    bias_rows,
    load_sem,
    weight_send,
    weight_recv,
    rows_send,
    rows_recv,
    y_send,
    y_recv,
    part_send,
    part_recv,
    ring_send,
    ring_recv,
    shared_send,
    shared_recv,
    last_send,
    last_recv,
    store_sem,
    credit,
):
    place = Place(wide_count)
    y, c, w, n = place.y, place.c, place.w, place.n
    sibling, partner = place.sibling, place.partner
    local, width = cot_in.shape
    patch = proj_in.shape[0] // 2
    seq = pos_in.shape[0]
    layers = scales.shape[0]
    cols = att_in.shape[2]
    heads = cols // HD
    hid = exp_in.shape[2]
    scale = HD ** (-0.5)
    diagonal = y == c
    chunks = seq // local

    barrier = pltpu.get_barrier_semaphore()
    for step in (1, 2, 3):
        pl.semaphore_signal(barrier, 1, device_id=(w, (n + step) % 4), device_id_type=MESH)
    pl.semaphore_signal(barrier, 1, device_id=place.pair, device_id_type=MESH)
    pl.semaphore_signal(barrier, 1, device_id=place.inward, device_id_type=MESH)

    @pl.when(place.has_out)
    def _():
        pl.semaphore_signal(barrier, 1, device_id=place.outward, device_id_type=MESH)
        pl.semaphore_wait(barrier, 6)

    @pl.when(jnp.logical_not(place.has_out))
    def _():
        pl.semaphore_wait(barrier, 5)

    def span(index, size):
        return pl.ds(pl.multiple_of(index * size, size), size)

    far = (w, 2 - y)
    near = (w, 3 * y)
    here = span(c, local)
    row_copies = []
    for k, (src, dst, here) in enumerate(
        ((patches_in, rows_all, here), (cot_in, cot, here), (kinds_in, kinds_all, pl.ds(c, 1)))
    ):
        row_copies.append(
            (
                Copy(src, dst.at[here], rows_send.at[k, 0], rows_recv.at[k, c], far),
                Copy(src, dst.at[here], rows_send.at[k, 1], rows_recv.at[k, c], near),
                pltpu.make_async_copy(src, dst.at[here], rows_recv.at[k, c]),
            )
        )

    def send_rows(k):
        to_far, to_near, to_self = row_copies[k]
        to_far.start()

        @pl.when(diagonal)
        def _():
            to_self.start()

        @pl.when(jnp.logical_not(diagonal))
        def _():
            to_near.start()

    def wait_rows(k, dst, size):
        for h in range(2):
            spot = dst.at[pl.ds(h * size, size)]
            pltpu.make_async_copy(spot, spot, rows_recv.at[k, h]).wait()

    send_rows(0)
    send_rows(2)
    weights = []
    for layer in range(layers):
        for src, dst in ((att_in, wa), (comb_in, wc), (exp_in, we), (red_in, wr)):
            weights.append((src.at[layer], dst.at[layer]))
    own_loads = [pltpu.make_async_copy(src, dst.at[0], load_sem.at[k]) for k, (src, dst) in enumerate(weights)]
    sib_loads = [
        Copy(src, dst.at[1], weight_send.at[k], weight_recv.at[k], sibling) for k, (src, dst) in enumerate(weights)
    ]
    proj_load = pltpu.make_async_copy(proj_in, proj, load_sem.at[8])
    pos_load = pltpu.make_async_copy(pos_in, pos, load_sem.at[9])
    abias_copy = Copy(abias_in, abias.at[1], weight_send.at[8], weight_recv.at[8], sibling)
    ebias_copy = Copy(ebias_in, ebias.at[1], weight_send.at[9], weight_recv.at[9], sibling)
    abias_copy.start()
    ebias_copy.start()
    proj_load.start()
    pos_load.start()
    for k in range(8):
        own_loads[k].start()
        sib_loads[k].start()
        if k == 3:
            send_rows(1)
    abias[0] = abias_in[...]
    ebias[0] = ebias_in[...]
    small[...] = jnp.zeros_like(small)
    bias_rows[...] = jnp.zeros_like(bias_rows)

    def need(k):
        own_loads[k].wait()
        sib_loads[k].wait_recv()

    def note(row, values):
        small[row : row + 1, :] += column_sums(values)

    def param(ref, layer, row):
        return ref[layer, row : row + 1, :].astype(F32)

    def y_copy(index, slot, rows):
        return Copy(
            give.at[slot, rows], take.at[slot, rows], y_send.at[index[0], index[1]], y_recv.at[index[0], index[1]], partner
        )

    def offer(exchange, slot, ch, values):
        rows = span(ch, local)
        give[slot, rows, :] = values.astype(BF)
        y_copy((exchange, ch), slot, rows).start()

    def collect(exchange, slot, ch):
        rows = span(ch, local)
        y_copy((exchange, ch), slot, rows).wait()
        return give[slot, rows, :].astype(F32) + take[slot, rows, :].astype(F32)

    def head_mask(rows, h):
        lane = lax.broadcasted_iota(jnp.int32, (rows, cols), 1)
        return (lane >= h * HD) & (lane < (h + 1) * HD)

    place_col = lax.broadcasted_iota(jnp.int32, (seq, slots_in.shape[1]), 0)
    slot_row = slots_in[pl.ds(c, 1), :]
    masked = jnp.max(jnp.where(place_col == slot_row, 1.0, 0.0).astype(F32), axis=1, keepdims=True)
    wait_rows(0, rows_all, local)
    wait_rows(2, kinds_all, 1)
    for h in range(2):
        kinds = jnp.broadcast_to(jnp.where(kinds_all[h : h + 1, :] == 1, 1.0, 0.0), (128, 128)).astype(F32)
        flags[pl.ds(h * local, local), :] = kinds.T.astype(BF)
    proj_load.wait()
    pos_load.wait()
    wide_flags = jnp.concatenate([flags[...]] * (patch // 128), axis=1)
    patches = rows_all[...]
    kind_one = patches * wide_flags
    kind_zero = patches - kind_one
    is_one = flags[:, 0:1].astype(F32)
    lifted = nn(kind_zero, proj[0:patch, :]) + nn(kind_one, proj[patch : 2 * patch, :])
    offset = jnp.where(is_one > 0.5, offs_in[1:2, :].astype(F32), offs_in[0:1, :].astype(F32))
    stream[0] = jnp.where(masked > 0.5, plc_in[...].reshape(1, width).astype(F32), lifted + offset) + pos[...].astype(F32)

    def before_attention(layer):
        def norm(ch):
            rows = span(ch, local)
            hat, _ = hat_of(stream[layer, rows, :])
            first[layer, rows, :] = (hat * param(scales, layer, 0) + param(shifts, layer, 0)).astype(BF)

        loop(chunks, norm)

    def project(layer):
        need(4 * layer)
        if layer == 0:
            abias_copy.wait_recv()
            ebias_copy.wait_recv()

        def group(g):
            rows = first[layer]
            query = (nt(rows, wa[layer, g, 0]) + abias[g, layer, 0:1, :].astype(F32)) * scale
            qkv[layer, g, 0] = query.astype(BF)
            qkv[layer, g, 1] = nt(rows, wa[layer, g, 1]).astype(BF)
            qkv[layer, g, 2] = (nt(rows, wa[layer, g, 2]) + abias[g, layer, 1:2, :].astype(F32)).astype(BF)

        loop(2, group)

    def attend(layer, exchange, slot):
        need(4 * layer + 1)

        def chunk(ch):
            rows = span(ch, local)

            def group(g):
                total_mixed = jnp.zeros((local, cols), F32)
                query, key, value = qkv[layer, g, 0, rows, :], qkv[layer, g, 1], qkv[layer, g, 2]
                for h in range(heads):
                    scores = nt(jnp.where(head_mask(local, h), query, 0), key)
                    raised = jnp.exp(scores - jnp.max(scores, axis=-1, keepdims=True))
                    prob = (raised / jnp.sum(raised, axis=-1, keepdims=True)).astype(BF)
                    probs[layer, g * heads + h, rows, :] = prob
                    total_mixed += nn(prob, jnp.where(head_mask(seq, h), value, 0))
                mixed[layer, g, rows, :] = total_mixed.astype(BF)

            loop(2, group)
            offer(exchange, slot, ch, nn(mixed[layer, 0, rows, :], wc[layer, 0]) + nn(mixed[layer, 1, rows, :], wc[layer, 1]))

        loop(chunks, chunk)

    def to_middle(layer, exchange, slot, ch):
        rows = span(ch, local)
        values = stream[layer, rows, :] + collect(exchange, slot, ch) + cbias[layer : layer + 1, :].astype(F32)
        middle[layer, rows, :] = values
        hat, _ = hat_of(values)
        second[layer, rows, :] = (hat * param(scales, layer, 1) + param(shifts, layer, 1)).astype(BF)

    def activate(layer, g, rows):
        value = nn(second[layer, rows, :], we[layer, g]) + ebias[g, layer : layer + 1, :].astype(F32)
        cdf = 0.5 * (1.0 + lax.erf(value * (0.5**0.5)))
        hidden[layer, g, rows, :] = (value * cdf).astype(BF)
        density = jnp.exp(-0.5 * value * value) * 0.3989422804014327
        slope[layer, g, rows, :] = (cdf + value * density).astype(BF)

    def feed_back(layer, g, rows):
        grad_hidden = nt(out_round[rows, :], wr[layer, g])
        grad_pre = grad_hidden * slope[layer, g, rows, :].astype(F32)
        bias_rows[layer, g, 0:1, :] += column_sums(grad_pre)
        pre[g, rows, :] = grad_pre.astype(BF)

    def settle(row, layer, part, base, values, gain_row):
        hat, inverse = hat_of(base)
        note(2 * layer + part, values * hat)
        note(4 + 2 * layer + part, values)
        scaled = values * param(scales, layer, part)
        inner = scaled - jnp.mean(scaled, axis=-1, keepdims=True)
        return inverse * (inner - hat * jnp.mean(scaled * hat, axis=-1, keepdims=True))

    for layer in range(layers):
        before_attention(layer)
        project(layer)
        attend(layer, 2 * layer, 0)
        need(4 * layer + 2)
        need(4 * layer + 3)
        if layer + 1 < layers:

            def chunk(ch):
                rows = span(ch, local)
                to_middle(layer, 2 * layer, 0, ch)

                def group(g):
                    activate(layer, g, rows)
                    part = nn(hidden[layer, g, rows, :], wr[layer, g])

                    @pl.when(g == 0)
                    def _():
                        acc[...] = part

                    @pl.when(g == 1)
                    def _():
                        acc[...] += part

                loop(2, group)
                offer(2 * layer + 1, 1, ch, acc[...])

            loop(chunks, chunk)

            def after(ch):
                rows = span(ch, local)
                stream[layer + 1, rows, :] = (
                    middle[layer, rows, :] + collect(2 * layer + 1, 1, ch) + rbias[layer : layer + 1, :].astype(F32)
                )

            loop(chunks, after)

    pieces = []
    at = 0
    cut = hid // 4
    spots = [(hid + (k // 2) * cut if k % 2 == 0 else (k // 2) * cut, cut) for k in range(8)]
    spots += [(2 * hid + j * cols, cols) for j in range(3)] + [(2 * hid + 3 * cols, cols + 32)]
    per_layer = len(spots)
    for layer in reversed(range(layers)):
        for row, count in spots:
            k = len(pieces)
            kind = kind_of(k, wide_count)
            piece = kind(
                place,
                total.at[layer],
                row,
                count,
                ring,
                at,
                sums_out.at[layer],
                ring_send.at[k],
                ring_recv.at[k],
                store_sem.at[k],
            )
            pieces.append((piece, layer, row, count))
            at += kind.space(count)

    def part_copy(k):
        _, _, row, count = pieces[k]
        return Copy(
            send_part.at[k % 4, pl.ds(0, count)],
            recv_part.at[pl.ds(row, count)],
            part_send.at[k],
            part_recv.at[k],
            sibling,
        )

    def begin(k, own, other):
        _, layer, row, count = pieces[k]
        if k >= 4:
            part_copy(k - 4).wait_send()
        if k == per_layer:
            pl.semaphore_wait(credit, 1)
        other(send_part.at[k % 4])
        part_copy(k).start()
        own(total.at[layer, pl.ds(row, count)])

    def join(k):
        piece, layer, row, count = pieces[k]
        part_copy(k).wait_recv()
        add_into(total.at[layer], row, recv_part, row, count)
        if k == per_layer - 1:
            pl.semaphore_signal(credit, 1, device_id=sibling, device_id_type=MESH)
        piece.stages[0]()

    ticks = iter(TICKS)

    def tick():
        for k, stage in next(ticks):
            stages = (pieces[k][0] if k < len(pieces) else shared_piece[0]).stages
            if stage < len(stages):
                stages[stage]()

    shared_piece = []

    def weight_grad(left, right):
        def into(ref):
            ref[pl.ds(0, left.shape[1]), :] = tn(left[...], right[...]).astype(BF)

        return into

    def run_pieces(base, works):
        for i, (own, other) in enumerate(works):
            begin(base + i, own, other)
            if i > 0:
                join(base + i - 1)
                tick()
        join(base + len(works) - 1)
        tick()

    def feed_grads(layer, base):
        works = []
        for k in range(8):
            lanes = pl.ds((k // 2) * cut, cut)
            if k % 2 == 0:
                works.append([weight_grad(hidden.at[layer, g, :, lanes], out_round) for g in range(2)])
            else:
                works.append([weight_grad(second.at[layer, :, lanes], pre.at[g]) for g in range(2)])
        run_pieces(base, works)

    def attention_grads(layer, base):
        def comb(g):
            grad_comb = weight_grad(mixed.at[layer, g], mid_round)

            def into(ref):
                grad_comb(ref)
                ref[pl.ds(cols, 32), :] = bias_rows[layer, g].astype(BF)

            return into

        works = [[weight_grad(grad_qkv.at[g, j], first.at[layer]) for g in range(2)] for j in range(3)]
        works.append([comb(g) for g in range(2)])
        run_pieces(base + 8, works)

    wait_rows(1, cot, local)
    last = layers - 1

    def start_back(ch):
        rows = span(ch, local)
        grad[rows, :] = cot[rows, :].astype(F32)

    loop(chunks, start_back)

    def top_send():
        return Copy(top_other, top_own, last_send.at[0], last_recv.at[0], sibling)

    top_copy = Copy(give.at[2], take_top, last_send.at[1], last_recv.at[1], partner)

    for layer in reversed(range(layers)):
        base = (last - layer) * per_layer
        exchange = 4 + 2 * (last - layer)

        def chunk(ch):
            rows = span(ch, local)
            note(10 + layer, grad[rows, :])
            out_round[rows, :] = grad[rows, :].astype(BF)
            if layer == last:
                to_middle(layer, 2 * layer, 0, ch)

            def group(g):
                if layer == last:
                    activate(layer, g, rows)
                feed_back(layer, g, rows)
                part = nt(pre[g, rows, :], we[layer, g])

                @pl.when(g == 0)
                def _():
                    acc[...] = part

                @pl.when(g == 1)
                def _():
                    acc[...] += part

            loop(2, group)
            offer(exchange, 1, ch, acc[...])

        loop(chunks, chunk)
        tick()

        if layer == last:

            def top(ch):
                rows = span(ch, local)
                give[2, rows, :] = (
                    nn(hidden[layer, 0, rows, :], wr[layer, 0]) + nn(hidden[layer, 1, rows, :], wr[layer, 1])
                ).astype(BF)

            loop(chunks, top)

            @pl.when(jnp.logical_not(diagonal))
            def _():
                top_copy.start()

        feed_grads(layer, base)

        def chunk(ch):
            rows = span(ch, local)
            grad_second = collect(exchange, 1, ch)
            grad_middle = grad[rows, :] + settle(rows, layer, 1, middle[layer, rows, :], grad_second, None)
            note(8 + layer, grad_middle)
            grad[rows, :] = grad_middle
            mid_round[rows, :] = grad_middle.astype(BF)

            def group(g):
                mixed_back = nt(mid_round[rows, :], wc[layer, g]).astype(BF)
                query, key, value = qkv[layer, g, 0, rows, :], qkv[layer, g, 1], qkv[layer, g, 2]
                query_acc = jnp.zeros((local, cols), F32)
                key_sum = jnp.zeros((seq, cols), F32)
                value_sum = jnp.zeros((seq, cols), F32)
                for h in range(heads):
                    prob = probs[layer, g * heads + h, rows, :]
                    back = jnp.where(head_mask(local, h), mixed_back, 0)
                    grad_probs = nt(back, value)
                    value_sum += tn(prob, back)
                    weight = prob.astype(F32)
                    center = jnp.sum(weight * grad_probs, axis=-1, keepdims=True)
                    grad_scores = (weight * (grad_probs - center)).astype(BF)
                    query_acc += nn(grad_scores, jnp.where(head_mask(seq, h), key, 0))
                    key_sum += tn(grad_scores, jnp.where(head_mask(local, h), query, 0))
                grad_query = (query_acc.astype(BF).astype(F32) * scale).astype(BF)
                grad_qkv[g, 0, rows, :] = grad_query
                bias_rows[layer, g, 1:2, 0:cols] += column_sums(grad_query.astype(F32))

                @pl.when(ch == 0)
                def _():
                    key_acc[g, 0] = key_sum
                    key_acc[g, 1] = value_sum

                @pl.when(ch > 0)
                def _():
                    key_acc[g, 0] += key_sum
                    key_acc[g, 1] += value_sum

            loop(2, group)

        loop(chunks, chunk)
        tick()

        def close(g):
            grad_qkv[g, 1] = key_acc[g, 0].astype(BF)
            grad_value = key_acc[g, 1].astype(BF)
            grad_qkv[g, 2] = grad_value
            bias_rows[layer, g, 2:3, 0:cols] += column_sums(grad_value.astype(F32))

        loop(2, close)

        def chunk(ch):
            rows = span(ch, local)

            def group(g):
                part = (
                    nn(grad_qkv[g, 0, rows, :], wa[layer, g, 0])
                    + nn(grad_qkv[g, 1, rows, :], wa[layer, g, 1])
                    + nn(grad_qkv[g, 2, rows, :], wa[layer, g, 2])
                )

                @pl.when(g == 0)
                def _():
                    acc[...] = part

                @pl.when(g == 1)
                def _():
                    acc[...] += part

            loop(2, group)
            offer(exchange + 1, 0, ch, acc[...])

        loop(chunks, chunk)
        tick()
        attention_grads(layer, base)

        if layer == last:

            @pl.when(jnp.logical_not(diagonal))
            def _():
                top_copy.wait_send()

            @pl.when(diagonal)
            def _():
                top_copy.wait_recv()

                def finish_top(dst, half):
                    rows = span(half, local)
                    dst[...] = (
                        middle[layer, rows, :]
                        + (give[2, rows, :].astype(F32) + take_top[rows, :].astype(F32))
                        + rbias[layer : layer + 1, :].astype(F32)
                    )

                finish_top(top_other, 1 - c)
                top_send().start()
                finish_top(top_own, c)

        def chunk(ch):
            rows = span(ch, local)
            grad_first = collect(exchange + 1, 0, ch)
            grad[rows, :] += settle(rows, layer, 0, stream[layer, rows, :], grad_first, None)

        loop(chunks, chunk)
        tick()

    lifted_grad = jnp.where(masked > 0.5, 0.0, grad[...])
    note(14, grad[...] - lifted_grad)
    one_grad = jnp.where(is_one > 0.5, lifted_grad, 0.0)
    note(12, lifted_grad - one_grad)
    note(13, one_grad)
    lifted_round = lifted_grad.astype(BF)
    shared_rows = shared.shape[0]
    half_rows = shared_rows // 2
    flag_side = jnp.where(y == 1, wide_flags.astype(F32), 1.0 - wide_flags.astype(F32)).astype(BF)
    shared[0:patch, :] = tn(rows_all[...] * flag_side, lifted_round).astype(BF)
    shared[patch : patch + local, :] = grad[span(y, local), :].astype(BF)
    shared[patch + local : shared_rows, :] = small[...].astype(BF)
    keep_row, give_row = span(c, half_rows), span(1 - c, half_rows)
    shared_part = Copy(
        shared.at[give_row], shared_buf.at[pl.ds(0, half_rows)], last_send.at[2], last_recv.at[2], sibling
    )
    shared_part.start()

    patch_copy = Copy(patch_other, patch_own, last_send.at[3], last_recv.at[3], sibling)

    @pl.when(diagonal)
    def _():
        def half_back(dst, half):
            rows = span(half, local)
            flag = flags[rows, :].astype(F32)[:, 0:1]
            masks = jnp.max(
                jnp.where(
                    lax.broadcasted_iota(jnp.int32, (local, slots_in.shape[1]), 0) + half * local == slot_row, 1.0, 0.0
                ).astype(F32),
                axis=1,
                keepdims=True,
            )
            values = jnp.where(masks > 0.5, 0.0, grad[rows, :]).astype(BF)
            dst[...] = jnp.where(flag > 0.5, nt(values, proj[patch : 2 * patch, :]), nt(values, proj[0:patch, :]))

        half_back(patch_other, 1 - c)
        patch_copy.start()
        half_back(patch_own, c)

    shared_part.wait()
    add_into(shared, pl.multiple_of(c * half_rows, 16), shared_buf, 0, half_rows)
    sum_shared = PairFirst(
        place,
        shared,
        pl.multiple_of(c * half_rows, 16),
        half_rows,
        shared_buf,
        half_rows,
        shared_out.at[y],
        shared_send,
        shared_recv,
        store_sem.at[len(pieces)],
    )
    across = Copy(shared_out.at[y, keep_row], shared_out.at[y, keep_row], last_send.at[4], last_recv.at[4], partner)
    across_back = Copy(
        shared_out.at[1 - y, keep_row], shared_out.at[1 - y, keep_row], last_send.at[4], last_recv.at[4], partner
    )
    ends = []
    for k in range(2):
        ends.append(
            (
                Copy(
                    shared_out.at[k, keep_row], shared_out.at[k, keep_row], last_send.at[5 + k], last_recv.at[5 + k], sibling
                ),
                Copy(
                    shared_out.at[k, give_row], shared_out.at[k, give_row], last_send.at[5 + k], last_recv.at[5 + k], sibling
                ),
            )
        )

    def to_partner():
        sum_shared.s5()
        across.start()

    def to_sibling():
        across.wait_send()
        across_back.wait_recv()
        for out, _ in ends:
            out.start()

    def close_shared():
        for out, back in ends:
            out.wait_send()
            back.wait_recv()

    sum_shared.stages = sum_shared.stages[:5] + [to_partner, to_sibling, close_shared]
    shared_piece.append(sum_shared)
    sum_shared.s0()
    tick()
    tick()
    count = len(pieces)

    @pl.when(diagonal)
    def _():
        top_send().wait_send()
        patch_copy.wait_send()

    @pl.when(jnp.logical_not(diagonal))
    def _():
        top_send().wait_recv()
        patch_copy.wait_recv()

    finals = (
        pltpu.make_async_copy(top_own, encoded_out, store_sem.at[count + 1]),
        pltpu.make_async_copy(patch_own, patches_out, store_sem.at[count + 2]),
    )
    for copy in finals:
        copy.start()
    for copy in finals:
        copy.wait()

    for to_far, to_near, _ in row_copies:
        to_far.wait_send()

        @pl.when(jnp.logical_not(diagonal))
        def _():
            to_near.wait_send()

    for copy in sib_loads + [abias_copy, ebias_copy]:
        copy.wait_send()
    for k in range(count - 4, count):
        part_copy(k).wait_send()


def per_device(
    wide_count,
    patches,
    token_kind,
    mask_slots,
    projector,
    offsets,
    placeholder,
    positions,
    scales,
    shifts,
    attention,
    attn_bias,
    combiner,
    comb_bias,
    expander,
    expand_bias,
    reducer,
    reduce_bias,
    cotangent,
):
    local, patch = patches.shape
    seq, width = positions.shape
    layers = scales.shape[0]
    cols = attention.shape[3]
    heads = cols // HD
    hid = expander.shape[2]
    per_layer = 2 * hid + 4 * cols + 32
    shared_rows = patch + local + 64
    pieces = 12 * layers
    counts = ([hid // 4] * 8 + [cols] * 3 + [cols + 32]) * layers
    ring_rows = sum(kind_of(k, wide_count).space(count) for k, count in enumerate(counts))
    vmem = pl.BlockSpec(memory_space=pltpu.VMEM)
    anyw = pl.BlockSpec(memory_space=pl.ANY)
    dma = pltpu.SemaphoreType.DMA
    scratch = [
        pltpu.VMEM((layers, 2, 3, cols, width), BF),
        pltpu.VMEM((layers, 2, cols, width), BF),
        pltpu.VMEM((layers, 2, width, hid), BF),
        pltpu.VMEM((layers, 2, hid, width), BF),
        pltpu.VMEM((2, layers, 2, cols), BF),
        pltpu.VMEM((2, layers, hid), BF),
        pltpu.VMEM((2 * patch, width), BF),
        pltpu.VMEM((seq, width), BF),
        pltpu.VMEM((seq, patch), BF),
        pltpu.VMEM((2, local), jnp.int32),
        pltpu.VMEM((seq, 128), BF),
        pltpu.VMEM((seq, width), F32),
        pltpu.VMEM((layers, seq, width), F32),
        pltpu.VMEM((layers, seq, width), F32),
        pltpu.VMEM((layers, seq, width), BF),
        pltpu.VMEM((layers, seq, width), BF),
        pltpu.VMEM((layers, 2, 3, seq, cols), BF),
        pltpu.VMEM((layers, 2 * heads, seq, seq), BF),
        pltpu.VMEM((layers, 2, seq, cols), BF),
        pltpu.VMEM((layers, 2, seq, hid), BF),
        pltpu.VMEM((layers, 2, seq, hid), BF),
        pltpu.VMEM((seq, width), BF),
        pltpu.VMEM((2, seq, hid), BF),
        pltpu.VMEM((seq, width), BF),
        pltpu.VMEM((8, 128), BF),
        pltpu.VMEM((2, 3, seq, cols), BF),
        pltpu.VMEM((2, 2, seq, cols), F32),
        pltpu.VMEM((local, width), F32),
        pltpu.VMEM((3, seq, width), BF),
        pltpu.VMEM((2, seq, width), BF),
        pltpu.VMEM((seq, width), BF),
        pltpu.VMEM((seq, width), BF),
        pltpu.VMEM((4, cols + 32, width), BF),
        pltpu.VMEM((per_layer, width), BF),
        pltpu.VMEM((layers, per_layer, width), BF),
        pltpu.VMEM((ring_rows, width), BF),
        pltpu.VMEM((shared_rows, width), BF),
        pltpu.VMEM((shared_rows // 2 + 3 * (shared_rows // 4), width), BF),
        pltpu.VMEM((local, width), F32),
        pltpu.VMEM((local, width), F32),
        pltpu.VMEM((local, patch), F32),
        pltpu.VMEM((local, patch), F32),
        pltpu.VMEM((64, width), F32),
        pltpu.VMEM((layers, 2, 32, width), F32),
        dma((10,)),
        dma((10,)),
        dma((10,)),
        dma((3, 2)),
        dma((3, 2)),
        dma((8, 2)),
        dma((8, 2)),
        dma((pieces,)),
        dma((pieces,)),
        dma((pieces, 11)),
        dma((pieces, 7)),
        dma((5,)),
        dma((5,)),
        dma((7,)),
        dma((7,)),
        dma((pieces + 3,)),
        pltpu.SemaphoreType.REGULAR,
    ]
    sums, shared, encoded, grad_patches = pl.pallas_call(
        functools.partial(encoder, wide_count),
        out_shape=(
            jax.ShapeDtypeStruct((layers, per_layer, width), BF),
            jax.ShapeDtypeStruct((2, shared_rows, width), BF),
            jax.ShapeDtypeStruct((local, width), F32),
            jax.ShapeDtypeStruct((local, patch), F32),
        ),
        in_specs=[anyw, vmem, anyw, vmem, anyw, vmem, vmem, anyw, vmem, vmem, anyw, vmem, anyw, vmem, anyw, vmem, anyw, vmem],
        out_specs=(anyw, anyw, anyw, anyw),
        scratch_shapes=scratch,
        compiler_params=pltpu.CompilerParams(
            collective_id=0, has_side_effects=True, vmem_limit_bytes=63 * 1024 * 1024 + 512 * 1024
        ),
        name="encoder",
    )(
        patches,
        token_kind.reshape(1, local),
        cotangent,
        mask_slots,
        projector.reshape(2 * patch, width),
        offsets,
        placeholder,
        positions,
        scales,
        shifts,
        attention.transpose(0, 1, 3, 2),
        attn_bias,
        combiner,
        comb_bias,
        expander,
        expand_bias,
        reducer,
        reduce_bias,
    )
    f32 = functools.partial(jax.ShapeDtypeStruct, dtype=F32)
    finished = pl.pallas_call(
        widen,
        out_shape=(
            f32((local, width)),
            f32((local, patch)),
            f32((2, patch, width)),
            f32((2, width)),
            f32((width,)),
            f32((seq, width)),
            f32((layers, 2, width)),
            f32((layers, 2, width)),
            f32((layers, 3, cols, width)),
            f32((layers, 2, cols)),
            f32((layers, cols, width)),
            f32((layers, width)),
            f32((layers, width, hid)),
            f32((layers, hid)),
            f32((layers, hid, width)),
            f32((layers, width)),
        ),
        in_specs=[anyw] * 4,
        out_specs=[anyw, anyw, anyw, vmem, vmem, anyw, vmem, vmem, anyw, vmem, anyw, vmem, anyw, vmem, anyw, vmem],
        scratch_shapes=[
            pltpu.VMEM((layers, per_layer, width), BF),
            pltpu.VMEM((layers, per_layer - 32, width), F32),
            pltpu.VMEM((2, shared_rows, width), BF),
            pltpu.VMEM((2, patch + local, width), F32),
            pltpu.VMEM((local, width), F32),
            pltpu.VMEM((local, patch), F32),
            dma((layers, 4)),
            dma((layers, 6)),
            dma((2,)),
            dma((2, 2)),
            dma((2, 2)),
        ],
        compiler_params=pltpu.CompilerParams(vmem_limit_bytes=62 * 1024 * 1024),
        name="widen",
    )(sums, shared, encoded, grad_patches)
    return tuple(item.transpose(0, 1, 3, 2) if k == 8 else item for k, item in enumerate(finished))


def widen(
    sums,
    shared,
    encoded,
    grad_patches,
    encoded_out,
    patches_out,
    projector,
    offsets,
    placeholder,
    positions,
    scales,
    shifts,
    attention,
    attn_bias,
    combiner,
    comb_bias,
    expander,
    expand_bias,
    reducer,
    reduce_bias,
    sums_in,
    sums_wide,
    shared_in,
    shared_wide,
    encoded_held,
    patches_held,
    load_sem,
    store_sem,
    shared_sem,
    shared_store,
    through_sem,
):
    layers, width, hid = expander.shape
    cols = combiner.shape[1]
    patch = projector.shape[1]
    local = encoded.shape[0]
    through = [
        (pltpu.make_async_copy(src, held, through_sem.at[k, 0]), pltpu.make_async_copy(held, dst, through_sem.at[k, 1]))
        for k, (src, held, dst) in enumerate(
            ((encoded, encoded_held, encoded_out), (grad_patches, patches_held, patches_out))
        )
    ]
    tail = sums.shape[1] - 3 * cols - 2 * hid
    cuts = ((0, hid), (hid, hid), (2 * hid, 3 * cols), (2 * hid + 3 * cols, tail))
    loads = []
    for layer in range(layers):
        for k, (row, count) in enumerate(cuts):
            spot = (layer, pl.ds(row, count))
            loads.append(pltpu.make_async_copy(sums.at[spot], sums_in.at[spot], load_sem.at[layer, k]))
    shared_loads = [pltpu.make_async_copy(shared.at[k], shared_in.at[k], shared_sem.at[k]) for k in range(2)]
    for copy in loads + shared_loads + [load for load, _ in through]:
        copy.start()
    stores = []

    def convert(src, dst, row, count):
        def step(t):
            rows = pl.ds(pl.multiple_of(row + t * 64, 64), 64)
            dst[rows, :] = src[rows, :].astype(F32)

        loop(count // 64, step)

    for layer in range(layers):
        for k, (row, count) in enumerate(cuts):
            loads[layer * len(cuts) + k].wait()
            wide = min(count, sums_wide.shape[1] - row)
            convert(sums_in.at[layer], sums_wide.at[layer], row, wide)
            if k == 2:
                targets = [(attention.at[layer, j], row + j * cols, cols, 2 + j) for j in range(3)]
            else:
                targets = [((expander, reducer, None, combiner)[k].at[layer], row, wide, (0, 1, None, 5)[k])]
            for target, start, size, sem in targets:
                copy = pltpu.make_async_copy(sums_wide.at[layer, pl.ds(start, size)], target, store_sem.at[layer, sem])
                copy.start()
                stores.append(copy)
        bias = sums_in[layer, pl.ds(2 * hid + 4 * cols, 16), :].astype(F32)
        expand_bias[layer : layer + 1, :] = bias[0:1, :]
        attn_bias[layer, 0:1, :] = bias[1:2, :cols]
        attn_bias[layer, 1:2, :] = bias[2:3, :cols]
    for k in range(2):
        shared_loads[k].wait()
        convert(shared_in.at[k], shared_wide.at[k], 0, patch + local)
        for target, start, size, sem in (
            (projector.at[k], 0, patch, 0),
            (positions.at[pl.ds(k * local, local)], patch, local, 1),
        ):
            copy = pltpu.make_async_copy(shared_wide.at[k, pl.ds(start, size)], target, shared_store.at[k, sem])
            copy.start()
            stores.append(copy)
    for load, store in through:
        load.wait()
        store.start()
    small = shared_in[0, pl.ds(patch + local, 16), :].astype(F32)
    for layer in range(layers):
        scales[layer] = small[2 * layer : 2 * layer + 2, :]
        shifts[layer] = small[4 + 2 * layer : 6 + 2 * layer, :]
    comb_bias[...] = small[8:10, :]
    reduce_bias[...] = small[10:12, :]
    offsets[...] = small[12:14, :]
    placeholder[...] = small[14:15, :].reshape(width)
    for copy in stores + [store for _, store in through]:
        copy.wait()


def solution(mesh):
    rows = ("wide", "narrow")
    return jax.shard_map(
        functools.partial(per_device, mesh.shape["wide"]),
        mesh=mesh,
        in_specs=(
            P(rows, None),
            P(rows),
            P("wide", None),
            P(),
            P(),
            P(),
            P(),
            P(),
            P(),
            P(None, None, None, "narrow"),
            P(None, None, "narrow"),
            P(None, "narrow", None),
            P(),
            P(None, None, "narrow"),
            P(None, "narrow"),
            P(None, "narrow", None),
            P(),
            P(rows, None),
        ),
        out_specs=(
            P(rows, None),
            P(rows, None),
            P(),
            P(),
            P(),
            P(),
            P(),
            P(),
            P(None, None, None, "narrow"),
            P(None, None, "narrow"),
            P(None, "narrow", None),
            P(),
            P(None, None, "narrow"),
            P(None, "narrow"),
            P(None, "narrow", None),
            P(),
        ),
        check_vma=False,
    )
```

```python
import functools

import jax
import jax.numpy as jnp
from jax import lax
from jax.experimental import pallas as pl
from jax.experimental.pallas import tpu as pltpu
from jax.sharding import PartitionSpec as P

HD = 64
EPS = 1e-06
BF = jnp.bfloat16
F32 = jnp.float32
MESH = pl.DeviceIdType.MESH


def nn(left, right):
    return jnp.dot(left, right, preferred_element_type=F32)


def nt(left, right):
    return lax.dot_general(left, right, (((1,), (1,)), ((), ())), preferred_element_type=F32)


def tn(left, right):
    return lax.dot_general(left, right, (((0,), (0,)), ((), ())), preferred_element_type=F32)


def rolled(count, body):
    def step(index, carry):
        body(index)
        return carry

    lax.fori_loop(0, count, step, 0)


def loop(count, body):
    for index in range(count):
        body(index)


def hat_of(values):
    center = values - jnp.mean(values, axis=-1, keepdims=True)
    variance = jnp.mean(center * center, axis=-1, keepdims=True)
    scale = lax.rsqrt(variance + EPS)
    return center * scale, scale


def column_sums(values):
    return jnp.sum(values, axis=0, keepdims=True)


class Copy:
    def __init__(self, src, dst, send, recv, target):
        self.args = dict(src_ref=src, dst_ref=dst, send_sem=send, recv_sem=recv, device_id=target, device_id_type=MESH)

    def start(self):
        pltpu.make_async_remote_copy(**self.args).start()

    def wait(self):
        pltpu.make_async_remote_copy(**self.args).wait()

    def wait_send(self):
        pltpu.make_async_remote_copy(**self.args).wait_send()

    def wait_recv(self):
        pltpu.make_async_remote_copy(**self.args).wait_recv()


def add_into(dst, dst_row, src, src_row, rows):
    block = next(b for b in (48, 32, 16) if rows % b == 0)

    def step(index):
        into = pl.ds(pl.multiple_of(dst_row + index * block, 16), block)
        give = pl.ds(pl.multiple_of(src_row + index * block, 16), block)
        dst[into, :] = (dst[into, :].astype(F32) + src[give, :].astype(F32)).astype(BF)

    rolled(rows // block, step)


class Place:
    def __init__(self, wide_count):
        self.w = lax.axis_index("wide")
        self.n = lax.axis_index("narrow")
        self.y = self.n // 2
        self.c = self.n % 2
        self.x = self.w % 2
        self.z = self.w // 2
        line = wide_count // 2
        self.half = line // 2
        self.low = self.z < self.half
        self.side = jnp.where(self.low, 0, 1)
        self.depth = jnp.where(self.low, self.z, line - 1 - self.z)
        step = jnp.where(self.low, 2, -2)
        self.sibling = (self.w, self.n + 1 - 2 * self.c)
        self.partner = (self.w, self.n + 2 - 4 * self.y)
        self.pair = (self.w + 1 - 2 * self.x, self.n)
        self.inward = (self.w + step, self.n)
        self.outward = (self.w - jnp.where(self.depth > 0, step, -step), self.n)
        self.has_out = self.depth > 0
        self.inner = self.depth == self.half - 1


def hops(count, hop):
    if count == 1:
        hop(0)
    elif count > 1:
        rolled(count, hop)


class PairFirst:
    @staticmethod
    def space(rows):
        return rows // 2 * 3

    def __init__(self, place, total, row, rows, buf, at, out, send, recv, store):
        self.place, self.total, self.buf = place, total, buf
        half = rows // 2
        self.half, self.at = half, at
        mine = pl.multiple_of(row + place.x * half, 16)
        other = pl.multiple_of(row + (1 - place.x) * half, 16)
        self.mine = mine
        keep, give = total.at[pl.ds(mine, half)], total.at[pl.ds(other, half)]
        out_keep, out_give = out.at[pl.ds(mine, half)], out.at[pl.ds(other, half)]
        slots = [buf.at[pl.ds(at + k * half, half)] for k in range(3)]
        self.pair_in = Copy(give, slots[0], send.at[0], recv.at[0], place.pair)
        self.line_in = Copy(keep, slots[1], send.at[1], recv.at[1], place.inward)
        self.middle = Copy(keep, slots[2], send.at[2], recv.at[2], place.inward)
        self.line_out = Copy(keep, out_keep, send.at[3], recv.at[3], place.outward)
        self.line_on = Copy(out_keep, out_keep, send.at[3], recv.at[3], place.outward)
        self.pair_out = Copy(keep, out_keep, send.at[4], recv.at[4], place.pair)
        self.pair_on = Copy(out_keep, out_keep, send.at[4], recv.at[4], place.pair)
        self.other = Copy(out_give, out_give, send.at[4], recv.at[4], place.pair)
        self.store = pltpu.make_async_copy(keep, out_keep, store)
        self.stages = [self.s0, self.s1, self.s2, self.s3, self.s4, self.s5]

    def s0(self):
        self.pair_in.start()

    def s1(self):
        place = self.place
        self.pair_in.wait()
        add_into(self.total, self.mine, self.buf, self.at, self.half)
        if place.half == 1:
            self.middle.start()
            return

        @pl.when(place.depth == 0)
        def _():
            self.line_in.start()

    def s2(self):
        place = self.place

        def hop(k):
            @pl.when(place.depth == k + 1)
            def _():
                self.line_in.wait_recv()
                add_into(self.total, self.mine, self.buf, self.at + self.half, self.half)

            @pl.when((place.depth == k + 1) & jnp.logical_not(place.inner))
            def _():
                self.line_in.start()

        hops(place.half - 1, hop)
        if place.half > 1:

            @pl.when(place.inner)
            def _():
                self.middle.start()

    def s3(self):
        place = self.place

        @pl.when(place.inner)
        def _():
            self.middle.wait()
            add_into(self.total, self.mine, self.buf, self.at + 2 * self.half, self.half)
            if place.half > 1:
                self.line_out.start()
            self.pair_out.start()
            self.store.start()

    def s4(self):
        place = self.place

        def hop(k):
            @pl.when(place.depth == place.half - 2 - k)
            def _():
                self.line_on.wait_recv()
                self.pair_on.start()

            @pl.when((place.depth == place.half - 2 - k) & place.has_out)
            def _():
                self.line_on.start()

        hops(place.half - 1, hop)

    def s5(self):
        place = self.place

        @pl.when(place.inner)
        def _():
            self.store.wait()

        if place.half > 1:

            @pl.when(jnp.logical_not(place.inner))
            def _():
                self.line_in.wait_send()

            @pl.when(place.has_out)
            def _():
                self.line_out.wait_send()

        self.pair_out.wait_send()
        self.other.wait_recv()


class LineScatter:
    @staticmethod
    def space(rows):
        return rows // 4 * 7

    def __init__(self, place, total, row, rows, buf, at, out, send, recv, store):
        quarter = rows // 4
        self.place, self.total, self.row, self.quarter = place, total, row, quarter
        self.buf, self.at = buf, at
        mine = pl.multiple_of(row + place.z * quarter, 16)
        self.mine = mine
        low, high = (place.w - 2, place.n), (place.w + 2, place.n)

        def own(start, stop):
            return total.at[pl.ds(row + start * quarter, (stop - start) * quarter)]

        def slot(start, count):
            return buf.at[pl.ds(at + start * quarter, count * quarter)]

        self.up = [Copy(own(z + 1, 4), slot(z, 3 - z), send.at[0], recv.at[0], high) for z in range(3)]
        self.down = [Copy(own(0, z), slot(3, z), send.at[1], recv.at[1], low) for z in range(4)]
        keep, land = total.at[pl.ds(mine, quarter)], out.at[pl.ds(mine, quarter)]
        self.across = Copy(keep, slot(6, 1), send.at[2], recv.at[2], place.pair)
        self.store = pltpu.make_async_copy(keep, land, store)

        def spread(src, dst, k, target, way):
            return Copy(src, dst, send.at[3 + 4 * way + k], recv.at[3 + k], target)

        spots = [out.at[pl.ds(row + k * quarter, quarter)] for k in range(4)]
        self.first_up = [spread(own(k, k + 1), spots[k], k, high, 0) for k in range(4)]
        self.first_down = [spread(own(k, k + 1), spots[k], k, low, 1) for k in range(4)]
        self.on_up = [spread(spots[k], spots[k], k, high, 0) for k in range(4)]
        self.on_down = [spread(spots[k], spots[k], k, low, 1) for k in range(4)]
        self.stages = [self.s0, self.s1, self.s2, self.s3, self.s4, self.s5, self.s6, self.s7]

    def at_z(self, *works):
        for z, work in works:
            pl.when(self.place.z == z)(work)

    def take(self, copy, first, slot, count):
        copy.wait_recv()
        add_into(self.total, self.row + first * self.quarter, self.buf, self.at + slot * self.quarter, count * self.quarter)

    def s0(self):
        self.at_z((0, self.up[0].start), (3, self.down[3].start))

    def s1(self):
        def one():
            self.take(self.up[0], 1, 0, 3)
            self.up[1].start()

        def two():
            self.take(self.down[3], 0, 3, 3)
            self.down[2].start()

        self.at_z((1, one), (2, two))

    def s2(self):
        def one():
            self.take(self.down[2], 0, 3, 2)
            self.down[1].start()

        def two():
            self.take(self.up[1], 2, 1, 2)
            self.up[2].start()

        self.at_z((1, one), (2, two))

    def s3(self):
        self.at_z((0, lambda: self.take(self.down[1], 0, 3, 1)), (3, lambda: self.take(self.up[2], 3, 2, 1)))
        self.across.start()

    def s4(self):
        self.across.wait()
        add_into(self.total, self.mine, self.buf, self.at + 6 * self.quarter, self.quarter)
        self.store.start()

        def both(z):
            def work():
                self.first_up[z].start()
                self.first_down[z].start()

            return work

        self.at_z((0, self.first_up[0].start), (1, both(1)), (2, both(2)), (3, self.first_down[3].start))

    def s5(self):
        def one():
            self.on_up[0].wait_recv()
            self.on_up[0].start()
            self.on_down[2].wait_recv()
            self.on_down[2].start()

        def two():
            self.on_down[3].wait_recv()
            self.on_down[3].start()
            self.on_up[1].wait_recv()
            self.on_up[1].start()

        self.at_z((1, one), (2, two))

    def s6(self):
        def one():
            self.on_down[3].wait_recv()
            self.on_down[3].start()

        def two():
            self.on_up[0].wait_recv()
            self.on_up[0].start()

        self.at_z((1, one), (2, two))

    def s7(self):
        self.store.wait()

        def zero():
            for k in (1, 2, 3):
                self.on_down[k].wait_recv()
            for copy in (self.up[0], self.first_up[0]):
                copy.wait_send()

        def one():
            for copy in (self.up[1], self.down[1], self.first_up[1], self.on_up[0]):
                copy.wait_send()
            for copy in (self.first_down[1], self.on_down[2], self.on_down[3]):
                copy.wait_send()

        def two():
            for copy in (self.up[2], self.down[2], self.first_up[2], self.on_up[1], self.on_up[0]):
                copy.wait_send()
            for copy in (self.first_down[2], self.on_down[3]):
                copy.wait_send()

        def three():
            for k in (0, 1, 2):
                self.on_up[k].wait_recv()
            for copy in (self.down[3], self.first_down[3]):
                copy.wait_send()

        self.at_z((0, zero), (1, one), (2, two), (3, three))


KINDS = (PairFirst, LineScatter,)
PLAN = (1, 1, 0, 0, 0, 0, 0, 1, 1, 0, 0, 0, 0, 0, 0, 1, 0, 0, 0, 0, 1, 0, 1, 0)
TICKS = (
    (),
    (),
    (),
    (),
    (),
    (),
    (),
    (),
    (),
    ((0, 1),),
    ((1, 1), (2, 1)),
    (),
    (),
    ((5, 1),),
    ((4, 1), (7, 1), (2, 2), (1, 2), (3, 1), (0, 2)),
    (),
    ((8, 1), (0, 3), (1, 3), (5, 2), (2, 3)),
    ((10, 1), (8, 2), (0, 4), (6, 1), (4, 2)),
    ((1, 4),),
    ((7, 2),),
    ((5, 3), (3, 2), (8, 3), (10, 2)),
    ((7, 3), (4, 3), (13, 1)),
    (),
    (),
    ((11, 1), (5, 4), (9, 1), (1, 5), (3, 3), (0, 5), (6, 2)),
    ((15, 1), (10, 3), (14, 1)),
    ((6, 3), (7, 4), (11, 2)),
    ((0, 6), (2, 4), (13, 2), (3, 4), (16, 1)),
    ((15, 2),),
    ((10, 4), (1, 6)),
    ((9, 2),),
    ((8, 4),),
    ((11, 3), (13, 3), (12, 1), (19, 1), (20, 1), (1, 7), (7, 5), (14, 2), (9, 3), (7, 6), (22, 1), (16, 2), (4, 4), (20, 2), (0, 7), (8, 5), (12, 2), (9, 4), (14, 3), (16, 3), (23, 1), (11, 4), (19, 2), (24, 1), (15, 3), (18, 1), (13, 4), (8, 6), (4, 5), (2, 5), (20, 3), (12, 3), (24, 2), (21, 1), (22, 2), (16, 4), (14, 4), (8, 7), (19, 3), (22, 3), (23, 2), (9, 5), (17, 1), (24, 3), (6, 4), (5, 5), (11, 5), (18, 2), (23, 3), (21, 2), (16, 5), (14, 5), (17, 2), (15, 4), (10, 5), (18, 3), (21, 3), (19, 4), (24, 4), (23, 4), (20, 4), (15, 5), (17, 3), (22, 4), (20, 5), (24, 5), (6, 5), (22, 5), (21, 4), (3, 5), (18, 4), (20, 6), (7, 7), (13, 5), (22, 6), (12, 4), (17, 4), (15, 6), (23, 5), (20, 7), (24, 6), (19, 5), (12, 5), (21, 5), (22, 7), (18, 5), (24, 7), (15, 7), (17, 5)),
    (),
)


def kind_of(k, wide_count):
    return KINDS[PLAN[k]] if wide_count == 8 else PairFirst


def encoder(
    wide_count,
    patches_in,
    kinds_in,
    cot_in,
    slots_in,
    proj_in,
    offs_in,
    plc_in,
    pos_in,
    scales,
    shifts,
    att_in,
    abias_in,
    comb_in,
    cbias,
    exp_in,
    ebias_in,
    red_in,
    rbias,
    sums_out,
    shared_out,
    encoded_out,
    patches_out,
    wa,
    wc,
    we,
    wr,
    abias,
    ebias,
    proj,
    pos,
    rows_all,
    kinds_all,
    flags,
    grad,
    stream,
    middle,
    first,
    second,
    qkv,
    probs,
    mixed,
    slope,
    hidden,
    out_round,
    pre,
    mid_round,
    grad_qkv,
    key_acc,
    give,
    take,
    take_top,
    cot,
    send_part,
    recv_part,
    total,
    ring,
    shared,
    shared_buf,
    top_own,
    top_other,
    patch_own,
    patch_other,
    small,
    bias_rows,
    load_sem,
    weight_send,
    weight_recv,
    rows_send,
    rows_recv,
    y_send,
    y_recv,
    part_send,
    part_recv,
    ring_send,
    ring_recv,
    shared_send,
    shared_recv,
    last_send,
    last_recv,
    store_sem,
    credit,
):
    place = Place(wide_count)
    y, c, w, n = place.y, place.c, place.w, place.n
    sibling, partner = place.sibling, place.partner
    local, width = cot_in.shape
    patch = proj_in.shape[0] // 2
    seq = pos_in.shape[0]
    layers = scales.shape[0]
    cols = att_in.shape[2]
    heads = cols // HD
    hid = exp_in.shape[2]
    scale = HD ** (-0.5)
    diagonal = y == c
    chunks = seq // local

    barrier = pltpu.get_barrier_semaphore()
    for step in (1, 2, 3):
        pl.semaphore_signal(barrier, 1, device_id=(w, (n + step) % 4), device_id_type=MESH)
    pl.semaphore_signal(barrier, 1, device_id=place.pair, device_id_type=MESH)
    pl.semaphore_signal(barrier, 1, device_id=place.inward, device_id_type=MESH)

    @pl.when(place.has_out)
    def _():
        pl.semaphore_signal(barrier, 1, device_id=place.outward, device_id_type=MESH)

    def span(index, size):
        if isinstance(index, int):
            return pl.ds(index * size, size)
        return pl.ds(pl.multiple_of(index * size, size), size)

    far = (w, 2 - y)
    near = (w, 3 * y)
    here = span(c, local)
    row_copies = []
    for k, (src, dst, here) in enumerate(
        ((patches_in, rows_all, here), (cot_in, cot, here), (kinds_in, kinds_all, pl.ds(c, 1)))
    ):
        row_copies.append(
            (
                Copy(src, dst.at[here], rows_send.at[k, 0], rows_recv.at[k, c], far),
                Copy(src, dst.at[here], rows_send.at[k, 1], rows_recv.at[k, c], near),
                pltpu.make_async_copy(src, dst.at[here], rows_recv.at[k, c]),
            )
        )

    def send_rows(k):
        to_far, to_near, to_self = row_copies[k]
        to_far.start()

        @pl.when(diagonal)
        def _():
            to_self.start()

        @pl.when(jnp.logical_not(diagonal))
        def _():
            to_near.start()

    def wait_rows(k, dst, size):
        for h in range(2):
            spot = dst.at[pl.ds(h * size, size)]
            pltpu.make_async_copy(spot, spot, rows_recv.at[k, h]).wait()

    weights = []
    for layer in range(layers):
        for src, dst in ((att_in, wa), (comb_in, wc), (exp_in, we), (red_in, wr)):
            if dst is wc:
                halves = [wc.at[layer, pl.ds(k * cols, cols)] for k in range(2)]
            else:
                halves = [dst.at[layer, k] for k in range(2)]
            weights.append((src.at[layer], *halves))
    own_loads = [pltpu.make_async_copy(src, own, load_sem.at[k]) for k, (src, own, _) in enumerate(weights)]
    sib_loads = [
        Copy(src, sib, weight_send.at[k], weight_recv.at[k], sibling) for k, (src, _, sib) in enumerate(weights)
    ]
    proj_load = pltpu.make_async_copy(proj_in, proj, load_sem.at[8])
    pos_load = pltpu.make_async_copy(pos_in, pos, load_sem.at[9])
    abias_copy = Copy(abias_in, abias.at[1], weight_send.at[8], weight_recv.at[8], sibling)
    ebias_copy = Copy(ebias_in, ebias.at[1], weight_send.at[9], weight_recv.at[9], sibling)
    proj_load.start()
    pos_load.start()
    own_loads[0].start()

    @pl.when(place.has_out)
    def _():
        pl.semaphore_wait(barrier, 6)

    @pl.when(jnp.logical_not(place.has_out))
    def _():
        pl.semaphore_wait(barrier, 5)

    send_rows(0)
    send_rows(2)
    sib_loads[0].start()
    abias_copy.start()
    ebias_copy.start()
    abias[0] = abias_in[...]
    ebias[0] = ebias_in[...]

    def need(k):
        own_loads[k].wait()
        sib_loads[k].wait_recv()

    def note(row, values):
        small[row : row + 1, :] += column_sums(values)

    def param(ref, layer, row):
        return ref[layer, row : row + 1, :].astype(F32)

    def y_copy(index, slot, rows):
        return Copy(
            give.at[slot, rows], take.at[slot, rows], y_send.at[index[0], index[1]], y_recv.at[index[0], index[1]], partner
        )

    def offer(exchange, slot, ch, values):
        rows = span(ch, local)
        give[slot, rows, :] = values.astype(BF)
        y_copy((exchange, ch), slot, rows).start()

    def collect(exchange, slot, ch):
        rows = span(ch, local)
        y_copy((exchange, ch), slot, rows).wait()
        return give[slot, rows, :].astype(F32) + take[slot, rows, :].astype(F32)

    def head_mask(rows, h):
        lane = lax.broadcasted_iota(jnp.int32, (rows, cols), 1)
        return (lane >= h * HD) & (lane < (h + 1) * HD)

    place_col = lax.broadcasted_iota(jnp.int32, (seq, slots_in.shape[1]), 0)
    slot_row = slots_in[pl.ds(c, 1), :]
    masked = jnp.max(jnp.where(place_col == slot_row, 1.0, 0.0).astype(F32), axis=1, keepdims=True)
    wait_rows(0, rows_all, local)
    wait_rows(2, kinds_all, 1)
    for h in range(2):
        kinds = jnp.broadcast_to(jnp.where(kinds_all[h : h + 1, :] == 1, 1.0, 0.0), (128, 128)).astype(F32)
        flags[pl.ds(h * local, local), :] = kinds.T.astype(BF)
    proj_load.wait()
    pos_load.wait()
    wide_flags = jnp.concatenate([flags[...]] * (patch // 128), axis=1)
    patches = rows_all[...]
    kind_one = patches * wide_flags
    kind_zero = patches - kind_one
    is_one = flags[:, 0:1].astype(F32)
    lifted = nn(kind_zero, proj[0:patch, :]) + nn(kind_one, proj[patch : 2 * patch, :])
    offset = jnp.where(is_one > 0.5, offs_in[1:2, :].astype(F32), offs_in[0:1, :].astype(F32))
    stream[0] = jnp.where(masked > 0.5, plc_in[...].reshape(1, width).astype(F32), lifted + offset) + pos[...].astype(F32)

    def norm(layer, ch):
        rows = span(ch, local)
        hat, _ = hat_of(stream[layer, rows, :])
        first[layer, rows, :] = (hat * param(scales, layer, 0) + param(shifts, layer, 0)).astype(BF)

    def project(layer):
        rows = slice(None)

        def group(g):
            values = first[layer, rows, :]
            query = (nt(values, wa[layer, g, 0]) + abias[g, layer, 0:1, :].astype(F32)) * scale
            qkv[layer, g, 0, rows, :] = query.astype(BF)
            qkv[layer, g, 1, rows, :] = nt(values, wa[layer, g, 1]).astype(BF)
            qkv[layer, g, 2, rows, :] = (nt(values, wa[layer, g, 2]) + abias[g, layer, 1:2, :].astype(F32)).astype(BF)

        loop(2, group)

    def attend(layer):
        def chunk(ch):
            rows = span(ch, local)

            groups = []
            for g in range(2):
                total_mixed = 0.0
                query, key, value = qkv[layer, g, 0, rows, :], qkv[layer, g, 1], qkv[layer, g, 2]
                for h in range(heads):
                    scores = nt(jnp.where(head_mask(local, h), query, 0), key)
                    raised = jnp.exp(scores - jnp.max(scores, axis=-1, keepdims=True))
                    prob = (raised / jnp.sum(raised, axis=-1, keepdims=True)).astype(BF)
                    probs[layer, g * heads + h, rows, :] = prob
                    total_mixed += nn(prob, jnp.where(head_mask(seq, h), value, 0))
                groups.append(total_mixed.astype(BF))
            together = jnp.concatenate(groups, axis=1)
            mixed[layer, rows, :] = together
            offer(2 * layer, 0, ch, nn(together, wc[layer]))

        loop(chunks, chunk)

    def to_middle(layer, ch):
        rows = span(ch, local)
        values = stream[layer, rows, :] + collect(2 * layer, 0, ch) + cbias[layer : layer + 1, :].astype(F32)
        middle[layer, rows, :] = values
        hat, _ = hat_of(values)
        second[layer, rows, :] = (hat * param(scales, layer, 1) + param(shifts, layer, 1)).astype(BF)

    def activate(layer, g, rows):
        value = nn(second[layer, rows, :], we[layer, g]) + ebias[g, layer : layer + 1, :].astype(F32)
        cdf = 0.5 * (1.0 + lax.erf(value * (0.5**0.5)))
        hidden[layer, g, rows, :] = (value * cdf).astype(BF)
        density = jnp.exp(-0.5 * value * value) * 0.3989422804014327
        slope[layer, g, rows, :] = (cdf + value * density).astype(BF)

    def feed_back(layer, g, rows):
        grad_hidden = nt(out_round[rows, :], wr[layer, g])
        grad_pre = grad_hidden * slope[layer, g, rows, :].astype(F32)
        bias_rows[layer, g, 0:1, :] += column_sums(grad_pre)
        pre[g, rows, :] = grad_pre.astype(BF)

    def settle(row, layer, part, base, values, gain_row):
        hat, inverse = hat_of(base)
        note(2 * layer + part, values * hat)
        note(4 + 2 * layer + part, values)
        scaled = values * param(scales, layer, part)
        inner = scaled - jnp.mean(scaled, axis=-1, keepdims=True)
        return inverse * (inner - hat * jnp.mean(scaled * hat, axis=-1, keepdims=True))

    for own, sib in zip(own_loads[1:], sib_loads[1:]):
        own.start()
        sib.start()
    small[...] = jnp.zeros_like(small)
    bias_rows[...] = jnp.zeros_like(bias_rows)

    need(0)
    abias_copy.wait_recv()
    ebias_copy.wait_recv()
    for ch in range(2):
        norm(0, ch)
    project(0)
    for layer in range(layers):
        need(4 * layer + 1)
        attend(layer)
        need(4 * layer + 2)
        need(4 * layer + 3)
        if layer + 1 < layers:

            def chunk(ch):
                rows = span(ch, local)
                to_middle(layer, ch)

                part = 0.0
                for g in range(2):
                    activate(layer, g, rows)
                    part += nn(hidden[layer, g, rows, :], wr[layer, g])
                offer(2 * layer + 1, 1, ch, part)

            loop(chunks, chunk)
            if layer == 0:
                send_rows(1)
            need(4 * layer + 4)

            def after(ch):
                rows = span(ch, local)
                stream[layer + 1, rows, :] = (
                    middle[layer, rows, :] + collect(2 * layer + 1, 1, ch) + rbias[layer : layer + 1, :].astype(F32)
                )
                norm(layer + 1, ch)

            loop(chunks, after)
            project(layer + 1)

    last = layers - 1
    pieces = []
    at = 0
    cut = hid // 4
    spots = [(hid + k * cut if k < 4 else (k - 4) * cut, cut) for k in range(8)]
    spots += [(2 * hid + j * cols, cols) for j in range(3)] + [(2 * hid + 3 * cols, cols + 32)]
    per_layer = len(spots)
    for layer in reversed(range(layers)):
        for row, count in spots:
            k = len(pieces)
            kind = kind_of(k, wide_count)
            piece = kind(
                place,
                total.at[layer],
                row,
                count,
                ring,
                at,
                sums_out.at[layer],
                ring_send.at[k],
                ring_recv.at[k],
                store_sem.at[k],
            )
            pieces.append((piece, layer, row, count))
            at += kind.space(count)

    shares = []
    for layer in reversed(range(layers)):
        for batch, (row, size, count) in enumerate(
            ((hid, hid // 2, 2), (0, hid // 2, 2), (2 * hid, 3 * cols, 1), (2 * hid + 3 * cols, cols + 32, 1))
        ):
            shares.append((len(shares), layer, min(batch, 2), row, size, count))

    def share_copy(share, u):
        k, layer, batch, row, size, _ = share
        slot = ((last - layer) * 3 + batch) % 2
        start = row - (hid, 0, 2 * hid)[batch] + u * size
        return Copy(
            send_part.at[slot, pl.ds(start, size)],
            recv_part.at[pl.ds(row + u * size, size)],
            part_send.at[k, u],
            part_recv.at[k, u],
            sibling,
        )

    def free_slot(layer, batch):
        old = (last - layer) * 3 + batch - 2
        for share in shares:
            if (last - share[1]) * 3 + share[2] == old:
                for u in range(share[5]):
                    share_copy(share, u).wait_send()

    def join(share, u):
        k, layer, _, row, size, _ = share
        share_copy(share, u).wait_recv()
        start = row + u * size
        add_into(total.at[layer], start, recv_part, start, size)
        if k == 3:
            pl.semaphore_signal(credit, 1, device_id=sibling, device_id_type=MESH)
        for piece, owner, spot, _ in pieces:
            if owner == layer and start <= spot < start + size:
                piece.stages[0]()
                tick()

    ticks = iter(TICKS)

    def tick():
        for k, stage in next(ticks):
            stages = (pieces[k][0] if k < len(pieces) else shared_piece[0]).stages
            if stage < len(stages):
                stages[stage]()

    shared_piece = []

    def feed_grads(layer, batch):
        share = shares[4 * (last - layer) + batch]
        row = share[3]
        slot = ((last - layer) * 3 + batch) % 2
        free_slot(layer, batch)
        if layer < last and batch == 0:
            pl.semaphore_wait(credit, 1)

        def half(u):
            def block(t):
                lanes = pl.ds(pl.multiple_of((u * (hid // 256) + t) * 128, 128), 128)
                into = pl.ds(pl.multiple_of((u * (hid // 256) + t) * 128, 128), 128)
                for g in (1, 0):
                    if batch == 0:
                        values = tn(hidden[layer, g, :, lanes], out_round[...])
                    else:
                        values = tn(second[layer, :, lanes], pre[g])
                    if g == 1:
                        send_part[slot, into, :] = values.astype(BF)
                    else:
                        total[layer, pl.ds(row + into.start, 128), :] = values.astype(BF)

            rolled(hid // 256, block)
            share_copy(share, u).start()

        rolled(2, half)
        for u in range(2):
            join(share, u)

    def attention_grads(layer):
        three, one = shares[4 * (last - layer) + 2], shares[4 * (last - layer) + 3]
        slot = ((last - layer) * 3 + 2) % 2
        row = 2 * hid
        free_slot(layer, 2)

        def block(j):
            into = pl.ds(pl.multiple_of(j * cols, 16), cols)
            send_part[slot, into, :] = tn(grad_qkv[1, j], first[layer]).astype(BF)
            total[layer, pl.ds(row + into.start, cols), :] = tn(grad_qkv[0, j], first[layer]).astype(BF)

        rolled(3, block)
        share_copy(three, 0).start()
        both = tn(mixed[layer], mid_round[...])
        send_part[slot, pl.ds(3 * cols, cols), :] = both[cols:].astype(BF)
        send_part[slot, pl.ds(4 * cols, 32), :] = bias_rows[layer, 1].astype(BF)
        share_copy(one, 0).start()
        total[layer, pl.ds(row + 3 * cols, cols), :] = both[:cols].astype(BF)
        total[layer, pl.ds(row + 4 * cols, 32), :] = bias_rows[layer, 0].astype(BF)
        join(three, 0)
        join(one, 0)

    wait_rows(1, cot, local)

    def start_back(ch):
        rows = span(ch, local)
        grad[rows, :] = cot[rows, :].astype(F32)

    loop(chunks, start_back)

    def top_send():
        return Copy(top_other, top_own, last_send.at[0], last_recv.at[0], sibling)

    top_copy = Copy(give.at[2], take_top, last_send.at[1], last_recv.at[1], partner)

    for layer in reversed(range(layers)):
        exchange = 4 + 2 * (last - layer)

        def chunk(ch):
            rows = span(ch, local)
            note(10 + layer, grad[rows, :])
            out_round[rows, :] = grad[rows, :].astype(BF)
            if layer == last:
                to_middle(layer, ch)
                loop(2, lambda g: activate(layer, g, rows))
            part = 0.0
            for g in range(2):
                feed_back(layer, g, rows)
                part += nt(pre[g, rows, :], we[layer, g])
            offer(exchange, 1, ch, part)

        loop(chunks, chunk)
        tick()

        if layer == last:

            def top(ch):
                rows = span(ch, local)
                give[2, rows, :] = (
                    nn(hidden[layer, 0, rows, :], wr[layer, 0]) + nn(hidden[layer, 1, rows, :], wr[layer, 1])
                ).astype(BF)

            loop(chunks, top)

            @pl.when(jnp.logical_not(diagonal))
            def _():
                top_copy.start()

        feed_grads(layer, 0)
        feed_grads(layer, 1)

        def chunk(ch):
            rows = span(ch, local)
            grad_second = collect(exchange, 1, ch)
            grad_middle = grad[rows, :] + settle(rows, layer, 1, middle[layer, rows, :], grad_second, None)
            note(8 + layer, grad_middle)
            grad[rows, :] = grad_middle
            mid_round[rows, :] = grad_middle.astype(BF)

            def group(g):
                mixed_back = nt(mid_round[rows, :], wc[layer, span(g, cols), :]).astype(BF)
                query, key, value = qkv[layer, g, 0, rows, :], qkv[layer, g, 1], qkv[layer, g, 2]
                query_acc, key_sum, value_sum = 0.0, 0.0, 0.0
                for h in range(heads):
                    prob = probs[layer, g * heads + h, rows, :]
                    back = jnp.where(head_mask(local, h), mixed_back, 0)
                    grad_probs = nt(back, value)
                    value_sum += tn(prob, back)
                    weight = prob.astype(F32)
                    center = jnp.sum(weight * grad_probs, axis=-1, keepdims=True)
                    grad_scores = (weight * (grad_probs - center)).astype(BF)
                    query_acc += nn(grad_scores, jnp.where(head_mask(seq, h), key, 0))
                    key_sum += tn(grad_scores, jnp.where(head_mask(local, h), query, 0))
                grad_query = (query_acc.astype(BF).astype(F32) * scale).astype(BF)
                grad_qkv[g, 0, rows, :] = grad_query
                bias_rows[layer, g, 1:2, 0:cols] += column_sums(grad_query.astype(F32))

                if ch == 0:
                    key_acc[g, 0] = key_sum
                    key_acc[g, 1] = value_sum
                else:
                    key_acc[g, 0] += key_sum
                    key_acc[g, 1] += value_sum

            loop(2, group)

        loop(chunks, chunk)
        tick()

        def close(g):
            grad_qkv[g, 1] = key_acc[g, 0].astype(BF)
            grad_value = key_acc[g, 1].astype(BF)
            grad_qkv[g, 2] = grad_value
            bias_rows[layer, g, 2:3, 0:cols] += column_sums(grad_value.astype(F32))

        loop(2, close)

        def chunk(ch):
            rows = span(ch, local)

            part = 0.0
            for g in range(2):
                for j in range(3):
                    part += nn(grad_qkv[g, j, rows, :], wa[layer, g, j])
            offer(exchange + 1, 0, ch, part)

        loop(chunks, chunk)
        tick()
        attention_grads(layer)

        if layer == last:

            @pl.when(jnp.logical_not(diagonal))
            def _():
                top_copy.wait_send()

            @pl.when(diagonal)
            def _():
                top_copy.wait_recv()

                def finish_top(dst, half):
                    rows = span(half, local)
                    dst[...] = (
                        middle[layer, rows, :]
                        + (give[2, rows, :].astype(F32) + take_top[rows, :].astype(F32))
                        + rbias[layer : layer + 1, :].astype(F32)
                    )

                finish_top(top_other, 1 - c)
                top_send().start()
                finish_top(top_own, c)

        def chunk(ch):
            rows = span(ch, local)
            grad_first = collect(exchange + 1, 0, ch)
            grad[rows, :] += settle(rows, layer, 0, stream[layer, rows, :], grad_first, None)

        loop(chunks, chunk)
        tick()

    lifted_grad = jnp.where(masked > 0.5, 0.0, grad[...])
    note(14, grad[...] - lifted_grad)
    one_grad = jnp.where(is_one > 0.5, lifted_grad, 0.0)
    note(12, lifted_grad - one_grad)
    note(13, one_grad)
    lifted_round = lifted_grad.astype(BF)
    shared_rows = shared.shape[0]
    half_rows = shared_rows // 2
    flag_side = jnp.where(y == 1, wide_flags.astype(F32), 1.0 - wide_flags.astype(F32)).astype(BF)
    shared[0:patch, :] = tn(rows_all[...] * flag_side, lifted_round).astype(BF)
    shared[patch : patch + local, :] = grad[span(y, local), :].astype(BF)
    shared[patch + local : shared_rows, :] = small[...].astype(BF)
    keep_row, give_row = span(c, half_rows), span(1 - c, half_rows)
    shared_part = Copy(
        shared.at[give_row], shared_buf.at[pl.ds(0, half_rows)], last_send.at[2], last_recv.at[2], sibling
    )
    shared_part.start()

    patch_copy = Copy(patch_other, patch_own, last_send.at[3], last_recv.at[3], sibling)

    @pl.when(diagonal)
    def _():
        def half_back(dst, half):
            rows = span(half, local)
            flag = flags[rows, :].astype(F32)[:, 0:1]
            masks = jnp.max(
                jnp.where(
                    lax.broadcasted_iota(jnp.int32, (local, slots_in.shape[1]), 0) + half * local == slot_row, 1.0, 0.0
                ).astype(F32),
                axis=1,
                keepdims=True,
            )
            values = jnp.where(masks > 0.5, 0.0, grad[rows, :]).astype(BF)
            dst[...] = jnp.where(flag > 0.5, nt(values, proj[patch : 2 * patch, :]), nt(values, proj[0:patch, :]))

        half_back(patch_other, 1 - c)
        patch_copy.start()
        half_back(patch_own, c)

    shared_part.wait()
    add_into(shared, pl.multiple_of(c * half_rows, 16), shared_buf, 0, half_rows)
    sum_shared = PairFirst(
        place,
        shared,
        pl.multiple_of(c * half_rows, 16),
        half_rows,
        shared_buf,
        half_rows,
        shared_out.at[y],
        shared_send,
        shared_recv,
        store_sem.at[len(pieces)],
    )
    across = Copy(shared_out.at[y, keep_row], shared_out.at[y, keep_row], last_send.at[4], last_recv.at[4], partner)
    across_back = Copy(
        shared_out.at[1 - y, keep_row], shared_out.at[1 - y, keep_row], last_send.at[4], last_recv.at[4], partner
    )
    ends = []
    for k in range(2):
        ends.append(
            (
                Copy(
                    shared_out.at[k, keep_row], shared_out.at[k, keep_row], last_send.at[5 + k], last_recv.at[5 + k], sibling
                ),
                Copy(
                    shared_out.at[k, give_row], shared_out.at[k, give_row], last_send.at[5 + k], last_recv.at[5 + k], sibling
                ),
            )
        )

    def to_partner():
        sum_shared.s5()
        across.start()

    def to_sibling():
        across.wait_send()
        across_back.wait_recv()
        for out, _ in ends:
            out.start()

    def close_shared():
        for out, back in ends:
            out.wait_send()
            back.wait_recv()

    sum_shared.stages = sum_shared.stages[:5] + [to_partner, to_sibling, close_shared]
    shared_piece.append(sum_shared)
    sum_shared.s0()
    tick()
    tick()
    count = len(pieces)

    @pl.when(diagonal)
    def _():
        top_send().wait_send()
        patch_copy.wait_send()

    @pl.when(jnp.logical_not(diagonal))
    def _():
        top_send().wait_recv()
        patch_copy.wait_recv()

    finals = (
        pltpu.make_async_copy(top_own, encoded_out, store_sem.at[count + 1]),
        pltpu.make_async_copy(patch_own, patches_out, store_sem.at[count + 2]),
    )
    for copy in finals:
        copy.start()
    for copy in finals:
        copy.wait()

    for to_far, to_near, _ in row_copies:
        to_far.wait_send()

        @pl.when(jnp.logical_not(diagonal))
        def _():
            to_near.wait_send()

    for copy in sib_loads + [abias_copy, ebias_copy]:
        copy.wait_send()
    free_slot(-1, 0)
    free_slot(-1, 1)


def per_device(
    wide_count,
    patches,
    token_kind,
    mask_slots,
    projector,
    offsets,
    placeholder,
    positions,
    scales,
    shifts,
    attention,
    attn_bias,
    combiner,
    comb_bias,
    expander,
    expand_bias,
    reducer,
    reduce_bias,
    cotangent,
):
    local, patch = patches.shape
    seq, width = positions.shape
    layers = scales.shape[0]
    cols = attention.shape[3]
    heads = cols // HD
    hid = expander.shape[2]
    per_layer = 2 * hid + 4 * cols + 32
    shared_rows = patch + local + 64
    pieces = 12 * layers
    counts = ([hid // 4] * 8 + [cols] * 3 + [cols + 32]) * layers
    ring_rows = sum(kind_of(k, wide_count).space(count) for k, count in enumerate(counts))
    vmem = pl.BlockSpec(memory_space=pltpu.VMEM)
    anyw = pl.BlockSpec(memory_space=pl.ANY)
    dma = pltpu.SemaphoreType.DMA
    scratch = [
        pltpu.VMEM((layers, 2, 3, cols, width), BF),
        pltpu.VMEM((layers, 2 * cols, width), BF),
        pltpu.VMEM((layers, 2, width, hid), BF),
        pltpu.VMEM((layers, 2, hid, width), BF),
        pltpu.VMEM((2, layers, 2, cols), BF),
        pltpu.VMEM((2, layers, hid), BF),
        pltpu.VMEM((2 * patch, width), BF),
        pltpu.VMEM((seq, width), BF),
        pltpu.VMEM((seq, patch), BF),
        pltpu.VMEM((2, local), jnp.int32),
        pltpu.VMEM((seq, 128), BF),
        pltpu.VMEM((seq, width), F32),
        pltpu.VMEM((layers, seq, width), F32),
        pltpu.VMEM((layers, seq, width), F32),
        pltpu.VMEM((layers, seq, width), BF),
        pltpu.VMEM((layers, seq, width), BF),
        pltpu.VMEM((layers, 2, 3, seq, cols), BF),
        pltpu.VMEM((layers, 2 * heads, seq, seq), BF),
        pltpu.VMEM((layers, seq, 2 * cols), BF),
        pltpu.VMEM((layers, 2, seq, hid), BF),
        pltpu.VMEM((layers, 2, seq, hid), BF),
        pltpu.VMEM((seq, width), BF),
        pltpu.VMEM((2, seq, hid), BF),
        pltpu.VMEM((seq, width), BF),
        pltpu.VMEM((2, 3, seq, cols), BF),
        pltpu.VMEM((2, 2, seq, cols), F32),
        pltpu.VMEM((3, seq, width), BF),
        pltpu.VMEM((2, seq, width), BF),
        pltpu.VMEM((seq, width), BF),
        pltpu.VMEM((seq, width), BF),
        pltpu.VMEM((2, 4 * cols + 32, width), BF),
        pltpu.VMEM((per_layer, width), BF),
        pltpu.VMEM((layers, per_layer, width), BF),
        pltpu.VMEM((ring_rows, width), BF),
        pltpu.VMEM((shared_rows, width), BF),
        pltpu.VMEM((shared_rows // 2 + 3 * (shared_rows // 4), width), BF),
        pltpu.VMEM((local, width), F32),
        pltpu.VMEM((local, width), F32),
        pltpu.VMEM((local, patch), F32),
        pltpu.VMEM((local, patch), F32),
        pltpu.VMEM((64, width), F32),
        pltpu.VMEM((layers, 2, 32, width), F32),
        dma((10,)),
        dma((10,)),
        dma((10,)),
        dma((3, 2)),
        dma((3, 2)),
        dma((8, 2)),
        dma((8, 2)),
        dma((4 * layers, 2)),
        dma((4 * layers, 2)),
        dma((pieces, 11)),
        dma((pieces, 7)),
        dma((5,)),
        dma((5,)),
        dma((7,)),
        dma((7,)),
        dma((pieces + 3,)),
        pltpu.SemaphoreType.REGULAR,
    ]
    sums, shared, encoded, grad_patches = pl.pallas_call(
        functools.partial(encoder, wide_count),
        out_shape=(
            jax.ShapeDtypeStruct((layers, per_layer, width), BF),
            jax.ShapeDtypeStruct((2, shared_rows, width), BF),
            jax.ShapeDtypeStruct((local, width), F32),
            jax.ShapeDtypeStruct((local, patch), F32),
        ),
        in_specs=[anyw, vmem, anyw, vmem, anyw, vmem, vmem, anyw, vmem, vmem, anyw, vmem, anyw, vmem, anyw, vmem, anyw, vmem],
        out_specs=(anyw, anyw, anyw, anyw),
        scratch_shapes=scratch,
        compiler_params=pltpu.CompilerParams(
            collective_id=0, has_side_effects=True, vmem_limit_bytes=63 * 1024 * 1024 + 512 * 1024
        ),
        name="encoder",
    )(
        patches,
        token_kind.reshape(1, local),
        cotangent,
        mask_slots,
        projector.reshape(2 * patch, width),
        offsets,
        placeholder,
        positions,
        scales,
        shifts,
        attention.transpose(0, 1, 3, 2),
        attn_bias,
        combiner,
        comb_bias,
        expander,
        expand_bias,
        reducer,
        reduce_bias,
    )
    f32 = functools.partial(jax.ShapeDtypeStruct, dtype=F32)
    finished = pl.pallas_call(
        widen,
        out_shape=(
            f32((local, width)),
            f32((local, patch)),
            f32((2, patch, width)),
            f32((2, width)),
            f32((width,)),
            f32((seq, width)),
            f32((layers, 2, width)),
            f32((layers, 2, width)),
            f32((layers, 3, cols, width)),
            f32((layers, 2, cols)),
            f32((layers, cols, width)),
            f32((layers, width)),
            f32((layers, width, hid)),
            f32((layers, hid)),
            f32((layers, hid, width)),
            f32((layers, width)),
        ),
        in_specs=[anyw] * 4,
        out_specs=[anyw, anyw, anyw, vmem, vmem, anyw, vmem, vmem, anyw, vmem, anyw, vmem, anyw, vmem, anyw, vmem],
        scratch_shapes=[
            pltpu.VMEM((layers, per_layer, width), BF),
            pltpu.VMEM((layers, per_layer - 32, width), F32),
            pltpu.VMEM((2, shared_rows, width), BF),
            pltpu.VMEM((2, patch + local, width), F32),
            pltpu.VMEM((local, width), F32),
            pltpu.VMEM((local, patch), F32),
            dma((layers, 8)),
            dma((layers, 8)),
            dma((2,)),
            dma((2, 2)),
            dma((2, 2)),
        ],
        compiler_params=pltpu.CompilerParams(vmem_limit_bytes=62 * 1024 * 1024),
        name="widen",
    )(sums, shared, encoded, grad_patches)
    return tuple(item.transpose(0, 1, 3, 2) if k == 8 else item for k, item in enumerate(finished))


def widen(
    sums,
    shared,
    encoded,
    grad_patches,
    encoded_out,
    patches_out,
    projector,
    offsets,
    placeholder,
    positions,
    scales,
    shifts,
    attention,
    attn_bias,
    combiner,
    comb_bias,
    expander,
    expand_bias,
    reducer,
    reduce_bias,
    sums_in,
    sums_wide,
    shared_in,
    shared_wide,
    encoded_held,
    patches_held,
    load_sem,
    store_sem,
    shared_sem,
    shared_store,
    through_sem,
):
    layers, width, hid = expander.shape
    cols = combiner.shape[1]
    patch = projector.shape[1]
    local = encoded.shape[0]
    through = [
        (pltpu.make_async_copy(src, held, through_sem.at[k, 0]), pltpu.make_async_copy(held, dst, through_sem.at[k, 1]))
        for k, (src, held, dst) in enumerate(
            ((encoded, encoded_held, encoded_out), (grad_patches, patches_held, patches_out))
        )
    ]
    half = hid // 2
    cuts = []
    for k, array in enumerate((expander, reducer)):
        cuts += [(k * hid + u * half, half, array, u) for u in range(2)]
    cuts += [(2 * hid + j * cols, cols, attention, j) for j in range(3)]
    cuts.append((2 * hid + 3 * cols, sums.shape[1] - 3 * cols - 2 * hid, combiner, 0))
    loads = []
    for layer in range(layers):
        for k, (row, count, _, _) in enumerate(cuts):
            spot = (layer, pl.ds(row, count))
            loads.append(pltpu.make_async_copy(sums.at[spot], sums_in.at[spot], load_sem.at[layer, k]))
    shared_loads = [pltpu.make_async_copy(shared.at[k], shared_in.at[k], shared_sem.at[k]) for k in range(2)]
    for copy in loads + shared_loads + [load for load, _ in through]:
        copy.start()
    stores = []

    def convert(src, dst, row, count):
        def step(t):
            rows = pl.ds(pl.multiple_of(row + t * 64, 64), 64)
            dst[rows, :] = src[rows, :].astype(F32)

        rolled(count // 64, step)

    for layer in range(layers):
        for k, (row, count, array, u) in enumerate(cuts):
            loads[layer * len(cuts) + k].wait()
            wide = min(count, sums_wide.shape[1] - row)
            convert(sums_in.at[layer], sums_wide.at[layer], row, wide)
            target = array.at[layer, u] if array is attention else array.at[layer, pl.ds(u * half, wide)]
            copy = pltpu.make_async_copy(sums_wide.at[layer, pl.ds(row, wide)], target, store_sem.at[layer, k])
            copy.start()
            stores.append(copy)
        bias = sums_in[layer, pl.ds(2 * hid + 4 * cols, 16), :].astype(F32)
        expand_bias[layer : layer + 1, :] = bias[0:1, :]
        attn_bias[layer, 0:1, :] = bias[1:2, :cols]
        attn_bias[layer, 1:2, :] = bias[2:3, :cols]
    for k in range(2):
        shared_loads[k].wait()
        convert(shared_in.at[k], shared_wide.at[k], 0, patch + local)
        for target, start, size, sem in (
            (projector.at[k], 0, patch, 0),
            (positions.at[pl.ds(k * local, local)], patch, local, 1),
        ):
            copy = pltpu.make_async_copy(shared_wide.at[k, pl.ds(start, size)], target, shared_store.at[k, sem])
            copy.start()
            stores.append(copy)
    for load, store in through:
        load.wait()
        store.start()
    small = shared_in[0, pl.ds(patch + local, 16), :].astype(F32)
    for layer in range(layers):
        scales[layer] = small[2 * layer : 2 * layer + 2, :]
        shifts[layer] = small[4 + 2 * layer : 6 + 2 * layer, :]
    comb_bias[...] = small[8:10, :]
    reduce_bias[...] = small[10:12, :]
    offsets[...] = small[12:14, :]
    placeholder[...] = small[14:15, :].reshape(width)
    for copy in stores + [store for _, store in through]:
        copy.wait()


def solution(mesh):
    rows = ("wide", "narrow")
    return jax.shard_map(
        functools.partial(per_device, mesh.shape["wide"]),
        mesh=mesh,
        in_specs=(
            P(rows, None),
            P(rows),
            P("wide", None),
            P(),
            P(),
            P(),
            P(),
            P(),
            P(),
            P(None, None, None, "narrow"),
            P(None, None, "narrow"),
            P(None, "narrow", None),
            P(),
            P(None, None, "narrow"),
            P(None, "narrow"),
            P(None, "narrow", None),
            P(),
            P(rows, None),
        ),
        out_specs=(
            P(rows, None),
            P(rows, None),
            P(),
            P(),
            P(),
            P(),
            P(),
            P(),
            P(None, None, None, "narrow"),
            P(None, None, "narrow"),
            P(None, "narrow", None),
            P(),
            P(None, None, "narrow"),
            P(None, "narrow"),
            P(None, "narrow", None),
            P(),
        ),
        check_vma=False,
    )
```

```python
import functools

import jax
import jax.numpy as jnp
from jax import lax
from jax.experimental import pallas as pl
from jax.experimental.pallas import tpu as pltpu
from jax.sharding import PartitionSpec as P

HD = 64
EPS = 1e-06
BF = jnp.bfloat16
F32 = jnp.float32
MESH = pl.DeviceIdType.MESH


def nn(left, right):
    return jnp.dot(left, right, preferred_element_type=F32)


def nt(left, right):
    return lax.dot_general(left, right, (((1,), (1,)), ((), ())), preferred_element_type=F32)


def tn(left, right):
    return lax.dot_general(left, right, (((0,), (0,)), ((), ())), preferred_element_type=F32)


def rolled(count, body):
    def step(index, carry):
        body(index)
        return carry

    lax.fori_loop(0, count, step, 0)


def loop(count, body):
    for index in range(count):
        body(index)


def hat_of(values):
    center = values - jnp.mean(values, axis=-1, keepdims=True)
    variance = jnp.mean(center * center, axis=-1, keepdims=True)
    scale = lax.rsqrt(variance + EPS)
    return center * scale, scale


def column_sums(values):
    return jnp.sum(values, axis=0, keepdims=True)


class Copy:
    def __init__(self, src, dst, send, recv, target):
        self.args = dict(src_ref=src, dst_ref=dst, send_sem=send, recv_sem=recv, device_id=target, device_id_type=MESH)

    def start(self):
        pltpu.make_async_remote_copy(**self.args).start()

    def wait(self):
        pltpu.make_async_remote_copy(**self.args).wait()

    def wait_send(self):
        pltpu.make_async_remote_copy(**self.args).wait_send()

    def wait_recv(self):
        pltpu.make_async_remote_copy(**self.args).wait_recv()


def add_into(dst, dst_row, src, src_row, rows):
    block = next(b for b in (48, 32, 16) if rows % b == 0)

    def step(index):
        into = pl.ds(pl.multiple_of(dst_row + index * block, 16), block)
        give = pl.ds(pl.multiple_of(src_row + index * block, 16), block)
        dst[into, :] = (dst[into, :].astype(F32) + src[give, :].astype(F32)).astype(BF)

    rolled(rows // block, step)


class Place:
    def __init__(self, wide_count):
        self.w = lax.axis_index("wide")
        self.n = lax.axis_index("narrow")
        self.y = self.n // 2
        self.c = self.n % 2
        self.x = self.w % 2
        self.z = self.w // 2
        line = wide_count // 2
        self.half = line // 2
        self.low = self.z < self.half
        self.side = jnp.where(self.low, 0, 1)
        self.depth = jnp.where(self.low, self.z, line - 1 - self.z)
        step = jnp.where(self.low, 2, -2)
        self.sibling = (self.w, self.n + 1 - 2 * self.c)
        self.partner = (self.w, self.n + 2 - 4 * self.y)
        self.pair = (self.w + 1 - 2 * self.x, self.n)
        self.inward = (self.w + step, self.n)
        self.outward = (self.w - jnp.where(self.depth > 0, step, -step), self.n)
        self.has_out = self.depth > 0
        self.inner = self.depth == self.half - 1


def hops(count, hop):
    if count == 1:
        hop(0)
    elif count > 1:
        rolled(count, hop)


class PairFirst:
    @staticmethod
    def space(rows):
        return rows // 2 * 3

    def __init__(self, place, total, row, rows, buf, at, out, send, recv, store):
        self.place, self.total, self.buf = place, total, buf
        half = rows // 2
        self.half, self.at = half, at
        mine = pl.multiple_of(row + place.x * half, 16)
        other = pl.multiple_of(row + (1 - place.x) * half, 16)
        self.mine = mine
        keep, give = total.at[pl.ds(mine, half)], total.at[pl.ds(other, half)]
        out_keep, out_give = out.at[pl.ds(mine, half)], out.at[pl.ds(other, half)]
        slots = [buf.at[pl.ds(at + k * half, half)] for k in range(3)]
        self.pair_in = Copy(give, slots[0], send.at[0], recv.at[0], place.pair)
        self.line_in = Copy(keep, slots[1], send.at[1], recv.at[1], place.inward)
        self.middle = Copy(keep, slots[2], send.at[2], recv.at[2], place.inward)
        self.line_out = Copy(keep, out_keep, send.at[3], recv.at[3], place.outward)
        self.line_on = Copy(out_keep, out_keep, send.at[3], recv.at[3], place.outward)
        self.pair_out = Copy(keep, out_keep, send.at[4], recv.at[4], place.pair)
        self.pair_on = Copy(out_keep, out_keep, send.at[4], recv.at[4], place.pair)
        self.other = Copy(out_give, out_give, send.at[4], recv.at[4], place.pair)
        self.store = pltpu.make_async_copy(keep, out_keep, store)
        self.stages = [self.s0, self.s1, self.s2, self.s3, self.s4, self.s5]

    def s0(self):
        self.pair_in.start()

    def s1(self):
        place = self.place
        self.pair_in.wait()
        add_into(self.total, self.mine, self.buf, self.at, self.half)
        if place.half == 1:
            self.middle.start()
            return

        @pl.when(place.depth == 0)
        def _():
            self.line_in.start()

    def s2(self):
        place = self.place

        def hop(k):
            @pl.when(place.depth == k + 1)
            def _():
                self.line_in.wait_recv()
                add_into(self.total, self.mine, self.buf, self.at + self.half, self.half)

            @pl.when((place.depth == k + 1) & jnp.logical_not(place.inner))
            def _():
                self.line_in.start()

        hops(place.half - 1, hop)
        if place.half > 1:

            @pl.when(place.inner)
            def _():
                self.middle.start()

    def s3(self):
        place = self.place

        @pl.when(place.inner)
        def _():
            self.middle.wait()
            add_into(self.total, self.mine, self.buf, self.at + 2 * self.half, self.half)
            if place.half > 1:
                self.line_out.start()
            self.pair_out.start()
            self.store.start()

    def s4(self):
        place = self.place

        def hop(k):
            @pl.when(place.depth == place.half - 2 - k)
            def _():
                self.line_on.wait_recv()
                self.pair_on.start()

            @pl.when((place.depth == place.half - 2 - k) & place.has_out)
            def _():
                self.line_on.start()

        hops(place.half - 1, hop)

    def s5(self):
        place = self.place

        @pl.when(place.inner)
        def _():
            self.store.wait()

        if place.half > 1:

            @pl.when(jnp.logical_not(place.inner))
            def _():
                self.line_in.wait_send()

            @pl.when(place.has_out)
            def _():
                self.line_out.wait_send()

        self.pair_out.wait_send()
        self.other.wait_recv()


class LineScatter:
    @staticmethod
    def space(rows):
        return rows // 4 * 7

    def __init__(self, place, total, row, rows, buf, at, out, send, recv, store):
        quarter = rows // 4
        self.place, self.total, self.row, self.quarter = place, total, row, quarter
        self.buf, self.at = buf, at
        mine = pl.multiple_of(row + place.z * quarter, 16)
        self.mine = mine
        low, high = (place.w - 2, place.n), (place.w + 2, place.n)

        def own(start, stop):
            return total.at[pl.ds(row + start * quarter, (stop - start) * quarter)]

        def slot(start, count):
            return buf.at[pl.ds(at + start * quarter, count * quarter)]

        self.up = [Copy(own(z + 1, 4), slot(z, 3 - z), send.at[0], recv.at[0], high) for z in range(3)]
        self.down = [Copy(own(0, z), slot(3, z), send.at[1], recv.at[1], low) for z in range(4)]
        keep, land = total.at[pl.ds(mine, quarter)], out.at[pl.ds(mine, quarter)]
        self.across = Copy(keep, slot(6, 1), send.at[2], recv.at[2], place.pair)
        self.store = pltpu.make_async_copy(keep, land, store)

        def spread(src, dst, k, target, way):
            return Copy(src, dst, send.at[3 + 4 * way + k], recv.at[3 + k], target)

        spots = [out.at[pl.ds(row + k * quarter, quarter)] for k in range(4)]
        self.first_up = [spread(own(k, k + 1), spots[k], k, high, 0) for k in range(4)]
        self.first_down = [spread(own(k, k + 1), spots[k], k, low, 1) for k in range(4)]
        self.on_up = [spread(spots[k], spots[k], k, high, 0) for k in range(4)]
        self.on_down = [spread(spots[k], spots[k], k, low, 1) for k in range(4)]
        self.stages = [self.s0, self.s1, self.s2, self.s3, self.s4, self.s5, self.s6, self.s7]

    def at_z(self, *works):
        for z, work in works:
            pl.when(self.place.z == z)(work)

    def take(self, copy, first, slot, count):
        copy.wait_recv()
        add_into(self.total, self.row + first * self.quarter, self.buf, self.at + slot * self.quarter, count * self.quarter)

    def s0(self):
        self.at_z((0, self.up[0].start), (3, self.down[3].start))

    def s1(self):
        def one():
            self.take(self.up[0], 1, 0, 3)
            self.up[1].start()

        def two():
            self.take(self.down[3], 0, 3, 3)
            self.down[2].start()

        self.at_z((1, one), (2, two))

    def s2(self):
        def one():
            self.take(self.down[2], 0, 3, 2)
            self.down[1].start()

        def two():
            self.take(self.up[1], 2, 1, 2)
            self.up[2].start()

        self.at_z((1, one), (2, two))

    def s3(self):
        self.at_z((0, lambda: self.take(self.down[1], 0, 3, 1)), (3, lambda: self.take(self.up[2], 3, 2, 1)))
        self.across.start()

    def s4(self):
        self.across.wait()
        add_into(self.total, self.mine, self.buf, self.at + 6 * self.quarter, self.quarter)
        self.store.start()

        def both(z):
            def work():
                self.first_up[z].start()
                self.first_down[z].start()

            return work

        self.at_z((0, self.first_up[0].start), (1, both(1)), (2, both(2)), (3, self.first_down[3].start))

    def s5(self):
        def one():
            self.on_up[0].wait_recv()
            self.on_up[0].start()
            self.on_down[2].wait_recv()
            self.on_down[2].start()

        def two():
            self.on_down[3].wait_recv()
            self.on_down[3].start()
            self.on_up[1].wait_recv()
            self.on_up[1].start()

        self.at_z((1, one), (2, two))

    def s6(self):
        def one():
            self.on_down[3].wait_recv()
            self.on_down[3].start()

        def two():
            self.on_up[0].wait_recv()
            self.on_up[0].start()

        self.at_z((1, one), (2, two))

    def s7(self):
        self.store.wait()

        def zero():
            for k in (1, 2, 3):
                self.on_down[k].wait_recv()
            for copy in (self.up[0], self.first_up[0]):
                copy.wait_send()

        def one():
            for copy in (self.up[1], self.down[1], self.first_up[1], self.on_up[0]):
                copy.wait_send()
            for copy in (self.first_down[1], self.on_down[2], self.on_down[3]):
                copy.wait_send()

        def two():
            for copy in (self.up[2], self.down[2], self.first_up[2], self.on_up[1], self.on_up[0]):
                copy.wait_send()
            for copy in (self.first_down[2], self.on_down[3]):
                copy.wait_send()

        def three():
            for k in (0, 1, 2):
                self.on_up[k].wait_recv()
            for copy in (self.down[3], self.first_down[3]):
                copy.wait_send()

        self.at_z((0, zero), (1, one), (2, two), (3, three))


KINDS = (PairFirst, LineScatter,)
PLAN = (1, 1, 0, 0, 0, 0, 0, 1, 1, 0, 0, 0, 0, 0, 0, 1, 0, 0, 0, 0, 1, 0, 1, 0)
TICKS = (
    (),
    (),
    (),
    (),
    (),
    (),
    (),
    (),
    (),
    ((0, 1),),
    ((1, 1), (2, 1)),
    (),
    (),
    ((5, 1),),
    ((4, 1), (7, 1), (2, 2), (1, 2), (3, 1), (0, 2)),
    (),
    ((8, 1), (0, 3), (1, 3), (5, 2), (2, 3)),
    ((10, 1), (8, 2), (0, 4), (6, 1), (4, 2)),
    ((1, 4),),
    ((7, 2),),
    ((5, 3), (3, 2), (8, 3), (10, 2)),
    ((7, 3), (4, 3), (13, 1)),
    (),
    (),
    ((11, 1), (5, 4), (9, 1), (1, 5), (3, 3), (0, 5), (6, 2)),
    ((15, 1), (10, 3), (14, 1)),
    ((6, 3), (7, 4), (11, 2)),
    ((0, 6), (2, 4), (13, 2), (3, 4), (16, 1)),
    ((15, 2),),
    ((10, 4), (1, 6)),
    ((9, 2),),
    ((8, 4),),
    ((11, 3), (13, 3), (12, 1), (19, 1), (20, 1), (1, 7), (7, 5), (14, 2), (9, 3), (7, 6), (22, 1), (16, 2), (4, 4), (20, 2), (0, 7), (8, 5), (12, 2), (9, 4), (14, 3), (16, 3), (23, 1), (11, 4), (19, 2), (24, 1), (15, 3), (18, 1), (13, 4), (8, 6), (4, 5), (2, 5), (20, 3), (12, 3), (24, 2), (21, 1), (22, 2), (16, 4), (14, 4), (8, 7), (19, 3), (22, 3), (23, 2), (9, 5), (17, 1), (24, 3), (6, 4), (5, 5), (11, 5), (18, 2), (23, 3), (21, 2), (16, 5), (14, 5), (17, 2), (15, 4), (10, 5), (18, 3), (21, 3), (19, 4), (24, 4), (23, 4), (20, 4), (15, 5), (17, 3), (22, 4), (20, 5), (24, 5), (6, 5), (22, 5), (21, 4), (3, 5), (18, 4), (20, 6), (7, 7), (13, 5), (22, 6), (12, 4), (17, 4), (15, 6), (23, 5), (20, 7), (24, 6), (19, 5), (12, 5), (21, 5), (22, 7), (18, 5), (24, 7), (15, 7), (17, 5)),
    (),
)


def kind_of(k, wide_count):
    return KINDS[PLAN[k]] if wide_count == 8 else PairFirst


def encoder(
    wide_count,
    patches_in,
    kinds_in,
    cot_in,
    slots_in,
    proj_in,
    offs_in,
    plc_in,
    pos_in,
    scales,
    shifts,
    att_in,
    abias_in,
    comb_in,
    cbias,
    exp_in,
    ebias_in,
    red_in,
    rbias,
    sums_out,
    shared_out,
    encoded_out,
    patches_out,
    wa,
    wc,
    we,
    wr,
    abias,
    ebias,
    proj,
    pos,
    rows_all,
    kinds_all,
    flags,
    grad,
    stream,
    middle,
    first,
    second,
    qkv,
    probs,
    mixed,
    slope,
    hidden,
    out_round,
    pre,
    mid_round,
    grad_qkv,
    key_acc,
    give,
    take,
    take_top,
    cot,
    send_part,
    recv_part,
    total,
    ring,
    shared,
    shared_buf,
    top_own,
    top_other,
    patch_own,
    patch_other,
    small,
    bias_rows,
    load_sem,
    weight_send,
    weight_recv,
    rows_send,
    rows_recv,
    y_send,
    y_recv,
    part_send,
    part_recv,
    ring_send,
    ring_recv,
    shared_send,
    shared_recv,
    last_send,
    last_recv,
    store_sem,
    credit,
):
    place = Place(wide_count)
    y, c, w, n = place.y, place.c, place.w, place.n
    sibling, partner = place.sibling, place.partner
    local, width = cot_in.shape
    patch = proj_in.shape[0] // 2
    seq = pos_in.shape[0]
    layers = scales.shape[0]
    cols = att_in.shape[2]
    heads = cols // HD
    hid = exp_in.shape[2]
    scale = HD ** (-0.5)
    diagonal = y == c
    chunks = seq // local

    barrier = pltpu.get_barrier_semaphore()
    for step in (1, 2, 3):
        pl.semaphore_signal(barrier, 1, device_id=(w, (n + step) % 4), device_id_type=MESH)
    pl.semaphore_signal(barrier, 1, device_id=place.pair, device_id_type=MESH)
    pl.semaphore_signal(barrier, 1, device_id=place.inward, device_id_type=MESH)

    @pl.when(place.has_out)
    def _():
        pl.semaphore_signal(barrier, 1, device_id=place.outward, device_id_type=MESH)

    def span(index, size):
        if isinstance(index, int):
            return pl.ds(index * size, size)
        return pl.ds(pl.multiple_of(index * size, size), size)

    far = (w, 2 - y)
    near = (w, 3 * y)
    here = span(c, local)
    row_copies = []
    for k, (src, dst, here) in enumerate(
        ((patches_in, rows_all, here), (cot_in, cot, here), (kinds_in, kinds_all, pl.ds(c, 1)))
    ):
        row_copies.append(
            (
                Copy(src, dst.at[here], rows_send.at[k, 0], rows_recv.at[k, c], far),
                Copy(src, dst.at[here], rows_send.at[k, 1], rows_recv.at[k, c], near),
                pltpu.make_async_copy(src, dst.at[here], rows_recv.at[k, c]),
            )
        )

    def send_rows(k):
        to_far, to_near, to_self = row_copies[k]
        to_far.start()

        @pl.when(diagonal)
        def _():
            to_self.start()

        @pl.when(jnp.logical_not(diagonal))
        def _():
            to_near.start()

    def wait_rows(k, dst, size):
        for h in range(2):
            spot = dst.at[pl.ds(h * size, size)]
            pltpu.make_async_copy(spot, spot, rows_recv.at[k, h]).wait()

    weights = []
    for layer in range(layers):
        for src, dst in ((att_in, wa), (comb_in, wc), (exp_in, we), (red_in, wr)):
            if dst is wc:
                halves = [wc.at[layer, pl.ds(k * cols, cols)] for k in range(2)]
            else:
                halves = [dst.at[layer, k] for k in range(2)]
            weights.append((src.at[layer], *halves))
    own_loads = [pltpu.make_async_copy(src, own, load_sem.at[k]) for k, (src, own, _) in enumerate(weights)]
    sib_loads = [
        Copy(src, sib, weight_send.at[k], weight_recv.at[k], sibling) for k, (src, _, sib) in enumerate(weights)
    ]
    proj_load = pltpu.make_async_copy(proj_in, proj, load_sem.at[8])
    pos_load = pltpu.make_async_copy(pos_in, pos, load_sem.at[9])
    abias_copy = Copy(abias_in, abias.at[1], weight_send.at[8], weight_recv.at[8], sibling)
    ebias_copy = Copy(ebias_in, ebias.at[1], weight_send.at[9], weight_recv.at[9], sibling)
    proj_load.start()
    pos_load.start()
    own_loads[0].start()

    @pl.when(place.has_out)
    def _():
        pl.semaphore_wait(barrier, 6)

    @pl.when(jnp.logical_not(place.has_out))
    def _():
        pl.semaphore_wait(barrier, 5)

    send_rows(0)
    send_rows(2)
    sib_loads[0].start()
    abias_copy.start()
    ebias_copy.start()
    abias[0] = abias_in[...]
    ebias[0] = ebias_in[...]

    def need(k):
        own_loads[k].wait()
        sib_loads[k].wait_recv()

    def note(row, values):
        small[row : row + 1, :] += column_sums(values)

    def param(ref, layer, row):
        return ref[layer, row : row + 1, :].astype(F32)

    def y_copy(index, slot, rows):
        return Copy(
            give.at[slot, rows], take.at[slot, rows], y_send.at[index[0], index[1]], y_recv.at[index[0], index[1]], partner
        )

    def offer(exchange, slot, ch, values):
        rows = span(ch, local)
        give[slot, rows, :] = values.astype(BF)
        y_copy((exchange, ch), slot, rows).start()

    def collect(exchange, slot, ch):
        rows = span(ch, local)
        y_copy((exchange, ch), slot, rows).wait()
        return give[slot, rows, :].astype(F32) + take[slot, rows, :].astype(F32)

    def head_mask(rows, h):
        lane = lax.broadcasted_iota(jnp.int32, (rows, cols), 1)
        return (lane >= h * HD) & (lane < (h + 1) * HD)

    place_col = lax.broadcasted_iota(jnp.int32, (seq, slots_in.shape[1]), 0)
    slot_row = slots_in[pl.ds(c, 1), :]
    masked = jnp.max(jnp.where(place_col == slot_row, 1.0, 0.0).astype(F32), axis=1, keepdims=True)
    wait_rows(0, rows_all, local)
    wait_rows(2, kinds_all, 1)
    for h in range(2):
        kinds = jnp.broadcast_to(jnp.where(kinds_all[h : h + 1, :] == 1, 1.0, 0.0), (128, 128)).astype(F32)
        flags[pl.ds(h * local, local), :] = kinds.T.astype(BF)
    proj_load.wait()
    pos_load.wait()
    wide_flags = jnp.concatenate([flags[...]] * (patch // 128), axis=1)
    patches = rows_all[...]
    kind_one = patches * wide_flags
    kind_zero = patches - kind_one
    is_one = flags[:, 0:1].astype(F32)
    lifted = nn(kind_zero, proj[0:patch, :]) + nn(kind_one, proj[patch : 2 * patch, :])
    offset = jnp.where(is_one > 0.5, offs_in[1:2, :].astype(F32), offs_in[0:1, :].astype(F32))
    stream[0] = jnp.where(masked > 0.5, plc_in[...].reshape(1, width).astype(F32), lifted + offset) + pos[...].astype(F32)

    def norm(layer, ch):
        rows = span(ch, local)
        hat, _ = hat_of(stream[layer, rows, :])
        first[layer, rows, :] = (hat * param(scales, layer, 0) + param(shifts, layer, 0)).astype(BF)

    def project(layer):
        rows = slice(None)

        def group(g):
            values = first[layer, rows, :]
            query = (nt(values, wa[layer, g, 0]) + abias[g, layer, 0:1, :].astype(F32)) * scale
            qkv[layer, g, 0, rows, :] = query.astype(BF)
            qkv[layer, g, 1, rows, :] = nt(values, wa[layer, g, 1]).astype(BF)
            qkv[layer, g, 2, rows, :] = (nt(values, wa[layer, g, 2]) + abias[g, layer, 1:2, :].astype(F32)).astype(BF)

        loop(2, group)

    def attend(layer):
        def chunk(ch):
            rows = span(ch, local)

            groups = []
            for g in range(2):
                total_mixed = 0.0
                query, key, value = qkv[layer, g, 0, rows, :], qkv[layer, g, 1], qkv[layer, g, 2]
                for h in range(heads):
                    scores = nt(jnp.where(head_mask(local, h), query, 0), key)
                    raised = jnp.exp(scores - jnp.max(scores, axis=-1, keepdims=True))
                    prob = (raised / jnp.sum(raised, axis=-1, keepdims=True)).astype(BF)
                    probs[layer, g * heads + h, rows, :] = prob
                    total_mixed += nn(prob, jnp.where(head_mask(seq, h), value, 0))
                groups.append(total_mixed.astype(BF))
            together = jnp.concatenate(groups, axis=1)
            mixed[layer, rows, :] = together
            offer(2 * layer, 0, ch, nn(together, wc[layer]))

        loop(chunks, chunk)

    def to_middle(layer, ch):
        rows = span(ch, local)
        values = stream[layer, rows, :] + collect(2 * layer, 0, ch) + cbias[layer : layer + 1, :].astype(F32)
        middle[layer, rows, :] = values
        hat, _ = hat_of(values)
        second[layer, rows, :] = (hat * param(scales, layer, 1) + param(shifts, layer, 1)).astype(BF)

    def activate(layer, g, rows):
        value = nn(second[layer, rows, :], we[layer, g]) + ebias[g, layer : layer + 1, :].astype(F32)
        cdf = 0.5 * (1.0 + lax.erf(value * (0.5**0.5)))
        hidden[layer, g, rows, :] = (value * cdf).astype(BF)
        density = jnp.exp(-0.5 * value * value) * 0.3989422804014327
        slope[layer, g, rows, :] = (cdf + value * density).astype(BF)

    def feed_back(layer, g, rows):
        grad_hidden = nt(out_round[rows, :], wr[layer, g])
        grad_pre = grad_hidden * slope[layer, g, rows, :].astype(F32)
        bias_rows[layer, g, 0:1, :] += column_sums(grad_pre)
        pre[g, rows, :] = grad_pre.astype(BF)

    def settle(row, layer, part, base, values, gain_row):
        hat, inverse = hat_of(base)
        note(2 * layer + part, values * hat)
        note(4 + 2 * layer + part, values)
        scaled = values * param(scales, layer, part)
        inner = scaled - jnp.mean(scaled, axis=-1, keepdims=True)
        return inverse * (inner - hat * jnp.mean(scaled * hat, axis=-1, keepdims=True))

    for own, sib in zip(own_loads[1:], sib_loads[1:]):
        own.start()
        sib.start()
    small[...] = jnp.zeros_like(small)
    bias_rows[...] = jnp.zeros_like(bias_rows)

    need(0)
    abias_copy.wait_recv()
    ebias_copy.wait_recv()
    for ch in range(2):
        norm(0, ch)
    project(0)
    for layer in range(layers):
        need(4 * layer + 1)
        attend(layer)
        need(4 * layer + 2)
        need(4 * layer + 3)
        if layer + 1 < layers:

            def chunk(ch):
                rows = span(ch, local)
                to_middle(layer, ch)

                part = 0.0
                for g in range(2):
                    activate(layer, g, rows)
                    part += nn(hidden[layer, g, rows, :], wr[layer, g])
                offer(2 * layer + 1, 1, ch, part)

            loop(chunks, chunk)
            if layer == 0:
                send_rows(1)
            need(4 * layer + 4)

            def after(ch):
                rows = span(ch, local)
                stream[layer + 1, rows, :] = (
                    middle[layer, rows, :] + collect(2 * layer + 1, 1, ch) + rbias[layer : layer + 1, :].astype(F32)
                )
                norm(layer + 1, ch)

            loop(chunks, after)
            project(layer + 1)

    last = layers - 1
    pieces = []
    at = 0
    cut = hid // 4
    spots = [(hid + k * cut if k < 4 else (k - 4) * cut, cut) for k in range(8)]
    spots += [(2 * hid + j * cols, cols) for j in range(3)] + [(2 * hid + 3 * cols, cols + 32)]
    per_layer = len(spots)
    for layer in reversed(range(layers)):
        for row, count in spots:
            k = len(pieces)
            kind = kind_of(k, wide_count)
            piece = kind(
                place,
                total.at[layer],
                row,
                count,
                ring,
                at,
                sums_out.at[layer],
                ring_send.at[k],
                ring_recv.at[k],
                store_sem.at[k],
            )
            pieces.append((piece, layer, row, count))
            at += kind.space(count)

    shares = []
    for layer in reversed(range(layers)):
        for batch, (row, size, count) in enumerate(
            ((hid, hid // 2, 2), (0, hid // 2, 2), (2 * hid, 3 * cols, 1), (2 * hid + 3 * cols, cols + 32, 1))
        ):
            shares.append((len(shares), layer, min(batch, 2), row, size, count))

    def share_copy(share, u):
        k, layer, batch, row, size, _ = share
        slot = ((last - layer) * 3 + batch) % 2
        start = row - (hid, 0, 2 * hid)[batch] + u * size
        return Copy(
            send_part.at[slot, pl.ds(start, size)],
            recv_part.at[pl.ds(row + u * size, size)],
            part_send.at[k, u],
            part_recv.at[k, u],
            sibling,
        )

    def free_slot(layer, batch):
        old = (last - layer) * 3 + batch - 2
        for share in shares:
            if (last - share[1]) * 3 + share[2] == old:
                for u in range(share[5]):
                    share_copy(share, u).wait_send()

    def join(share, u):
        k, layer, _, row, size, _ = share
        share_copy(share, u).wait_recv()
        start = row + u * size
        add_into(total.at[layer], start, recv_part, start, size)
        if k == 3:
            pl.semaphore_signal(credit, 1, device_id=sibling, device_id_type=MESH)
        for piece, owner, spot, _ in pieces:
            if owner == layer and start <= spot < start + size:
                piece.stages[0]()
                tick()

    ticks = iter(TICKS)

    def tick():
        for k, stage in next(ticks):
            stages = (pieces[k][0] if k < len(pieces) else shared_piece[0]).stages
            if stage < len(stages):
                stages[stage]()

    shared_piece = []

    def feed_grads(layer, batch):
        share = shares[4 * (last - layer) + batch]
        row = share[3]
        slot = ((last - layer) * 3 + batch) % 2
        free_slot(layer, batch)
        if layer < last and batch == 0:
            pl.semaphore_wait(credit, 1)

        def half(u):
            def block(t):
                lanes = pl.ds(pl.multiple_of((u * (hid // 256) + t) * 128, 128), 128)
                into = pl.ds(pl.multiple_of((u * (hid // 256) + t) * 128, 128), 128)
                for g in (1, 0):
                    if batch == 0:
                        values = tn(hidden[layer, g, :, lanes], out_round[...])
                    else:
                        values = tn(second[layer, :, lanes], pre[g])
                    if g == 1:
                        send_part[slot, into, :] = values.astype(BF)
                    else:
                        total[layer, pl.ds(row + into.start, 128), :] = values.astype(BF)

            rolled(hid // 256, block)
            share_copy(share, u).start()

        rolled(2, half)
        for u in range(2):
            join(share, u)

    def attention_grads(layer):
        three, one = shares[4 * (last - layer) + 2], shares[4 * (last - layer) + 3]
        slot = ((last - layer) * 3 + 2) % 2
        row = 2 * hid
        free_slot(layer, 2)

        def block(j):
            into = pl.ds(pl.multiple_of(j * cols, 16), cols)
            send_part[slot, into, :] = tn(grad_qkv[1, j], first[layer]).astype(BF)
            total[layer, pl.ds(row + into.start, cols), :] = tn(grad_qkv[0, j], first[layer]).astype(BF)

        rolled(3, block)
        share_copy(three, 0).start()
        both = tn(mixed[layer], mid_round[...])
        send_part[slot, pl.ds(3 * cols, cols), :] = both[cols:].astype(BF)
        send_part[slot, pl.ds(4 * cols, 32), :] = bias_rows[layer, 1].astype(BF)
        share_copy(one, 0).start()
        total[layer, pl.ds(row + 3 * cols, cols), :] = both[:cols].astype(BF)
        total[layer, pl.ds(row + 4 * cols, 32), :] = bias_rows[layer, 0].astype(BF)
        join(three, 0)
        join(one, 0)

    wait_rows(1, cot, local)

    def start_back(ch):
        rows = span(ch, local)
        grad[rows, :] = cot[rows, :].astype(F32)

    loop(chunks, start_back)

    def top_send():
        return Copy(top_other, top_own, last_send.at[0], last_recv.at[0], sibling)

    top_copy = Copy(give.at[2], take_top, last_send.at[1], last_recv.at[1], partner)

    for layer in reversed(range(layers)):
        exchange = 4 + 2 * (last - layer)

        def chunk(ch):
            rows = span(ch, local)
            note(10 + layer, grad[rows, :])
            out_round[rows, :] = grad[rows, :].astype(BF)
            if layer == last:
                to_middle(layer, ch)
                loop(2, lambda g: activate(layer, g, rows))
            part = 0.0
            for g in range(2):
                feed_back(layer, g, rows)
                part += nt(pre[g, rows, :], we[layer, g])
            offer(exchange, 1, ch, part)

        loop(chunks, chunk)
        tick()

        if layer == last:

            def top(ch):
                rows = span(ch, local)
                give[2, rows, :] = (
                    nn(hidden[layer, 0, rows, :], wr[layer, 0]) + nn(hidden[layer, 1, rows, :], wr[layer, 1])
                ).astype(BF)

            loop(chunks, top)

            @pl.when(jnp.logical_not(diagonal))
            def _():
                top_copy.start()

        feed_grads(layer, 0)
        feed_grads(layer, 1)

        def chunk(ch):
            rows = span(ch, local)
            grad_second = collect(exchange, 1, ch)
            grad_middle = grad[rows, :] + settle(rows, layer, 1, middle[layer, rows, :], grad_second, None)
            note(8 + layer, grad_middle)
            grad[rows, :] = grad_middle
            mid_round[rows, :] = grad_middle.astype(BF)

            def group(g):
                mixed_back = nt(mid_round[rows, :], wc[layer, span(g, cols), :]).astype(BF)
                query, key, value = qkv[layer, g, 0, rows, :], qkv[layer, g, 1], qkv[layer, g, 2]
                query_acc, key_sum, value_sum = 0.0, 0.0, 0.0
                for h in range(heads):
                    prob = probs[layer, g * heads + h, rows, :]
                    back = jnp.where(head_mask(local, h), mixed_back, 0)
                    grad_probs = nt(back, value)
                    value_sum += tn(prob, back)
                    weight = prob.astype(F32)
                    center = jnp.sum(weight * grad_probs, axis=-1, keepdims=True)
                    grad_scores = (weight * (grad_probs - center)).astype(BF)
                    query_acc += nn(grad_scores, jnp.where(head_mask(seq, h), key, 0))
                    key_sum += tn(grad_scores, jnp.where(head_mask(local, h), query, 0))
                grad_query = (query_acc.astype(BF).astype(F32) * scale).astype(BF)
                grad_qkv[g, 0, rows, :] = grad_query
                bias_rows[layer, g, 1:2, 0:cols] += column_sums(grad_query.astype(F32))

                if ch == 0:
                    key_acc[g, 0] = key_sum
                    key_acc[g, 1] = value_sum
                else:
                    key_acc[g, 0] += key_sum
                    key_acc[g, 1] += value_sum

            loop(2, group)

        loop(chunks, chunk)
        tick()

        def close(g):
            grad_qkv[g, 1] = key_acc[g, 0].astype(BF)
            grad_value = key_acc[g, 1].astype(BF)
            grad_qkv[g, 2] = grad_value
            bias_rows[layer, g, 2:3, 0:cols] += column_sums(grad_value.astype(F32))

        loop(2, close)

        def chunk(ch):
            rows = span(ch, local)

            part = 0.0
            for g in range(2):
                for j in range(3):
                    part += nn(grad_qkv[g, j, rows, :], wa[layer, g, j])
            offer(exchange + 1, 0, ch, part)

        loop(chunks, chunk)
        tick()
        attention_grads(layer)

        if layer == last:

            @pl.when(jnp.logical_not(diagonal))
            def _():
                top_copy.wait_send()

            @pl.when(diagonal)
            def _():
                top_copy.wait_recv()

                def finish_top(dst, half):
                    rows = span(half, local)
                    dst[...] = (
                        middle[layer, rows, :]
                        + (give[2, rows, :].astype(F32) + take_top[rows, :].astype(F32))
                        + rbias[layer : layer + 1, :].astype(F32)
                    )

                finish_top(top_other, 1 - c)
                top_send().start()
                finish_top(top_own, c)

        def chunk(ch):
            rows = span(ch, local)
            grad_first = collect(exchange + 1, 0, ch)
            grad[rows, :] += settle(rows, layer, 0, stream[layer, rows, :], grad_first, None)

        loop(chunks, chunk)
        tick()

    lifted_grad = jnp.where(masked > 0.5, 0.0, grad[...])
    note(14, grad[...] - lifted_grad)
    one_grad = jnp.where(is_one > 0.5, lifted_grad, 0.0)
    note(12, lifted_grad - one_grad)
    note(13, one_grad)
    lifted_round = lifted_grad.astype(BF)
    shared_rows = shared.shape[0]
    half_rows = shared_rows // 2
    flag_side = jnp.where(y == 1, wide_flags.astype(F32), 1.0 - wide_flags.astype(F32)).astype(BF)
    shared[0:patch, :] = tn(rows_all[...] * flag_side, lifted_round).astype(BF)
    shared[patch : patch + local, :] = grad[span(y, local), :].astype(BF)
    shared[patch + local : shared_rows, :] = small[...].astype(BF)
    keep_row, give_row = span(c, half_rows), span(1 - c, half_rows)
    shared_part = Copy(
        shared.at[give_row], shared_buf.at[pl.ds(0, half_rows)], last_send.at[2], last_recv.at[2], sibling
    )
    shared_part.start()

    patch_copy = Copy(patch_other, patch_own, last_send.at[3], last_recv.at[3], sibling)

    @pl.when(diagonal)
    def _():
        def half_back(dst, half):
            rows = span(half, local)
            flag = flags[rows, :].astype(F32)[:, 0:1]
            masks = jnp.max(
                jnp.where(
                    lax.broadcasted_iota(jnp.int32, (local, slots_in.shape[1]), 0) + half * local == slot_row, 1.0, 0.0
                ).astype(F32),
                axis=1,
                keepdims=True,
            )
            values = jnp.where(masks > 0.5, 0.0, grad[rows, :]).astype(BF)
            dst[...] = jnp.where(flag > 0.5, nt(values, proj[patch : 2 * patch, :]), nt(values, proj[0:patch, :]))

        half_back(patch_other, 1 - c)
        patch_copy.start()
        half_back(patch_own, c)

    shared_part.wait()
    add_into(shared, pl.multiple_of(c * half_rows, 16), shared_buf, 0, half_rows)
    sum_shared = PairFirst(
        place,
        shared,
        pl.multiple_of(c * half_rows, 16),
        half_rows,
        shared_buf,
        half_rows,
        shared_out.at[y],
        shared_send,
        shared_recv,
        store_sem.at[len(pieces)],
    )
    across = Copy(shared_out.at[y, keep_row], shared_out.at[y, keep_row], last_send.at[4], last_recv.at[4], partner)
    across_back = Copy(
        shared_out.at[1 - y, keep_row], shared_out.at[1 - y, keep_row], last_send.at[4], last_recv.at[4], partner
    )
    ends = []
    for k in range(2):
        ends.append(
            (
                Copy(
                    shared_out.at[k, keep_row], shared_out.at[k, keep_row], last_send.at[5 + k], last_recv.at[5 + k], sibling
                ),
                Copy(
                    shared_out.at[k, give_row], shared_out.at[k, give_row], last_send.at[5 + k], last_recv.at[5 + k], sibling
                ),
            )
        )

    def to_partner():
        sum_shared.s5()
        across.start()

    def to_sibling():
        across.wait_send()
        across_back.wait_recv()
        for out, _ in ends:
            out.start()

    def close_shared():
        for out, back in ends:
            out.wait_send()
            back.wait_recv()

    sum_shared.stages = sum_shared.stages[:5] + [to_partner, to_sibling, close_shared]
    shared_piece.append(sum_shared)
    count = len(pieces)
    sum_shared.s0()
    tick()

    @pl.when(diagonal)
    def _():
        top_send().wait_send()
        patch_copy.wait_send()

    @pl.when(jnp.logical_not(diagonal))
    def _():
        top_send().wait_recv()
        patch_copy.wait_recv()

    finals = (
        pltpu.make_async_copy(top_own, encoded_out, store_sem.at[count + 1]),
        pltpu.make_async_copy(patch_own, patches_out, store_sem.at[count + 2]),
    )
    for copy in finals:
        copy.start()
    tick()

    for copy in finals:
        copy.wait()

    for to_far, to_near, _ in row_copies:
        to_far.wait_send()

        @pl.when(jnp.logical_not(diagonal))
        def _():
            to_near.wait_send()

    for copy in sib_loads + [abias_copy, ebias_copy]:
        copy.wait_send()
    free_slot(-1, 0)
    free_slot(-1, 1)


def per_device(
    wide_count,
    patches,
    token_kind,
    mask_slots,
    projector,
    offsets,
    placeholder,
    positions,
    scales,
    shifts,
    attention,
    attn_bias,
    combiner,
    comb_bias,
    expander,
    expand_bias,
    reducer,
    reduce_bias,
    cotangent,
):
    local, patch = patches.shape
    seq, width = positions.shape
    layers = scales.shape[0]
    cols = attention.shape[3]
    heads = cols // HD
    hid = expander.shape[2]
    per_layer = 2 * hid + 4 * cols + 32
    shared_rows = patch + local + 64
    pieces = 12 * layers
    counts = ([hid // 4] * 8 + [cols] * 3 + [cols + 32]) * layers
    ring_rows = sum(kind_of(k, wide_count).space(count) for k, count in enumerate(counts))
    vmem = pl.BlockSpec(memory_space=pltpu.VMEM)
    anyw = pl.BlockSpec(memory_space=pl.ANY)
    dma = pltpu.SemaphoreType.DMA
    scratch = [
        pltpu.VMEM((layers, 2, 3, cols, width), BF),
        pltpu.VMEM((layers, 2 * cols, width), BF),
        pltpu.VMEM((layers, 2, width, hid), BF),
        pltpu.VMEM((layers, 2, hid, width), BF),
        pltpu.VMEM((2, layers, 2, cols), BF),
        pltpu.VMEM((2, layers, hid), BF),
        pltpu.VMEM((2 * patch, width), BF),
        pltpu.VMEM((seq, width), BF),
        pltpu.VMEM((seq, patch), BF),
        pltpu.VMEM((2, local), jnp.int32),
        pltpu.VMEM((seq, 128), BF),
        pltpu.VMEM((seq, width), F32),
        pltpu.VMEM((layers, seq, width), F32),
        pltpu.VMEM((layers, seq, width), F32),
        pltpu.VMEM((layers, seq, width), BF),
        pltpu.VMEM((layers, seq, width), BF),
        pltpu.VMEM((layers, 2, 3, seq, cols), BF),
        pltpu.VMEM((layers, 2 * heads, seq, seq), BF),
        pltpu.VMEM((layers, seq, 2 * cols), BF),
        pltpu.VMEM((layers, 2, seq, hid), BF),
        pltpu.VMEM((layers, 2, seq, hid), BF),
        pltpu.VMEM((seq, width), BF),
        pltpu.VMEM((2, seq, hid), BF),
        pltpu.VMEM((seq, width), BF),
        pltpu.VMEM((2, 3, seq, cols), BF),
        pltpu.VMEM((2, 2, seq, cols), F32),
        pltpu.VMEM((3, seq, width), BF),
        pltpu.VMEM((2, seq, width), BF),
        pltpu.VMEM((seq, width), BF),
        pltpu.VMEM((seq, width), BF),
        pltpu.VMEM((2, 4 * cols + 32, width), BF),
        pltpu.VMEM((per_layer, width), BF),
        pltpu.VMEM((layers, per_layer, width), BF),
        pltpu.VMEM((ring_rows, width), BF),
        pltpu.VMEM((shared_rows, width), BF),
        pltpu.VMEM((shared_rows // 2 + 3 * (shared_rows // 4), width), BF),
        pltpu.VMEM((local, width), F32),
        pltpu.VMEM((local, width), F32),
        pltpu.VMEM((local, patch), F32),
        pltpu.VMEM((local, patch), F32),
        pltpu.VMEM((64, width), F32),
        pltpu.VMEM((layers, 2, 32, width), F32),
        dma((10,)),
        dma((10,)),
        dma((10,)),
        dma((3, 2)),
        dma((3, 2)),
        dma((8, 2)),
        dma((8, 2)),
        dma((4 * layers, 2)),
        dma((4 * layers, 2)),
        dma((pieces, 11)),
        dma((pieces, 7)),
        dma((5,)),
        dma((5,)),
        dma((7,)),
        dma((7,)),
        dma((pieces + 3,)),
        pltpu.SemaphoreType.REGULAR,
    ]
    sums, shared, encoded, grad_patches = pl.pallas_call(
        functools.partial(encoder, wide_count),
        out_shape=(
            jax.ShapeDtypeStruct((layers, per_layer, width), BF),
            jax.ShapeDtypeStruct((2, shared_rows, width), BF),
            jax.ShapeDtypeStruct((local, width), F32),
            jax.ShapeDtypeStruct((local, patch), F32),
        ),
        in_specs=[anyw, vmem, anyw, vmem, anyw, vmem, vmem, anyw, vmem, vmem, anyw, vmem, anyw, vmem, anyw, vmem, anyw, vmem],
        out_specs=(anyw, anyw, anyw, anyw),
        scratch_shapes=scratch,
        compiler_params=pltpu.CompilerParams(
            collective_id=0, has_side_effects=True, vmem_limit_bytes=63 * 1024 * 1024 + 512 * 1024
        ),
        name="encoder",
    )(
        patches,
        token_kind.reshape(1, local),
        cotangent,
        mask_slots,
        projector.reshape(2 * patch, width),
        offsets,
        placeholder,
        positions,
        scales,
        shifts,
        attention.transpose(0, 1, 3, 2),
        attn_bias,
        combiner,
        comb_bias,
        expander,
        expand_bias,
        reducer,
        reduce_bias,
    )
    f32 = functools.partial(jax.ShapeDtypeStruct, dtype=F32)
    finished = pl.pallas_call(
        widen,
        out_shape=(
            f32((local, width)),
            f32((local, patch)),
            f32((2, patch, width)),
            f32((2, width)),
            f32((width,)),
            f32((seq, width)),
            f32((layers, 2, width)),
            f32((layers, 2, width)),
            f32((layers, 3, cols, width)),
            f32((layers, 2, cols)),
            f32((layers, cols, width)),
            f32((layers, width)),
            f32((layers, width, hid)),
            f32((layers, hid)),
            f32((layers, hid, width)),
            f32((layers, width)),
        ),
        in_specs=[anyw] * 4,
        out_specs=[anyw, anyw, anyw, vmem, vmem, anyw, vmem, vmem, anyw, vmem, anyw, vmem, anyw, vmem, anyw, vmem],
        scratch_shapes=[
            pltpu.VMEM((layers, per_layer, width), BF),
            pltpu.VMEM((layers, per_layer - 32, width), F32),
            pltpu.VMEM((2, shared_rows, width), BF),
            pltpu.VMEM((2, patch + local, width), F32),
            pltpu.VMEM((local, width), F32),
            pltpu.VMEM((local, patch), F32),
            dma((layers, 8)),
            dma((layers, 8)),
            dma((2,)),
            dma((2, 2)),
            dma((2, 2)),
        ],
        compiler_params=pltpu.CompilerParams(vmem_limit_bytes=62 * 1024 * 1024),
        name="widen",
    )(sums, shared, encoded, grad_patches)
    return tuple(item.transpose(0, 1, 3, 2) if k == 8 else item for k, item in enumerate(finished))


def widen(
    sums,
    shared,
    encoded,
    grad_patches,
    encoded_out,
    patches_out,
    projector,
    offsets,
    placeholder,
    positions,
    scales,
    shifts,
    attention,
    attn_bias,
    combiner,
    comb_bias,
    expander,
    expand_bias,
    reducer,
    reduce_bias,
    sums_in,
    sums_wide,
    shared_in,
    shared_wide,
    encoded_held,
    patches_held,
    load_sem,
    store_sem,
    shared_sem,
    shared_store,
    through_sem,
):
    layers, width, hid = expander.shape
    cols = combiner.shape[1]
    patch = projector.shape[1]
    local = encoded.shape[0]
    through = [
        (pltpu.make_async_copy(src, held, through_sem.at[k, 0]), pltpu.make_async_copy(held, dst, through_sem.at[k, 1]))
        for k, (src, held, dst) in enumerate(
            ((encoded, encoded_held, encoded_out), (grad_patches, patches_held, patches_out))
        )
    ]
    half = hid // 2
    cuts = []
    for k, array in enumerate((expander, reducer)):
        cuts += [(k * hid + u * half, half, array, u) for u in range(2)]
    cuts += [(2 * hid + j * cols, cols, attention, j) for j in range(3)]
    cuts.append((2 * hid + 3 * cols, sums.shape[1] - 3 * cols - 2 * hid, combiner, 0))
    loads = []
    for layer in range(layers):
        for k, (row, count, _, _) in enumerate(cuts):
            spot = (layer, pl.ds(row, count))
            loads.append(pltpu.make_async_copy(sums.at[spot], sums_in.at[spot], load_sem.at[layer, k]))
    shared_loads = [pltpu.make_async_copy(shared.at[k], shared_in.at[k], shared_sem.at[k]) for k in range(2)]
    for copy in loads + shared_loads + [load for load, _ in through]:
        copy.start()
    stores = []

    def convert(src, dst, row, count):
        def step(t):
            rows = pl.ds(pl.multiple_of(row + t * 64, 64), 64)
            dst[rows, :] = src[rows, :].astype(F32)

        rolled(count // 64, step)

    for layer in range(layers):
        for k, (row, count, array, u) in enumerate(cuts):
            loads[layer * len(cuts) + k].wait()
            wide = min(count, sums_wide.shape[1] - row)
            convert(sums_in.at[layer], sums_wide.at[layer], row, wide)
            target = array.at[layer, u] if array is attention else array.at[layer, pl.ds(u * half, wide)]
            copy = pltpu.make_async_copy(sums_wide.at[layer, pl.ds(row, wide)], target, store_sem.at[layer, k])
            copy.start()
            stores.append(copy)
        bias = sums_in[layer, pl.ds(2 * hid + 4 * cols, 16), :].astype(F32)
        expand_bias[layer : layer + 1, :] = bias[0:1, :]
        attn_bias[layer, 0:1, :] = bias[1:2, :cols]
        attn_bias[layer, 1:2, :] = bias[2:3, :cols]
    for k in range(2):
        shared_loads[k].wait()
        convert(shared_in.at[k], shared_wide.at[k], 0, patch + local)
        for target, start, size, sem in (
            (projector.at[k], 0, patch, 0),
            (positions.at[pl.ds(k * local, local)], patch, local, 1),
        ):
            copy = pltpu.make_async_copy(shared_wide.at[k, pl.ds(start, size)], target, shared_store.at[k, sem])
            copy.start()
            stores.append(copy)
    for load, store in through:
        load.wait()
        store.start()
    small = shared_in[0, pl.ds(patch + local, 16), :].astype(F32)
    for layer in range(layers):
        scales[layer] = small[2 * layer : 2 * layer + 2, :]
        shifts[layer] = small[4 + 2 * layer : 6 + 2 * layer, :]
    comb_bias[...] = small[8:10, :]
    reduce_bias[...] = small[10:12, :]
    offsets[...] = small[12:14, :]
    placeholder[...] = small[14:15, :].reshape(width)
    for copy in stores + [store for _, store in through]:
        copy.wait()


def solution(mesh):
    rows = ("wide", "narrow")
    return jax.shard_map(
        functools.partial(per_device, mesh.shape["wide"]),
        mesh=mesh,
        in_specs=(
            P(rows, None),
            P(rows),
            P("wide", None),
            P(),
            P(),
            P(),
            P(),
            P(),
            P(),
            P(None, None, None, "narrow"),
            P(None, None, "narrow"),
            P(None, "narrow", None),
            P(),
            P(None, None, "narrow"),
            P(None, "narrow"),
            P(None, "narrow", None),
            P(),
            P(rows, None),
        ),
        out_specs=(
            P(rows, None),
            P(rows, None),
            P(),
            P(),
            P(),
            P(),
            P(),
            P(),
            P(None, None, None, "narrow"),
            P(None, None, "narrow"),
            P(None, "narrow", None),
            P(),
            P(None, None, "narrow"),
            P(None, "narrow"),
            P(None, "narrow", None),
            P(),
        ),
        check_vma=False,
    )
```
